32 devices in a mesh: fsdp: 32 (over z, y, x, core).
Axes of the slice: x: 2, y: 2, z: 4, core: 2. Of those that a mesh axis runs over, the one named last changes fastest.
Arguments:
- characters: bfloat16 [2, 8192, 768], P(None, 'fsdp'), may hold values from -6 to 6
- segment_ids: int32 [2, 8192], P(None, 'fsdp'), may hold values from 0 to 31, never falling along the last dimension, each value on 1 to 1024 neighbouring positions
- cotangent: bfloat16 [2, 2048, 768], P(None, 'fsdp'), may hold values from -6 to 6
- local_params: bfloat16 [7087104], P('fsdp'), may hold values from -3 to 3, as said below
- conv_params: bfloat16 [2361600], P('fsdp'), may hold values from -3 to 3, as said below
Outputs:
- molecules: bfloat16 [2, 2048, 768], P(None, 'fsdp')
- char_grads: float32 [2, 8192, 768], P(None, 'fsdp')
- local_grads: float32 [7087104], P('fsdp')
- conv_grads: float32 [2361600], P('fsdp')
The draws below stay inside these ranges and needn't reach their ends.
Inputs may be any that keep to these rules, and one draw needn't show every extreme that they name: `local_params`: holds the layer's parameters flattened in the order of the first step (matrices row-major), the last 0 entries being padding that no output reads. `conv_params`: holds Wc row-major, then bc, g3, s3, the last 0 entries being padding that no output reads.
All inputs are finite; a program needn't handle non-finite values.
Results may differ from the reference program's by a relative error of at most 0.014.
Values may be sent and summed in bfloat16 or wider, within the bound.
A program may use at most 256 MiB of HBM per device.

```python
import math
import jax
import jax.numpy as jnp
import numpy as np
from jax import lax

D = 768
HEADS = 12
FF = 3072
WINDOW = 128
RATE = 4
MICRO = 2
HEAD_SIZE = 64
TOKENS = 8192
MOLS = 2048
LOCAL_COUNT = 7087104
CONV_COUNT = 2361600
LOCAL_FLAT = 7087104
CONV_FLAT = 2361600


def normal_piece(piece_key, length, scale):
    return jnp.clip(jax.random.normal(piece_key, (length,), jnp.float32), -6.0, 6.0) * scale


def gain_piece(piece_key, length):
    return jax.random.uniform(piece_key, (length,), jnp.float32, 0.6, 1.4)


def draw_local_params(key, part):
    keys_list = jax.random.split(key, 14)
    pieces = [normal_piece(keys_list[0], 3 * D * D, D ** (-0.5)), normal_piece(keys_list[1], D * D, 4.0 * D ** (-0.5)), normal_piece(keys_list[2], D * FF, D ** (-0.5)), normal_piece(keys_list[3], FF * D, FF ** (-0.5)), normal_piece(keys_list[4], FF, 0.3), gain_piece(keys_list[5], D), normal_piece(keys_list[6], D, 0.3), normal_piece(keys_list[7], D, 0.3), normal_piece(keys_list[8], D, 0.3), normal_piece(keys_list[9], D, 0.3), gain_piece(keys_list[10], D), normal_piece(keys_list[11], D, 0.3), normal_piece(keys_list[12], D, 0.3), jax.random.uniform(keys_list[13], (LOCAL_FLAT - LOCAL_COUNT,), jnp.float32, -1.0, 1.0)]
    return jnp.concatenate(pieces).astype(jnp.bfloat16)


def draw_conv_params(key, part):
    keys_list = jax.random.split(key, 5)
    pieces = [normal_piece(keys_list[0], RATE * D * D, (RATE * D) ** (-0.5)), normal_piece(keys_list[1], D, 0.3), gain_piece(keys_list[2], D), normal_piece(keys_list[3], D, 0.3), jax.random.uniform(keys_list[4], (CONV_FLAT - CONV_COUNT,), jnp.float32, -1.0, 1.0)]
    return jnp.concatenate(pieces).astype(jnp.bfloat16)


def with_spikes(values, rng, source, target, parts, factor):
    def block_of(axis_at):
        return (jnp.arange(values.shape[axis_at]) // (values.shape[axis_at] // parts)).reshape((-1,) + (1,) * (values.ndim - 1 - axis_at))

    first = jax.random.permutation(rng, parts)[block_of(target)]
    second = (block_of(target) + parts // 2) % parts
    return jnp.where((block_of(source) == first) | (block_of(source) == second), factor * values, values)


def block_scale(stream_key, dims, cuts, least, high):
    def one(position, shards_of):
        heights = jax.random.uniform(jax.random.fold_in(jax.random.fold_in(stream_key, 6), position), (shards_of,), jnp.float32, least / len(cuts), high / len(cuts))
        return jnp.repeat(jnp.exp(heights), dims[position] // shards_of).reshape((-1,) + (1,) * (len(dims) - position - 1))

    level = one(*cuts[0])
    for cut in cuts[1:]:
        level = level * one(*cut)
    return level


def split_up(number_of, total, reach, slope):
    loads = [(1 << 20) // math.isqrt(standing ** slope) + 1 for standing in range(2, number_of + 1)]
    spare, given = total - reach - (number_of - 1), [1] * (number_of - 1)
    while spare > 0:
        movable = [i for i in range(number_of - 1) if given[i] < reach]
        whole, budget = sum([loads[i] for i in movable]), spare
        for i in movable:
            addition = min(reach - given[i], max(1, budget * loads[i] // whole), spare)
            given[i] = given[i] + addition
            spare = spare - addition
    return np.array([reach] + given)


def ragged_sizes(rng, number_of, total, limit, lean):
    if number_of == 2:
        one = jax.random.randint(rng, (), max(1, total - limit), min(limit, total - 1) + 1)
        return jnp.stack([one, total - one])
    tallies = jnp.asarray(split_up(number_of, total, limit, lean), jnp.int32)
    couples = (number_of - 1) // 2
    giver, taker = tallies[1:1 + 2 * couples:2], tallies[2:2 + 2 * couples:2]
    margin = jnp.minimum(giver - 1, limit - taker)
    passed = jax.random.randint(jax.random.fold_in(rng, 1), (couples,), 0, 1 << 20) % (margin + 1)
    tallies = tallies.at[1:1 + 2 * couples:2].set(giver - passed).at[2:2 + 2 * couples:2].set(taker + passed)
    return tallies[jax.random.permutation(jax.random.fold_in(rng, 2), number_of)]


def scatter_about(own_key, shape, scale, most, cuts=(), kind=jnp.bfloat16):
    values = scale * jax.random.normal(own_key, shape, jnp.float32)
    if cuts:
        values = values * block_scale(own_key, shape, cuts, -0.22, 0.18)
    return jnp.clip(values, -most, most).astype(kind)


def bell_draw_with(rng, dims, width, most, shards, heavy, dtype=jnp.bfloat16):
    values = width * jax.random.normal(rng, dims, jnp.float32)
    if shards:
        values = values * block_scale(rng, dims, shards, -0.22, 0.18)
    return jnp.clip(with_spikes(values, jax.random.fold_in(rng, 3), *heavy), -most, most).astype(dtype)


def setup_inputs(seed: int = 0) -> dict:
    key_list = jax.random.split(jax.random.key(seed), 6)
    characters = scatter_about(key_list[0], (MICRO, TOKENS, D), 1.0, 6.0, ((1, 32),))
    segment_ids = jax.vmap(lambda own: jnp.searchsorted(jnp.cumsum(ragged_sizes(own, TOKENS // 256, TOKENS, min(1024, TOKENS // 2), 1)), jnp.arange(TOKENS), side="right"))(jax.random.split(key_list[1], MICRO)).reshape((MICRO, TOKENS)).astype(jnp.int32)
    cotangent = bell_draw_with(key_list[2], (MICRO, MOLS, D), 1.0, 6.0, ((1, 32),), (1, 2, 32, 2.75))
    local_params = draw_local_params(jax.random.fold_in(key_list[5], 71), 0)
    conv_params = draw_conv_params(jax.random.fold_in(key_list[5], 71), 0)
    return {"characters": characters, "segment_ids": segment_ids, "cotangent": cotangent, "local_params": local_params, "conv_params": conv_params}


EPSILON = 1e-05
HIGHEST_PRECISION = lax.Precision.HIGHEST

@jax.custom_vjp
def low(v):
    return lax.optimization_barrier(v.astype(jnp.bfloat16)).astype(jnp.float32)

@jax.custom_vjp
def low_back(v):
    return v

def low_keep(v):
    return (low(v), None)

def low_pass(kept, grad):
    return (grad,)

def back_keep(v):
    return (v, None)

def back_low(kept, grad):
    return (low(grad),)
low.defvjp(low_keep, low_pass)
low_back.defvjp(back_keep, back_low)

def local_layout():
    return ((D, 3 * D), (D, D), (D, FF), (FF, D), (FF,)) + ((D,),) * 8

def conv_layout():
    return ((RATE * D, D), (D,), (D,), (D,))

def unpack(packed, layout):
    offset = 0
    pieces = []
    for extent in layout:
        length = math.prod(extent)
        pieces.append(packed[offset:offset + length].reshape(extent))
        offset = offset + length
    return pieces

def normalize(values, gain, shift):
    average = lax.optimization_barrier(jnp.mean(values, axis=-1, keepdims=True))
    centred = values - average
    spread = lax.optimization_barrier(jnp.mean(centred * centred, axis=-1, keepdims=True))
    return centred * lax.rsqrt(spread + EPSILON) * gain + shift

def matmul(left, right):
    return jnp.dot(left, right, precision=HIGHEST_PRECISION, preferred_element_type=jnp.float32)

def gelu_exact(values):
    return jax.nn.gelu(values, approximate=False)

def forward(inputs, segments, local_flat, conv_flat):
    qkv_weight, out_weight, in_weight, down_weight, in_bias, gain_one, shift_one, query_bias, value_bias, out_bias, gain_two, shift_two, down_bias = unpack(local_flat, local_layout())
    conv_weight, conv_bias, gain_three, shift_three = unpack(conv_flat, conv_layout())
    row_count = inputs.shape[0]
    windows = row_count // WINDOW
    normed = low(normalize(inputs, gain_one, shift_one))
    proj_bias = jnp.concatenate([query_bias, jnp.zeros_like(query_bias), value_bias])
    projected = low(low_back(matmul(normed, qkv_weight) + proj_bias))
    heads_view = projected.reshape(windows, WINDOW, 3, HEADS, HEAD_SIZE)
    queries = heads_view[:, :, 0]
    keys_all = heads_view[:, :, 1]
    values = heads_view[:, :, 2]
    scores = jnp.einsum('bqhe,bkhe->bhqk', queries, keys_all, precision=HIGHEST_PRECISION) * HEAD_SIZE ** (-0.5)
    grouped = segments.reshape(windows, WINDOW)
    allowed = grouped[:, None, :, None] == grouped[:, None, None, :]
    scores = low_back(jnp.where(allowed, scores, -1e+30))
    weights = low(jax.nn.softmax(scores, axis=-1))
    attended = jnp.einsum('bhqk,bkhe->bqhe', weights, values, precision=HIGHEST_PRECISION)
    context = low(low_back(attended.reshape(row_count, D)))
    after_attention = inputs + low_back(matmul(context, out_weight)) + out_bias
    middle = low(normalize(after_attention, gain_two, shift_two))
    hidden = low(gelu_exact(low_back(matmul(middle, in_weight) + in_bias)))
    after_feed = after_attention + low_back(matmul(hidden, down_weight)) + down_bias
    grouped_rows = low(after_feed).reshape(row_count // RATE, RATE * D)
    conv_pre = low_back(matmul(grouped_rows, conv_weight) + conv_bias)
    return normalize(gelu_exact(conv_pre), gain_three, shift_three)

def reference(characters, segment_ids, cotangent, local_params, conv_params):
    local_flat = local_params.astype(jnp.float32)
    conv_flat = conv_params.astype(jnp.float32)
    block_rows = math.gcd(TOKENS, 4096)
    block_count = MICRO * TOKENS // block_rows
    char_blocks = characters.reshape(block_count, block_rows, D)
    segment_blocks = segment_ids.reshape(block_count, block_rows)
    cot_blocks = cotangent.reshape(block_count, block_rows // RATE, D)

    def advance(totals, inputs):
        chars_block, segs_block, cots_block = inputs

        def forward_block(values_in, local_in, conv_in):
            return forward(values_in, segs_block, local_in, conv_in)
        result, pullback = jax.vjp(forward_block, chars_block.astype(jnp.float32), local_flat, conv_flat)
        grad_chars, grad_local, grad_conv = pullback(cots_block.astype(jnp.float32))
        return ((totals[0] + grad_local, totals[1] + grad_conv), (result.astype(jnp.bfloat16), grad_chars))
    initial = (jnp.zeros_like(local_flat), jnp.zeros_like(conv_flat))
    (local_total, conv_total), (mol_blocks, grad_blocks) = lax.scan(advance, initial, (char_blocks, segment_blocks, cot_blocks))
    return (mol_blocks.reshape(MICRO, TOKENS // RATE, D), grad_blocks.reshape(MICRO, TOKENS, D), local_total, conv_total)
```

```python
import functools
import math
from types import SimpleNamespace

import jax
import jax.numpy as jnp
from jax import lax
from jax.experimental import pallas as pl
from jax.experimental.pallas import tpu as pltpu
from jax.sharding import PartitionSpec as P

MESH = pl.DeviceIdType.MESH
F32, BF16 = jnp.float32, jnp.bfloat16
D, FF, HEADS, WINDOW, RATE, MICRO, HEAD_SIZE = 768, 3072, 12, 128, 4, 2, 64
LOCAL_COUNT, CONV_COUNT = 7087104, 2361600
LANE = 128
UNIT = 1152
EPS = EPSILON = 1e-05


DC = D // LANE
FC = FF // LANE
VB1, VG1, VS1, VBQ, VBV, VBO, VG2, VS2, VB2 = 0, 24, 30, 36, 42, 48, 54, 60, 66
VBC, VG3, VS3 = 78, 84, 90
QKV_ROW, O_ROW, W1_ROW, W2_ROW = 0, 18 * D, 24 * D, 48 * D

def nn(a, b): return jnp.dot(a, b, preferred_element_type=F32)
def nt(a, b): return lax.dot_general(a, b, (((1,), (1,)), ((), ())), preferred_element_type=F32)
def tn(a, b): return lax.dot_general(a, b, (((0,), (0,)), ((), ())), preferred_element_type=F32)

def loop(n, fn, unroll=1):
    def body(i, _):
        fn(i)
        return 0
    lax.fori_loop(0, n, body, 0, unroll=unroll)

def at(i, size): return pl.ds(pl.multiple_of(i * size, size), size)

def vec(r, row, blocks=DC):
    return jnp.concatenate([r.vecs[row + i:row + i + 1, :] for i in range(blocks)], axis=1)

def put(r, row, value):
    for i in range(value.shape[1] // LANE):
        r.vgrad[row + i:row + i + 1, :] = value[:, i * LANE:(i + 1) * LANE]

def add_to(r, row, value):
    for i in range(value.shape[1] // LANE):
        r.vgrad[row + i:row + i + 1, :] += value[:, i * LANE:(i + 1) * LANE]

def normal(v):
    mean = jnp.mean(v, axis=-1, keepdims=True)
    cen = v - mean
    var = jnp.mean(cen * cen, axis=-1, keepdims=True)
    s = lax.rsqrt(var + EPS)
    return cen * s, s

def normal_back(dn, nrm, s):
    return s * (dn - jnp.mean(dn, axis=-1, keepdims=True) - nrm * jnp.mean(dn * nrm, axis=-1, keepdims=True))

def colsum(v): return jnp.sum(v, axis=0, keepdims=True)

def gelu_both(h):
    cdf = 0.5 + 0.5 * lax.erf(h * (0.5 ** 0.5))
    pdf = jnp.exp(-0.5 * h * h) * (1.0 / math.sqrt(2 * math.pi))
    return h * cdf, cdf + h * pdf

RB = 64
def forward_norm(r):
    g1, s1 = vec(r, VG1), vec(r, VS1)
    def f(i):
        nrm, _ = normal(r.x[at(i, RB), :].astype(F32))
        r.a[at(i, RB), :] = (nrm * g1 + s1).astype(BF16)
    loop(r.rows // RB, f)

def forward_qkv(r):
    bias = jnp.concatenate([vec(r, VBQ), jnp.zeros((1, D), F32), vec(r, VBV)], axis=1)
    for i in range(18):
        r.bias[i:i + 1, :] = bias[:, i * LANE:(i + 1) * LANE]
    def f(i):
        b = jnp.concatenate([r.bias[pl.ds(2 * i, 1), :], r.bias[pl.ds(2 * i + 1, 1), :]], axis=1)
        r.P[:, at(i, 256)] = (nn(r.a[...], r.wqkv[:, at(i, 256)]) + b).astype(BF16)
    loop(9, f)

def halves(v):
    lo = lax.broadcasted_iota(jnp.int32, v.shape, 1) < 64
    w = v.astype(F32)
    z = jnp.zeros_like(w)
    return jnp.concatenate([jnp.where(lo, w, z), jnp.where(lo, z, w)], axis=0).astype(BF16)

def pick(v):
    lo = lax.broadcasted_iota(jnp.int32, (WINDOW, LANE), 1) < 64
    return jnp.where(lo, v[:WINDOW], v[WINDOW:])

def heads_of(r, i):
    w = i // DC
    hp = lax.rem(i, DC)
    rows = at(w, WINDOW)
    return w, rows, at(hp, LANE), at(hp + DC, LANE), at(hp + 2 * DC, LANE)

def forward_attention(r):
    def f(i):
        w, rows, cq, ck, cv = heads_of(r, i)
        q2 = halves(r.P[rows, cq])
        s = nt(q2, r.P[rows, ck]) * 0.125
        same = r.segc[rows, :] == r.segr[pl.ds(w, 1), :]
        same2 = jnp.concatenate([same.astype(F32)] * 2, axis=0) > 0.5
        s = jnp.where(same2, s, -1e30)
        e = jnp.exp(s - jnp.max(s, axis=-1, keepdims=True))
        p = (e / jnp.sum(e, axis=-1, keepdims=True)).astype(BF16)
        r.p[i] = p
        r.ctx[rows, cq] = pick(nn(p, r.P[rows, cv])).astype(BF16)
    loop(r.rows // WINDOW * DC, f)

def forward_out(r):
    bo = vec(r, VBO)
    for i in range(3):
        c = slice(i * 256, (i + 1) * 256)
        r.y1[:, c] = r.x[:, c].astype(F32) + nn(r.ctx[...], r.wo[:, c]) + bo[:, c]
    g2, s2 = vec(r, VG2), vec(r, VS2)
    def f(i):
        nrm, _ = normal(r.y1[at(i, RB), :])
        r.c[at(i, RB), :] = (nrm * g2 + s2).astype(BF16)
    loop(r.rows // RB, f)

def forward_up(r):
    def f(i):
        b = jnp.concatenate([r.vecs[pl.ds(VB1 + 2 * i, 1), :], r.vecs[pl.ds(VB1 + 2 * i + 1, 1), :]], axis=1)
        h = nn(r.c[...], r.w1[:, at(i, 256)]) + b
        hid, slope = gelu_both(h)
        r.hid[:, at(i, 256)] = hid.astype(BF16)
        r.slope[:, at(i, 256)] = slope.astype(BF16)
    loop(12, f)

def forward_down(r):
    b2 = vec(r, VB2)
    for i in range(3):
        c = slice(i * 256, (i + 1) * 256)
        v = r.y1[:, c] + nn(r.hid[...], r.w2[:, c]) + b2[:, c]
        r.ys[2 * i] = v[:, :LANE]
        r.ys[2 * i + 1] = v[:, LANE:]
    for j in range(RATE):
        for c in range(DC):
            r.u[j, :, c * LANE:(c + 1) * LANE] = r.ys[c, pl.ds(j, r.mols, stride=RATE), :].astype(BF16)

def forward_conv(r):
    z = vec(r, VBC)
    for j in range(RATE):
        z = z + nn(r.u[j], r.wc[j * D:(j + 1) * D, :])
    w, slope = gelu_both(z)
    nrm, s = normal(w)
    r.mol[...] = (nrm * vec(r, VG3) + vec(r, VS3)).astype(BF16)
    t = r.cot[...].astype(F32)
    put(r, VG3, colsum(t * nrm))
    put(r, VS3, colsum(t))
    dw = normal_back(t * vec(r, VG3), nrm, s)
    dz = (dw * slope).astype(BF16)
    r.dz[...] = dz
    put(r, VBC, colsum(dz.astype(F32)))

def emit_flat(r, dst, row0, tile):
    k, m = tile.shape[0], tile.shape[1] // LANE
    for c in range(m):
        r.scr[pl.ds(c, k, stride=m), :] = tile[:, c * LANE:(c + 1) * LANE]
    dst[pl.ds(pl.multiple_of(row0, 16), k * m), :] = r.scr[0:k * m, :].astype(BF16)

def grad_conv_weight(r):
    for j in range(RATE):
        def f(i):
            emit_flat(r, r.gc, (j * D + i * 256) * DC, tn(r.u[j, :, at(i, 256)], r.dz[...]))
        loop(3, f)

def back_conv(r):
    for j in range(RATE):
        v = nt(r.dz[...], r.wc[j * D:(j + 1) * D, :])
        for c in range(DC):
            r.ys[c, pl.ds(j, r.mols, stride=RATE), :] = v[:, c * LANE:(c + 1) * LANE]
    for c in range(DC):
        v = r.ys[c]
        r.df[:, c * LANE:(c + 1) * LANE] = v.astype(BF16)
        put(r, VB2 + c, colsum(v))

def grad_down_weight(r):
    loop(12, lambda i: emit_flat(r, r.gl, W2_ROW + i * 256 * DC, tn(r.hid[:, at(i, 256)], r.df[...])))

def back_down(r):
    def f(i):
        dh = (nt(r.df[...], r.w2[at(i, 256), :]) * r.slope[:, at(i, 256)].astype(F32)).astype(BF16)
        r.slope[:, at(i, 256)] = dh
        s = colsum(dh.astype(F32))
        r.vgrad[pl.ds(VB1 + 2 * i, 1), :] = s[:, :LANE]
        r.vgrad[pl.ds(VB1 + 2 * i + 1, 1), :] = s[:, LANE:]
    loop(12, f)

def grad_up_weight(r):
    loop(6, lambda i: emit_flat(r, r.gl, W1_ROW + i * 128 * FC, tn(r.c[:, at(i, 128)], r.slope[...])))

def back_up(r):
    for i in range(3):
        r.dc[:, i * 256:(i + 1) * 256] = nt(r.slope[...], r.w1[i * 256:(i + 1) * 256, :])
    g2 = vec(r, VG2)
    zero = jnp.zeros((1, D), F32)
    put(r, VG2, zero); put(r, VS2, zero); put(r, VBO, zero)
    def f(i):
        rows = at(i, RB)
        dc = r.dc[rows, :]
        nrm, s = normal(r.y1[rows, :])
        add_to(r, VG2, colsum(dc * nrm))
        add_to(r, VS2, colsum(dc))
        dy2 = jnp.concatenate([r.ys[c, rows, :] for c in range(DC)], axis=1)
        dy1 = dy2 + normal_back(dc * g2, nrm, s)
        r.dc[rows, :] = dy1
        add_to(r, VBO, colsum(dy1))
        r.df[rows, :] = dy1.astype(BF16)
    loop(r.rows // RB, f)

def grad_out_weight(r):
    loop(3, lambda i: emit_flat(r, r.gl, O_ROW + i * 256 * DC, tn(r.ctx[:, at(i, 256)], r.df[...])))

def back_out(r):
    for i in range(3):
        r.c[:, i * 256:(i + 1) * 256] = nt(r.df[...], r.wo[i * 256:(i + 1) * 256, :]).astype(BF16)

def back_attention(r):
    def f(i):
        w, rows, cq, ck, cv = heads_of(r, i)
        do2 = halves(r.c[rows, cq])
        q2 = halves(r.P[rows, cq])
        k = r.P[rows, ck]
        pb = r.p[i]
        p = pb.astype(F32)
        dp = nt(do2, r.P[rows, cv])
        ds = (p * (dp - jnp.sum(p * dp, axis=-1, keepdims=True))).astype(BF16)
        dq = pick(nn(ds, k)) * 0.125
        dk = tn(ds, q2) * 0.125
        dv = tn(pb, do2)
        r.P[rows, cq] = dq.astype(BF16)
        r.P[rows, ck] = dk.astype(BF16)
        r.P[rows, cv] = dv.astype(BF16)
    loop(r.rows // WINDOW * DC, f)

def grad_qkv_weight(r):
    for c in range(DC):
        r.vgrad[VBQ + c:VBQ + c + 1, :] = colsum(r.P[:, c * LANE:(c + 1) * LANE].astype(F32))
        r.vgrad[VBV + c:VBV + c + 1, :] = colsum(r.P[:, 2 * D + c * LANE:2 * D + (c + 1) * LANE].astype(F32))
    loop(6, lambda i: emit_flat(r, r.gl, QKV_ROW + i * 128 * 18, tn(r.a[:, at(i, 128)], r.P[...])))

def back_qkv(r):
    for i in range(3):
        r.y1[:, i * 256:(i + 1) * 256] = nt(r.P[...], r.wqkv[i * 256:(i + 1) * 256, :])
    g1 = vec(r, VG1)
    zero = jnp.zeros((1, D), F32)
    put(r, VG1, zero); put(r, VS1, zero)
    def f(i):
        rows = at(i, RB)
        da = r.y1[rows, :]
        nrm, s = normal(r.x[rows, :].astype(F32))
        add_to(r, VG1, colsum(da * nrm))
        add_to(r, VS1, colsum(da))
        r.dc[rows, :] = r.dc[rows, :] + normal_back(da * g1, nrm, s)
    loop(r.rows // RB, f)

def state_shapes(rows):
    mols = rows // RATE
    V = pltpu.VMEM
    return dict(
        a=V((rows, D), BF16), P=V((rows, 3 * D), BF16), p=V((rows // WINDOW * DC, 2 * WINDOW, LANE), BF16),
        ctx=V((rows, D), BF16), y1=V((rows, D), F32), c=V((rows, D), BF16), slope=V((rows, FF), BF16), hid=V((rows, FF), BF16),
        ys=V((DC, rows, LANE), F32), u=V((RATE, mols, D), BF16), dz=V((mols, D), BF16), df=V((rows, D), BF16), dc=V((rows, D), F32),
        scr=V((128 * FC, LANE), F32), bias=V((24, LANE), F32), vecs=V((96, LANE), F32))


class Geo:
    def __init__(self, n, local_shard, conv_shard):
        self.n = n
        self.Z = n // 8
        self.RL = (12 * D * D) // LANE // n
        self.RC = (4 * D * D) // LANE // n
        self.dl = local_shard - self.RL * LANE
        self.dc = conv_shard - self.RC * LANE
        self.HL = -(-(self.dl * n) // (8 * LANE)) * 8
        self.HC = -(-(self.dc * n) // (8 * LANE)) * 8
        self.XL = -(-local_shard // (8 * LANE)) * 8
        self.XC = -(-conv_shard // (8 * LANE)) * 8

def where_am_i():
    me = lax.axis_index("fsdp")
    core = lax.rem(me, 2)
    bx = lax.rem(me // 2, 2)
    by = lax.rem(me // 4, 2)
    z = me // 8
    sib = me + 1 - 2 * core
    xn = me + 2 - 4 * bx
    yn = me + 4 - 8 * by
    first = xn + core * (yn - xn)
    second = yn + core * (xn - yn)
    return me, core, z, sib, first, second

def realign(out_ref, out_base, lo, hi, x_ref, shift):
    q = shift // LANE
    r = lax.rem(shift, LANE)
    turn = lax.rem(LANE - r, LANE)
    lane = lax.broadcasted_iota(jnp.int32, (16, LANE), 1)
    keep = lane < (LANE - r)
    def body(i, _):
        low = x_ref[pl.ds(q + i * 16, 16), :]
        high = x_ref[pl.ds(q + i * 16 + 1, 16), :]
        val = jnp.where(keep, pltpu.roll(low, turn, 1), pltpu.roll(high, turn, 1))
        out_ref[pl.ds(pl.multiple_of(out_base + i * 16, 16), 16), :] = val.astype(out_ref.dtype)
        return 0
    lax.fori_loop(lo // 16, hi // 16, body, 0, unroll=2 if (hi - lo) % 32 == 0 else 1)

def widen(dst_ref, dst_base, src_ref, rows):
    step = 248 if rows % 248 == 0 else 8
    for i in range(rows // step):
        dst_ref[dst_base + i * step:dst_base + (i + 1) * step, :] = src_ref[i * step:(i + 1) * step, :].astype(F32)

def convert_unit(src_ref, base, w_ref, krow, cols, scr):
    groups = UNIT // (16 * cols)
    def body(g, _):
        scr[0:16 * cols, :] = src_ref[pl.ds(pl.multiple_of(base + g * 16 * cols, 16), 16 * cols), :].astype(F32)
        for cc in range(cols):
            v = scr[pl.ds(cc, 16, stride=cols), :]
            w_ref[pl.ds(pl.multiple_of(krow + g * 16, 16), 16), cc * LANE:(cc + 1) * LANE] = v.astype(BF16)
        return 0
    lax.fori_loop(0, groups, body, 0)


def start_gather(g):
    n, Z, geo, me, z = g.n, g.Z, g.geo, g.me, g.z
    RL, RC = geo.RL, geo.RC
    nxt = lax.rem(me + 1, n)
    bar = pltpu.get_barrier_semaphore()
    far = lax.rem(me + n + 2 * g.core - 1, n)
    for dev in (g.sib, g.first, g.second, far):
        pl.semaphore_signal(bar, inc=1, device_id=(dev,), device_id_type=MESH)
    @pl.when(z > 0)
    def _(): pl.semaphore_signal(bar, inc=1, device_id=(me - 8,), device_id_type=MESH)
    @pl.when(z < Z - 1)
    def _(): pl.semaphore_signal(bar, inc=1, device_id=(me + 8,), device_id_type=MESH)
    widen(g.xlf, geo.HL, g.xl, geo.XL)
    widen(g.xcf, geo.HC, g.xc, geo.XC)
    HA, HB = 80, 32
    lshift, cshift = geo.HL * LANE - geo.dl * me, geo.HC * LANE - geo.dc * me
    realign(g.gl, me * RL, HA, RL, g.xlf, lshift)
    realign(g.gc, me * RC, HB, RC, g.xcf, cshift)
    pl.semaphore_wait(bar, 4 + jnp.where(z > 0, 1, 0) + jnp.where(z < Z - 1, 1, 0))
    halo = pltpu.make_async_remote_copy(src_ref=g.hb, dst_ref=g.hr, send_sem=g.hsem.at[0], recv_sem=g.hsem.at[1], device_id=(nxt,), device_id_type=MESH)
    halo.start()
    halo.wait()
    g.xlf[0:geo.HL, :] = g.hr[0:geo.HL, :].astype(F32)
    g.xcf[0:geo.HC, :] = g.hr[geo.HL:geo.HL + geo.HC, :].astype(F32)
    realign(g.gl, me * RL, 0, HA, g.xlf, lshift)
    realign(g.gc, me * RC, 0, HB, g.xcf, cshift)
    @pl.when(me == n - 1)
    def _():
        g.tail[...] = g.hb[...]


def gather_weights(g):
    n, Z, geo, me, z = g.n, g.Z, g.geo, g.me, g.z
    RL, RC = geo.RL, geo.RC
    sib, first, second, last = g.sib, g.first, g.second, n - 1
    def pieces(src):
        return ((0, g.gl.at[pl.ds(pl.multiple_of(src * RL, 16), RL)]), (1, g.gc.at[pl.ds(pl.multiple_of(src * RC, 16), RC)]))
    def copies(src, dev, slot):
        return [pltpu.make_async_remote_copy(src_ref=ref, dst_ref=ref, send_sem=g.ssem.at[k, slot], recv_sem=g.rsem.at[k, src], device_id=(dev,), device_id_type=MESH) for k, ref in pieces(src)]
    def tail_copy(dev, slot):
        return pltpu.make_async_remote_copy(src_ref=g.tail, dst_ref=g.tail, send_sem=g.tsem.at[slot], recv_sem=g.tsem.at[5], device_id=(dev,), device_id_type=MESH)
    UP, DN, FI, SE, SI = 0, Z, 2 * Z, 3 * Z, 5 * Z
    def send(src, dev, slot, tslot):
        for cp in copies(src, dev, slot): cp.start()
        @pl.when(src == last)
        def _(): tail_copy(dev, tslot).start()
    def await_recv(src):
        for cp in copies(src, sib, 0): cp.wait_recv()
        @pl.when(src == last)
        def _(): tail_copy(sib, 0).wait_recv()
    def drain(src, dev, slot, tslot):
        for cp in copies(src, dev, slot): cp.wait_send()
        @pl.when(src == last)
        def _(): tail_copy(dev, tslot).wait_send()
    def valid(dz): return jnp.logical_and(z + dz >= 0, z + dz < Z)
    def src_of(dz, f, s): return me + 8 * dz + f * (first - me) + s * (second - me)
    def column(dz, act):
        src = src_of(dz, 0, 0)
        zi = z + dz
        if dz >= 0:
            @pl.when(z > 0)
            def _(): act(src, me - 8, DN + zi, 0)
        if dz <= 0:
            @pl.when(z < Z - 1)
            def _(): act(src, me + 8, UP + zi, 1)
        act(src, first, FI + zi, 2)
        act(src, second, SE + zi, 3)
        act(src, sib, SI + zi, 4)
    def firsts(dz, act):
        src = src_of(dz, 1, 0)
        act(src, second, SE + Z + z + dz, 3)
        act(src, sib, SI + Z + z + dz, 4)
    def seconds(dz, f, act):
        act(src_of(dz, f, 1), sib, SI + (2 + f) * Z + z + dz, 4)
    def convert(dz):
        for f in (0, 1):
            for s in (0, 1):
                src = src_of(dz, f, s)
                await_recv(src + sib - me)
                chip = src // 2
                for i in range(2 * RL // UNIT):
                    t = chip * (2 * RL // UNIT) + i
                    base = t * UNIT
                    @pl.when(t < 12)
                    def _(): convert_unit(g.gl, base, g.wqkv, t * 64, 18, g.scr)
                    @pl.when(jnp.logical_and(t >= 12, t < 16))
                    def _(): convert_unit(g.gl, base, g.wo, (t - 12) * 192, 6, g.scr)
                    @pl.when(jnp.logical_and(t >= 16, t < 32))
                    def _(): convert_unit(g.gl, base, g.w1, (t - 16) * 48, 24, g.scr)
                    @pl.when(t >= 32)
                    def _(): convert_unit(g.gl, base, g.w2, (t - 32) * 192, 6, g.scr)
                for i in range(2 * RC // UNIT):
                    t = chip * (2 * RC // UNIT) + i
                    convert_unit(g.gc, t * UNIT, g.wc, t * 192, 6, g.scr)
    def level(k): return [0] if k == 0 else ([k, -k] if k < Z else [])
    def guarded(k, fn):
        for dz in level(k):
            @pl.when(valid(dz))
            def _(): fn(dz)
    def e1(dz):
        if dz != 0: await_recv(src_of(dz, 0, 0))
        column(dz, send)
    def e2(dz):
        await_recv(src_of(dz, 1, 0))
        firsts(dz, send)
        await_recv(src_of(dz, 0, 1))
        seconds(dz, 0, send)
    def e4(dz):
        await_recv(src_of(dz, 1, 1))
        seconds(dz, 1, send)
        convert(dz)
    guarded(0, e1)
    for k in range(Z):
        guarded(k + 1, e1)
        guarded(k, e2)
        if k: guarded(k - 1, e4)
    guarded(Z - 1, e4)
    def finish(dz):
        column(dz, drain)
        firsts(dz, drain)
        seconds(dz, 0, drain)
        seconds(dz, 1, drain)
    for k in range(Z): guarded(k, finish)


PART = 576


def scatter_gradients(g):
    n, Z, geo, me, z = g.n, g.Z, g.geo, g.me, g.z
    sib, first, second, last = g.sib, g.first, g.second, n - 1
    own = (g.gl, g.gc)
    size = (geo.RL, geo.RC)
    def target(zt, f, s): return me + 8 * (zt - z) + f * (first - me) + s * (second - me)
    def rows(k, t): return pl.ds(pl.multiple_of(t * size[k], 16), size[k])
    def to_sib(k, t):
        c = t // 2
        return pltpu.make_async_remote_copy(src_ref=own[k].at[rows(k, t)], dst_ref=g.from_sib[k].at[rows(k, c)], send_sem=g.s_sib.at[k, c], recv_sem=g.r_sib.at[k, c], device_id=(sib,), device_id_type=MESH)
    def to_second(k, zt, f):
        t = target(zt, f, 1)
        c = 2 * zt + f
        return pltpu.make_async_remote_copy(src_ref=own[k].at[rows(k, t)], dst_ref=g.from_second[k].at[rows(k, c)], send_sem=g.s_second.at[k, c], recv_sem=g.r_second.at[k, c], device_id=(second,), device_id_type=MESH)
    def to_first(k, zt):
        t = target(zt, 1, 0)
        return pltpu.make_async_remote_copy(src_ref=own[k].at[rows(k, t)], dst_ref=g.from_first[k].at[rows(k, zt)], send_sem=g.s_first.at[k, zt], recv_sem=g.r_first.at[k, zt], device_id=(first,), device_id_type=MESH)
    def to_line(k, zt, up):
        t = target(zt, 0, 0)
        land, r = (g.from_below, g.r_below) if up else (g.from_above, g.r_above)
        return pltpu.make_async_remote_copy(src_ref=own[k].at[rows(k, t)], dst_ref=land[k].at[rows(k, zt)], send_sem=g.s_line.at[k, zt], recv_sem=r.at[k, zt], device_id=(me + 8 if up else me - 8,), device_id_type=MESH)
    def add_in(k, t, sources, out, out_base):
        parts = size[k] // PART
        def fetch(p, slot, i, go):
            ref, c, there = sources[i]
            cp = pltpu.make_async_copy(ref.at[pl.ds(pl.multiple_of(c * size[k] + p * PART, 16), PART)], g.tmp.at[slot, i], g.fsem.at[slot, i])
            if there is None: go(cp)
            else:
                @pl.when(there)
                def _(): go(cp)
        for i in range(len(sources)): fetch(0, 0, i, lambda cp: cp.start())
        for p in range(parts):
            slot = p % 2
            if p + 1 < parts:
                for i in range(len(sources)): fetch(p + 1, 1 - slot, i, lambda cp: cp.start())
            for i in range(len(sources)): fetch(p, slot, i, lambda cp: cp.wait())
            def body(b, _):
                at_ = pl.ds(pl.multiple_of(b * 16, 16), 16)
                acc = own[k][pl.ds(pl.multiple_of(t * size[k] + p * PART + b * 16, 16), 16), :].astype(F32)
                for i, (_r, _c, there) in enumerate(sources):
                    v = g.tmp[slot, i, at_, :].astype(F32)
                    acc = acc + (v if there is None else jnp.where(there, v, 0.0))
                out[pl.ds(pl.multiple_of(out_base + p * PART + b * 16, 16), 16), :] = acc.astype(out.dtype)
                return 0
            lax.fori_loop(0, PART // 16, body, 0, unroll=4)
    def p0(k, zt):
        for f in (0, 1):
            for s in (0, 1):
                to_sib(k, target(zt, f, s) + sib - me).start()
    def p1(k, zt):
        for f in (0, 1):
            t = target(zt, f, 1)
            to_sib(k, t).wait_recv()
            add_in(k, t, [(g.from_sib[k], t // 2, None)], own[k], t * size[k])
            to_second(k, zt, f).start()
    def p2(k, zt):
        t = target(zt, 1, 0)
        to_sib(k, t).wait_recv()
        to_second(k, zt, 1).wait_recv()
        add_in(k, t, [(g.from_sib[k], t // 2, None), (g.from_second[k], 2 * zt + 1, None)], own[k], t * size[k])
        to_first(k, zt).start()
    def p3(k, zt):
        t = target(zt, 0, 0)
        to_sib(k, t).wait_recv()
        to_second(k, zt, 0).wait_recv()
        to_first(k, zt).wait_recv()
        above = jnp.logical_and(z >= zt, z < Z - 1)
        below = jnp.logical_and(z <= zt, z > 0)
        @pl.when(above)
        def _(): to_line(k, zt, False).wait_recv()
        @pl.when(below)
        def _(): to_line(k, zt, True).wait_recv()
        srcs = [(g.from_sib[k], t // 2, None), (g.from_second[k], 2 * zt, None), (g.from_first[k], zt, None), (g.from_above[k], zt, above), (g.from_below[k], zt, below)]
        @pl.when(z == zt)
        def _(): add_in(k, t, srcs, (g.xlf, g.xcf)[k], 0)
        @pl.when(z != zt)
        def _(): add_in(k, t, srcs, own[k], t * size[k])
        @pl.when(z > zt)
        def _(): to_line(k, zt, False).start()
        @pl.when(z < zt)
        def _(): to_line(k, zt, True).start()
    def finish(k, zt):
        for f in (0, 1):
            for s in (0, 1):
                to_sib(k, target(zt, f, s) + sib - me).wait_send()
            to_second(k, zt, f).wait_send()
        to_first(k, zt).wait_send()
        @pl.when(z > zt)
        def _(): to_line(k, zt, False).wait_send()
        @pl.when(z < zt)
        def _(): to_line(k, zt, True).wait_send()
    steps = [(1, zt) for zt in reversed(range(Z))] + [(0, zt) for zt in reversed(range(Z))]
    for i in range(len(steps) + 2):
        if i < len(steps):
            p0(*steps[i])
            p1(*steps[i])
        if 1 <= i <= len(steps): p2(*steps[i - 1])
        if i >= 2: p3(*steps[i - 2])
    for st in steps: finish(*st)


def reduce_vectors(g):
    Z, me, z = g.Z, g.me, g.z
    core = lax.rem(me, 2)
    bx, by = lax.rem(me // 2, 2), lax.rem(me // 4, 2)
    def cp(slot, dev):
        return pltpu.make_async_remote_copy(src_ref=g.vgrad, dst_ref=g.vland.at[slot], send_sem=g.vsem.at[0], recv_sem=g.vsem.at[1 + slot], device_id=(dev,), device_id_type=MESH)
    def take(slot):
        cp(slot, g.sib).wait_recv()
        g.vgrad[...] = g.vgrad[...] + g.vland[slot]
    def give(slot, dev):
        c = cp(slot, dev)
        c.start()
        c.wait_send()
    on = core == 1
    @pl.when(jnp.logical_not(on))
    def _(): give(0, g.sib)
    @pl.when(on)
    def _():
        take(0)
        @pl.when(bx == 0)
        def _(): give(1, g.second)
        @pl.when(bx == 1)
        def _():
            take(1)
            @pl.when(by == 0)
            def _(): give(2, g.first)
            @pl.when(by == 1)
            def _():
                take(2)
                @pl.when(z > 0)
                def _(): take(3)
                @pl.when(z < Z - 1)
                def _(): give(3, me + 8)


def place_gradients(g):
    n, geo, me = g.n, g.geo, g.me
    prv = lax.rem(me + n - 1, n)
    HL, HC = geo.HL, geo.HC
    g.fs[0:HL, :] = g.xlf[0:HL, :]
    g.fs[HL:HL + HC, :] = g.xcf[0:HC, :]
    cp = pltpu.make_async_remote_copy(src_ref=g.fs, dst_ref=g.fr, send_sem=g.hsem.at[2], recv_sem=g.hsem.at[3], device_id=(prv,), device_id_type=MESH)
    cp.start()
    cp.wait()
    edge = me == n - 1
    g.xlf[geo.RL:geo.RL + HL, :] = jnp.where(edge, g.vgrad[0:HL, :], g.fr[0:HL, :])
    skip = VBC - HL
    g.xcf[geo.RC:geo.RC + HC - skip, :] = jnp.where(edge, g.vgrad[VBC:HL + HC, :], g.fr[HL:HL + HC - skip, :])
    realign(g.outl, 0, 0, geo.XL // 16 * 16 + 16, g.xlf, geo.dl * me)
    realign(g.outc, 0, 0, geo.XC // 16 * 16 + 16, g.xcf, geo.dc * me)


def local_layout():
    return ((D, 3 * D), (D, D), (D, FF), (FF, D), (FF,)) + ((D,),) * 8


def conv_layout():
    return ((RATE * D, D), (D,), (D,), (D,))


def unpack(packed, layout):
    offset = 0
    pieces = []
    for extent in layout:
        length = math.prod(extent)
        pieces.append(packed[offset : offset + length].reshape(extent))
        offset = offset + length
    return pieces


def normalize_parts(values):
    average = jnp.mean(values, axis=-1, keepdims=True)
    centred = values - average
    spread = jnp.mean(centred * centred, axis=-1, keepdims=True)
    scaling = lax.rsqrt(spread + EPSILON)
    return (centred * scaling, scaling)


def normal_back(grad_normed, normed, scaling):
    first_mean = jnp.mean(grad_normed, axis=-1, keepdims=True)
    second_mean = jnp.mean(grad_normed * normed, axis=-1, keepdims=True)
    return scaling * (grad_normed - first_mean - normed * second_mean)


def product(left, right):
    return jnp.dot(left, right, preferred_element_type=jnp.float32)


def rows_inner(left, right):
    return lax.dot_general(
        left, right, (((0,), (0,)), ((), ())), preferred_element_type=jnp.float32
    )


def times_transpose(left, right):
    return lax.dot_general(
        left, right, (((1,), (1,)), ((), ())), preferred_element_type=jnp.float32
    )


def gelu_exact(values):
    return jax.nn.gelu(values, approximate=False)


def gelu_grad(values, upstream):
    return jax.vjp(gelu_exact, values)[1](upstream)[0]


def window_scores(projected, segments_block):
    row_count = projected.shape[0]
    windows = row_count // WINDOW
    heads_view = projected.reshape(windows, WINDOW, 3, HEADS, HEAD_SIZE)
    queries = heads_view[:, :, 0]
    keys_all = heads_view[:, :, 1]
    values = heads_view[:, :, 2]
    scores = jnp.einsum(
        "bqhe,bkhe->bhqk", queries, keys_all, preferred_element_type=jnp.float32
    ) * HEAD_SIZE ** (-0.5)
    grouped = segments_block.reshape(windows, WINDOW)
    allowed = grouped[:, None, :, None] == grouped[:, None, None, :]
    return (jnp.where(allowed, scores, -1e30), queries, keys_all, values)


def forward_pass(characters_block, segments_block, local_weights, conv_weights):
    (
        qkv_weight,
        out_weight,
        in_weight,
        down_weight,
        in_bias,
        gain_one,
        shift_one,
        query_bias,
        value_bias,
        out_bias,
        gain_two,
        shift_two,
        down_bias,
    ) = local_weights
    conv_weight, conv_bias, gain_three, shift_three = conv_weights
    row_count = characters_block.shape[0]
    inputs = characters_block.astype(jnp.float32)
    norm_one, scale_one = normalize_parts(inputs)
    normed = (norm_one * gain_one + shift_one).astype(jnp.bfloat16)
    proj_bias = jnp.concatenate([query_bias, jnp.zeros_like(query_bias), value_bias])
    projected = (product(normed, qkv_weight) + proj_bias).astype(jnp.bfloat16)
    scores, queries, keys_all, values = window_scores(projected, segments_block)
    largest = jnp.max(scores, axis=-1, keepdims=True)
    raised = jnp.exp(scores - largest)
    totals = jnp.sum(raised, axis=-1, keepdims=True)
    log_totals = largest + jnp.log(totals)
    weights = (raised / totals).astype(jnp.bfloat16)
    attended = jnp.einsum("bhqk,bkhe->bqhe", weights, values, preferred_element_type=jnp.float32)
    context = attended.reshape(row_count, D).astype(jnp.bfloat16)
    after_attention = inputs + product(context, out_weight) + out_bias
    norm_two, scale_two = normalize_parts(after_attention)
    middle = (norm_two * gain_two + shift_two).astype(jnp.bfloat16)
    pre_act = product(middle, in_weight) + in_bias
    hidden = gelu_exact(pre_act).astype(jnp.bfloat16)
    after_feed = after_attention + product(hidden, down_weight) + down_bias
    grouped_rows = after_feed.astype(jnp.bfloat16).reshape(row_count // RATE, RATE * D)
    conv_pre = product(grouped_rows, conv_weight) + conv_bias
    norm_three, scale_three = normalize_parts(gelu_exact(conv_pre))
    molecules = (norm_three * gain_three + shift_three).astype(jnp.bfloat16)
    saved_state = (
        segments_block,
        norm_one,
        scale_one,
        normed,
        projected,
        log_totals,
        context,
        norm_two,
        scale_two,
        middle,
        pre_act,
        hidden,
        grouped_rows,
        conv_pre,
        norm_three,
        scale_three,
    )
    return (molecules, saved_state)


def backward_pass(cotangent_block, saved_state, local_weights, conv_weights):
    (
        qkv_weight,
        out_weight,
        in_weight,
        down_weight,
        in_bias,
        gain_one,
        shift_one,
        query_bias,
        value_bias,
        out_bias,
        gain_two,
        shift_two,
        down_bias,
    ) = local_weights
    conv_weight, conv_bias, gain_three, shift_three = conv_weights
    (
        segments_block,
        norm_one,
        scale_one,
        normed,
        projected,
        log_totals,
        context,
        norm_two,
        scale_two,
        middle,
        pre_act,
        hidden,
        grouped_rows,
        conv_pre,
        norm_three,
        scale_three,
    ) = saved_state
    row_count = normed.shape[0]
    windows = row_count // WINDOW
    upstream = cotangent_block.astype(jnp.float32)
    grad_gain_three = jnp.sum(upstream * norm_three, axis=0)
    grad_shift_three = jnp.sum(upstream, axis=0)
    grad_activated = normal_back(upstream * gain_three, norm_three, scale_three)
    grad_conv_pre = gelu_grad(conv_pre, grad_activated).astype(jnp.bfloat16)
    grad_conv_bias = jnp.sum(grad_conv_pre.astype(jnp.float32), axis=0)
    grad_conv_weight = rows_inner(grouped_rows, grad_conv_pre)
    grad_feed = times_transpose(grad_conv_pre, conv_weight).reshape(row_count, D)
    grad_down_bias = jnp.sum(grad_feed, axis=0)
    grad_branch = grad_feed.astype(jnp.bfloat16)
    grad_down_weight = rows_inner(hidden, grad_branch)
    grad_hidden = times_transpose(grad_branch, down_weight)
    grad_pre = gelu_grad(pre_act, grad_hidden).astype(jnp.bfloat16)
    grad_in_bias = jnp.sum(grad_pre.astype(jnp.float32), axis=0)
    grad_in_weight = rows_inner(middle, grad_pre)
    grad_middle = times_transpose(grad_pre, in_weight)
    grad_gain_two = jnp.sum(grad_middle * norm_two, axis=0)
    grad_shift_two = jnp.sum(grad_middle, axis=0)
    grad_attention = grad_feed + normal_back(grad_middle * gain_two, norm_two, scale_two)
    grad_out_bias = jnp.sum(grad_attention, axis=0)
    grad_attn_out = grad_attention.astype(jnp.bfloat16)
    grad_out_weight = rows_inner(context, grad_attn_out)
    grad_context = times_transpose(grad_attn_out, out_weight).astype(jnp.bfloat16)
    grad_heads = grad_context.reshape(windows, WINDOW, HEADS, HEAD_SIZE)
    scores, queries, keys_all, values = window_scores(projected, segments_block)
    probs = jnp.exp(scores - log_totals)
    weights = probs.astype(jnp.bfloat16)
    grad_weights = jnp.einsum(
        "bqhe,bkhe->bhqk", grad_heads, values, preferred_element_type=jnp.float32
    )
    row_terms = jnp.sum(probs * grad_weights, axis=-1, keepdims=True)
    grad_scores = (probs * (grad_weights - row_terms)).astype(jnp.bfloat16)
    grad_queries = jnp.einsum(
        "bhqk,bkhe->bqhe", grad_scores, keys_all, preferred_element_type=jnp.float32
    ) * HEAD_SIZE ** (-0.5)
    grad_keys = jnp.einsum(
        "bhqk,bqhe->bkhe", grad_scores, queries, preferred_element_type=jnp.float32
    ) * HEAD_SIZE ** (-0.5)
    grad_values = jnp.einsum(
        "bhqk,bqhe->bkhe", weights, grad_heads, preferred_element_type=jnp.float32
    )
    grad_proj = (
        jnp.stack([grad_queries, grad_keys, grad_values], axis=2)
        .reshape(row_count, 3 * D)
        .astype(jnp.bfloat16)
    )
    proj_sums = jnp.sum(grad_proj.astype(jnp.float32), axis=0)
    grad_query_bias = proj_sums[:D]
    grad_value_bias = proj_sums[2 * D :]
    grad_qkv_weight = rows_inner(normed, grad_proj)
    grad_normed = times_transpose(grad_proj, qkv_weight)
    grad_gain_one = jnp.sum(grad_normed * norm_one, axis=0)
    grad_shift_one = jnp.sum(grad_normed, axis=0)
    grad_inputs = grad_attention + normal_back(grad_normed * gain_one, norm_one, scale_one)
    local_grad = jnp.concatenate(
        [
            grad_qkv_weight.reshape(-1),
            grad_out_weight.reshape(-1),
            grad_in_weight.reshape(-1),
            grad_down_weight.reshape(-1),
            grad_in_bias,
            grad_gain_one,
            grad_shift_one,
            grad_query_bias,
            grad_value_bias,
            grad_out_bias,
            grad_gain_two,
            grad_shift_two,
            grad_down_bias,
        ]
    )
    conv_grad = jnp.concatenate(
        [grad_conv_weight.reshape(-1), grad_conv_bias, grad_gain_three, grad_shift_three]
    )
    return (grad_inputs, local_grad, conv_grad)


def plain_device(characters, segment_ids, cotangent, local_params, conv_params):
    devices = lax.axis_size("fsdp")
    local_shard = local_params.shape[0]
    conv_shard = conv_params.shape[0]
    local_pad = local_shard * devices - LOCAL_COUNT
    conv_pad = conv_shard * devices - CONV_COUNT
    local_total = jnp.zeros((1, local_shard), jnp.float32)
    conv_total = jnp.zeros((1, conv_shard), jnp.float32)
    molecule_list = []
    gradient_list = []
    for micro_index in range(MICRO):
        local_full, conv_full = (
            lax.all_gather(local_params, "fsdp", axis=0, tiled=True),
            lax.all_gather(conv_params, "fsdp", axis=0, tiled=True),
        )
        molecules, saved_state = forward_pass(
            characters[micro_index],
            segment_ids[micro_index],
            unpack(local_full, local_layout()),
            unpack(conv_full, conv_layout()),
        )
        local_full, conv_full = (
            lax.all_gather(local_params, "fsdp", axis=0, tiled=True),
            lax.all_gather(conv_params, "fsdp", axis=0, tiled=True),
        )
        grad_inputs, local_grad, conv_grad = backward_pass(
            cotangent[micro_index],
            saved_state,
            unpack(local_full, local_layout()),
            unpack(conv_full, conv_layout()),
        )
        local_table = jnp.concatenate([local_grad, jnp.zeros((local_pad,), jnp.float32)]).reshape(
            devices, local_shard
        )
        conv_table = jnp.concatenate([conv_grad, jnp.zeros((conv_pad,), jnp.float32)]).reshape(
            devices, conv_shard
        )
        local_part, conv_part = (
            lax.psum_scatter(local_table, "fsdp", scatter_dimension=0, tiled=True),
            lax.psum_scatter(conv_table, "fsdp", scatter_dimension=0, tiled=True),
        )
        local_total = local_total + local_part
        conv_total = conv_total + conv_part
        molecule_list.append(molecules)
        gradient_list.append(grad_inputs)
    return (
        jnp.stack(molecule_list),
        jnp.stack(gradient_list),
        local_total.reshape(-1),
        conv_total.reshape(-1),
    )


def fused_kernel(geo, rows, in_names, out_names, scratch_names, *refs):
    n_in, n_out = len(in_names), len(out_names)
    every = dict(zip(list(in_names) + list(out_names) + list(scratch_names), refs))
    me, core, z, sib, first, second = where_am_i()
    g = SimpleNamespace(n=geo.n, Z=geo.Z, geo=geo, me=me, core=core, z=z, sib=sib, first=first, second=second, rows=rows, mols=rows // RATE, **every)
    for base in ("from_sib", "from_second", "from_first", "from_above", "from_below"):
        setattr(g, base, (every[base + "_l"], every[base + "_c"]))
    start_gather(g)
    gather_weights(g)
    g.vecs[...] = g.tail[...].astype(F32)
    g.vgrad[...] = jnp.zeros_like(g.vgrad)
    for f in (forward_norm, forward_qkv, forward_attention, forward_out, forward_up, forward_down, forward_conv, grad_conv_weight, back_conv,
              grad_down_weight, back_down, grad_up_weight, back_up, grad_out_weight, back_out, back_attention, grad_qkv_weight, back_qkv):
        f(g)
    cgc = pltpu.make_async_copy(g.dc, g.cg, g.osem.at[0])
    cgc.start()
    scatter_gradients(g)
    reduce_vectors(g)
    place_gradients(g)
    cgc.wait()


def fused(n, characters, segment_ids, cotangent, local_params, conv_params):
    geo = Geo(n, local_params.shape[0], conv_params.shape[0])
    micro, span, _ = characters.shape
    rows = micro * span
    x = characters.reshape(rows, D)
    cot = cotangent.reshape(rows // RATE, D)
    segc = segment_ids.reshape(rows, 1)
    segr = segment_ids.reshape(rows // WINDOW, WINDOW)
    xl = jnp.pad(local_params, (0, geo.XL * LANE - local_params.shape[0])).reshape(geo.XL, LANE)
    xc = jnp.pad(conv_params, (0, geo.XC * LANE - conv_params.shape[0])).reshape(geo.XC, LANE)
    hb = jnp.concatenate([local_params[-geo.HL * LANE:], conv_params[-geo.HC * LANE:]]).reshape(geo.HL + geo.HC, LANE)
    V = pl.BlockSpec(memory_space=pltpu.VMEM)
    A = pl.BlockSpec(memory_space=pl.ANY)
    S = jax.ShapeDtypeStruct
    Z, H = geo.Z, geo.HL + geo.HC
    ins = dict(x=x, segc=segc, segr=segr, cot=cot, xl=xl, xc=xc, hb=hb)
    outs = dict(mol=(V, S((rows // RATE, D), BF16)), cg=(A, S((rows, D), F32)), outl=(V, S((geo.XL // 16 * 16 + 16, LANE), F32)), outc=(V, S((geo.XC // 16 * 16 + 16, LANE), F32)))
    for name, count in (("from_sib", n // 2), ("from_second", 2 * Z), ("from_first", Z), ("from_above", Z), ("from_below", Z)):
        outs[name + "_l"] = (A, S((count * geo.RL, LANE), BF16))
        outs[name + "_c"] = (A, S((count * geo.RC, LANE), BF16))
    W = pltpu.VMEM
    DMA = pltpu.SemaphoreType.DMA
    sc = state_shapes(rows)
    sc.update(wqkv=W((D, 3 * D), BF16), wo=W((D, D), BF16), w1=W((D, FF), BF16), w2=W((FF, D), BF16), wc=W((FF, D), BF16))
    sc.update(gl=W((n * geo.RL, LANE), BF16), gc=W((n * geo.RC, LANE), BF16), hr=W((H, LANE), BF16), tail=W((H, LANE), BF16),
              xlf=W((geo.HL + geo.XL + 32, LANE), F32), xcf=W((geo.HC + geo.XC + 32, LANE), F32), vgrad=W((H, LANE), F32), vland=W((4, H, LANE), F32),
              fs=W((H, LANE), F32), fr=W((H, LANE), F32), tmp=W((2, 5, PART, LANE), BF16))
    sc.update(rsem=DMA((2, n)), ssem=DMA((2, 9 * Z)), hsem=DMA((4,)), tsem=DMA((6,)), osem=DMA((1,)), vsem=DMA((5,)), fsem=DMA((2, 5)),
              r_sib=DMA((2, n // 2)), s_sib=DMA((2, n // 2)), r_second=DMA((2, 2 * Z)), s_second=DMA((2, 2 * Z)), r_first=DMA((2, Z)), s_first=DMA((2, Z)),
              r_above=DMA((2, Z)), r_below=DMA((2, Z)), s_line=DMA((2, Z)))
    res = pl.pallas_call(
        functools.partial(fused_kernel, geo, rows, list(ins), list(outs), list(sc)),
        out_shape=[s for _, s in outs.values()],
        in_specs=[V] * len(ins),
        out_specs=[b for b, _ in outs.values()],
        scratch_shapes=list(sc.values()),
        compiler_params=pltpu.CompilerParams(collective_id=0, has_side_effects=True, vmem_limit_bytes=64 << 20),
        name="layer",
    )(*ins.values())
    mol, cg, outl, outc = res[:4]
    return (mol.reshape(micro, span // RATE, D), cg.reshape(micro, span, D), outl.reshape(-1)[:local_params.shape[0]], outc.reshape(-1)[:conv_params.shape[0]])


def on_device(characters, segment_ids, cotangent, local_params, conv_params):
    n = lax.axis_size("fsdp")
    rows = characters.shape[0] * characters.shape[1]
    whole = n % 8 == 0 and (2 * 72 * D) % (n * UNIT) == 0 and (2 * 24 * D) % (n * UNIT) == 0
    exact = local_params.shape[0] * n == LOCAL_COUNT and conv_params.shape[0] * n == CONV_COUNT
    if whole and exact and rows == 4 * WINDOW:
        return fused(n, characters, segment_ids, cotangent, local_params, conv_params)
    return plain_device(characters, segment_ids, cotangent, local_params, conv_params)


def solution(mesh):
    return jax.shard_map(
        on_device,
        mesh=mesh,
        in_specs=(P(None, "fsdp", None), P(None, "fsdp"), P(None, "fsdp", None), P("fsdp"), P("fsdp")),
        out_specs=(P(None, "fsdp", None), P(None, "fsdp", None), P("fsdp"), P("fsdp")),
        check_vma=False,
    )
```

```python
import functools
import math
from types import SimpleNamespace

import jax
import jax.numpy as jnp
from jax import lax
from jax.experimental import pallas as pl
from jax.experimental.pallas import tpu as pltpu
from jax.sharding import PartitionSpec as P

MESH = pl.DeviceIdType.MESH
F32, BF16 = jnp.float32, jnp.bfloat16
D, FF, HEADS, WINDOW, RATE, MICRO, HEAD_SIZE = 768, 3072, 12, 128, 4, 2, 64
LOCAL_COUNT, CONV_COUNT = 7087104, 2361600
LANE = 128
UNIT = 1152
EPS = EPSILON = 1e-05


DC = D // LANE
FC = FF // LANE
VB1, VG1, VS1, VBQ, VBV, VBO, VG2, VS2, VB2 = 0, 24, 30, 36, 42, 48, 54, 60, 66
VBC, VG3, VS3 = 78, 84, 90
QKV_ROW, O_ROW, W1_ROW, W2_ROW = 0, 18 * D, 24 * D, 48 * D

def nn(a, b): return jnp.dot(a, b, preferred_element_type=F32)
def nt(a, b): return lax.dot_general(a, b, (((1,), (1,)), ((), ())), preferred_element_type=F32)
def tn(a, b): return lax.dot_general(a, b, (((0,), (0,)), ((), ())), preferred_element_type=F32)

def loop(n, fn, unroll=1):
    def body(i, _):
        fn(i)
        return 0
    lax.fori_loop(0, n, body, 0, unroll=unroll)

def span(lo, hi, n, fn, unroll=1):
    hi = n if hi is None else hi
    def body(i, _):
        fn(i)
        return 0
    lax.fori_loop(lo, hi, body, 0, unroll=unroll)

def at(i, size): return pl.ds(pl.multiple_of(i * size, size), size)

def vec(r, row, blocks=DC):
    return jnp.concatenate([r.vecs[row + i:row + i + 1, :] for i in range(blocks)], axis=1)

def put(r, row, value):
    for i in range(value.shape[1] // LANE):
        r.vgrad[row + i:row + i + 1, :] = value[:, i * LANE:(i + 1) * LANE]

def add_to(r, row, value):
    for i in range(value.shape[1] // LANE):
        r.vgrad[row + i:row + i + 1, :] += value[:, i * LANE:(i + 1) * LANE]

def normal(v):
    mean = jnp.mean(v, axis=-1, keepdims=True)
    cen = v - mean
    var = jnp.mean(cen * cen, axis=-1, keepdims=True)
    s = lax.rsqrt(var + EPS)
    return cen * s, s

def normal_back(dn, nrm, s):
    return s * (dn - jnp.mean(dn, axis=-1, keepdims=True) - nrm * jnp.mean(dn * nrm, axis=-1, keepdims=True))

def colsum(v): return jnp.sum(v, axis=0, keepdims=True)

def gelu_both(h):
    cdf = 0.5 + 0.5 * lax.erf(h * (0.5 ** 0.5))
    pdf = jnp.exp(-0.5 * h * h) * (1.0 / math.sqrt(2 * math.pi))
    return h * cdf, cdf + h * pdf

RB = 64
def forward_norm(r):
    g1, s1 = vec(r, VG1), vec(r, VS1)
    def f(i):
        nrm, _ = normal(r.x[at(i, RB), :].astype(F32))
        r.a[at(i, RB), :] = (nrm * g1 + s1).astype(BF16)
    loop(r.rows // RB, f, 2)

def forward_qkv(r, lo=0, hi=9):
    bias = jnp.concatenate([vec(r, VBQ), jnp.zeros((1, D), F32), vec(r, VBV)], axis=1)
    for i in range(18):
        r.bias[i:i + 1, :] = bias[:, i * LANE:(i + 1) * LANE]
    def f(i):
        b = jnp.concatenate([r.bias[pl.ds(2 * i, 1), :], r.bias[pl.ds(2 * i + 1, 1), :]], axis=1)
        r.P[:, at(i, 256)] = (nn(r.a[...], r.wqkv[:, at(i, 256)]) + b).astype(BF16)
    span(lo, hi, 9, f)

def halves(v):
    lo = lax.broadcasted_iota(jnp.int32, v.shape, 1) < 64
    w = v.astype(F32)
    z = jnp.zeros_like(w)
    return jnp.concatenate([jnp.where(lo, w, z), jnp.where(lo, z, w)], axis=0).astype(BF16)

def pick(v):
    lo = lax.broadcasted_iota(jnp.int32, (WINDOW, LANE), 1) < 64
    return jnp.where(lo, v[:WINDOW], v[WINDOW:])

def heads_of(r, i):
    w = i // DC
    hp = lax.rem(i, DC)
    rows = at(w, WINDOW)
    return w, rows, at(hp, LANE), at(hp + DC, LANE), at(hp + 2 * DC, LANE)

def forward_attention(r):
    def f(i):
        w, rows, cq, ck, cv = heads_of(r, i)
        q2 = halves(r.P[rows, cq])
        s = nt(q2, r.P[rows, ck]) * 0.125
        same = r.segc[rows, :] == r.segr[pl.ds(w, 1), :]
        same2 = jnp.concatenate([same.astype(F32)] * 2, axis=0) > 0.5
        s = jnp.where(same2, s, -1e30)
        e = jnp.exp(s - jnp.max(s, axis=-1, keepdims=True))
        p = (e / jnp.sum(e, axis=-1, keepdims=True)).astype(BF16)
        r.p[i] = p
        r.ctx[rows, cq] = pick(nn(p, r.P[rows, cv])).astype(BF16)
    loop(r.rows // WINDOW * DC, f, 4)

def forward_out(r):
    bo = vec(r, VBO)
    for i in range(3):
        c = slice(i * 256, (i + 1) * 256)
        r.y1[:, c] = r.x[:, c].astype(F32) + nn(r.ctx[...], r.wo[:, c]) + bo[:, c]
    g2, s2 = vec(r, VG2), vec(r, VS2)
    def f(i):
        nrm, _ = normal(r.y1[at(i, RB), :])
        r.c[at(i, RB), :] = (nrm * g2 + s2).astype(BF16)
    loop(r.rows // RB, f, 2)

def forward_up(r, lo=0, hi=12):
    def f(i):
        b = jnp.concatenate([r.vecs[pl.ds(VB1 + 2 * i, 1), :], r.vecs[pl.ds(VB1 + 2 * i + 1, 1), :]], axis=1)
        h = nn(r.c[...], r.w1[:, at(i, 256)]) + b
        hid, slope = gelu_both(h)
        r.hid[:, at(i, 256)] = hid.astype(BF16)
        r.slope[:, at(i, 256)] = slope.astype(BF16)
    span(lo, hi, 12, f)

def forward_down(r):
    b2 = vec(r, VB2)
    for i in range(3):
        c = slice(i * 256, (i + 1) * 256)
        v = r.y1[:, c] + nn(r.hid[...], r.w2[:, c]) + b2[:, c]
        r.ys[2 * i] = v[:, :LANE]
        r.ys[2 * i + 1] = v[:, LANE:]
    for j in range(RATE):
        for c in range(DC):
            r.u[j * r.mols:(j + 1) * r.mols, c * LANE:(c + 1) * LANE] = r.ys[c, pl.ds(j, r.mols, stride=RATE), :].astype(BF16)

def forward_conv(r):
    z = vec(r, VBC)
    for j in range(RATE):
        z = z + nn(r.u[j * r.mols:(j + 1) * r.mols, :], r.wc[j * D:(j + 1) * D, :])
    w, slope = gelu_both(z)
    nrm, s = normal(w)
    r.mol[...] = (nrm * vec(r, VG3) + vec(r, VS3)).astype(BF16)
    t = r.cot[...].astype(F32)
    put(r, VG3, colsum(t * nrm))
    put(r, VS3, colsum(t))
    dw = normal_back(t * vec(r, VG3), nrm, s)
    dz = (dw * slope).astype(BF16)
    r.dz[...] = dz
    put(r, VBC, colsum(dz.astype(F32)))

def emit_flat(r, dst, row0, tile):
    k, m = tile.shape[0], tile.shape[1] // LANE
    for c in range(m):
        r.scr[pl.ds(c, k, stride=m), :] = tile[:, c * LANE:(c + 1) * LANE]
    dst[pl.ds(pl.multiple_of(row0, 16), k * m), :] = r.scr[0:k * m, :].astype(BF16)

def grad_conv_weight(r):
    for j in range(RATE):
        def f(i):
            emit_flat(r, r.gc, (j * D + i * 256) * DC, tn(r.u[j * r.mols:(j + 1) * r.mols, at(i, 256)], r.dz[...]))
        loop(3, f)

def back_conv(r):
    for j in range(RATE):
        v = nt(r.dz[...], r.wc[j * D:(j + 1) * D, :])
        for c in range(DC):
            r.ys[c, pl.ds(j, r.mols, stride=RATE), :] = v[:, c * LANE:(c + 1) * LANE]
    for c in range(DC):
        v = r.ys[c]
        r.u[:, c * LANE:(c + 1) * LANE] = v.astype(BF16)
        put(r, VB2 + c, colsum(v))

def grad_down_weight(r, lo=0, hi=12):
    span(lo, hi, 12, lambda i: emit_flat(r, r.gl, W2_ROW + i * 256 * DC, tn(r.hid[:, at(i, 256)], r.u[...])))

def back_down(r, lo=0, hi=12):
    def f(i):
        dh = (nt(r.u[...], r.w2[at(i, 256), :]) * r.slope[:, at(i, 256)].astype(F32)).astype(BF16)
        r.slope[:, at(i, 256)] = dh
        s = colsum(dh.astype(F32))
        r.vgrad[pl.ds(VB1 + 2 * i, 1), :] = s[:, :LANE]
        r.vgrad[pl.ds(VB1 + 2 * i + 1, 1), :] = s[:, LANE:]
    span(lo, hi, 12, f)

def grad_up_weight(r, lo=0, hi=6):
    span(lo, hi, 6, lambda i: emit_flat(r, r.gl, W1_ROW + i * 128 * FC, tn(r.c[:, at(i, 128)], r.slope[...])))

def fold(v):
    out = v[0:8]
    for i in range(1, v.shape[0] // 8):
        out = out + v[i * 8:(i + 1) * 8]
    return out

def row_sums(r, fn, count):
    def body(i, acc):
        return tuple(a + fold(v) for a, v in zip(acc, fn(at(i, RB))))
    acc = lax.fori_loop(0, r.rows // RB, body, tuple(jnp.zeros((8, D), F32) for _ in range(count)), unroll=2)
    return [colsum(a) for a in acc]

def back_up(r):
    for i in range(3):
        r.dc[:, i * 256:(i + 1) * 256] = nt(r.slope[...], r.w1[i * 256:(i + 1) * 256, :])
    g2 = vec(r, VG2)
    def f(rows):
        dc = r.dc[rows, :]
        nrm, s = normal(r.y1[rows, :])
        dy2 = jnp.concatenate([r.ys[c, rows, :] for c in range(DC)], axis=1)
        dy1 = dy2 + normal_back(dc * g2, nrm, s)
        r.dc[rows, :] = dy1
        r.u[rows, :] = dy1.astype(BF16)
        return dc * nrm, dc, dy1
    sums = row_sums(r, f, 3)
    put(r, VG2, sums[0])
    put(r, VS2, sums[1])
    put(r, VBO, sums[2])

def grad_out_weight(r):
    loop(3, lambda i: emit_flat(r, r.gl, O_ROW + i * 256 * DC, tn(r.ctx[:, at(i, 256)], r.u[...])))

def back_out(r):
    for i in range(3):
        r.c[:, i * 256:(i + 1) * 256] = nt(r.u[...], r.wo[i * 256:(i + 1) * 256, :]).astype(BF16)

AG = 4
def back_attention(r, lo=0, hi=None):
    def f(i):
        where = [heads_of(r, i * AG + j) for j in range(AG)]
        loads = [(r.c[rows, cq], r.P[rows, cq], r.P[rows, ck], r.P[rows, cv], r.p[i * AG + j]) for j, (w, rows, cq, ck, cv) in enumerate(where)]
        outs = []
        for do, q, k, v, pb in loads:
            do2, q2 = halves(do), halves(q)
            p = pb.astype(F32)
            dp = nt(do2, v)
            ds = (p * (dp - jnp.sum(p * dp, axis=-1, keepdims=True))).astype(BF16)
            outs.append((pick(nn(ds, k)) * 0.125, tn(ds, q2) * 0.125, tn(pb, do2)))
        for (w, rows, cq, ck, cv), (dq, dk, dv) in zip(where, outs):
            r.P[rows, cq] = dq.astype(BF16)
            r.P[rows, ck] = dk.astype(BF16)
            r.P[rows, cv] = dv.astype(BF16)
    span(lo, hi, r.rows // WINDOW * DC // AG, f)

def grad_qkv_weight(r):
    for c in range(DC):
        r.vgrad[VBQ + c:VBQ + c + 1, :] = colsum(r.P[:, c * LANE:(c + 1) * LANE].astype(F32))
        r.vgrad[VBV + c:VBV + c + 1, :] = colsum(r.P[:, 2 * D + c * LANE:2 * D + (c + 1) * LANE].astype(F32))
    loop(6, lambda i: emit_flat(r, r.gl, QKV_ROW + i * 128 * 18, tn(r.a[:, at(i, 128)], r.P[...])))

def back_qkv(r):
    for i in range(3):
        r.y1[:, i * 256:(i + 1) * 256] = nt(r.P[...], r.wqkv[i * 256:(i + 1) * 256, :])
    g1 = vec(r, VG1)
    def f(rows):
        da = r.y1[rows, :]
        nrm, s = normal(r.x[rows, :].astype(F32))
        r.dc[rows, :] = r.dc[rows, :] + normal_back(da * g1, nrm, s)
        return da * nrm, da
    sums = row_sums(r, f, 2)
    put(r, VG1, sums[0])
    put(r, VS1, sums[1])

def state_shapes(rows):
    mols = rows // RATE
    V = pltpu.VMEM
    return dict(
        a=V((rows, D), BF16), P=V((rows, 3 * D), BF16), p=V((rows // WINDOW * DC, 2 * WINDOW, LANE), BF16),
        ctx=V((rows, D), BF16), y1=V((rows, D), F32), c=V((rows, D), BF16), slope=V((rows, FF), BF16), hid=V((rows, FF), BF16),
        ys=V((DC, rows, LANE), F32), u=V((rows, D), BF16), dz=V((mols, D), BF16), dc=V((rows, D), F32),
        scr=V((128 * FC, LANE), F32), bias=V((24, LANE), F32), vecs=V((96, LANE), F32))


class Geo:
    def __init__(self, n, local_shard, conv_shard):
        self.n = n
        self.Z = n // 8
        self.RL = (12 * D * D) // LANE // n
        self.RC = (4 * D * D) // LANE // n
        self.dl = local_shard - self.RL * LANE
        self.dc = conv_shard - self.RC * LANE
        self.HL = -(-(self.dl * n) // (8 * LANE)) * 8
        self.HC = -(-(self.dc * n) // (8 * LANE)) * 8
        self.XL = -(-local_shard // (8 * LANE)) * 8
        self.XC = -(-conv_shard // (8 * LANE)) * 8

def where_am_i():
    me = lax.axis_index("fsdp")
    core = lax.rem(me, 2)
    bx = lax.rem(me // 2, 2)
    by = lax.rem(me // 4, 2)
    z = me // 8
    sib = me + 1 - 2 * core
    xn = me + 2 - 4 * bx
    yn = me + 4 - 8 * by
    first = xn + core * (yn - xn)
    second = yn + core * (xn - yn)
    return me, core, z, sib, first, second

def realign(out_ref, out_base, lo, hi, x_ref, shift):
    q = shift // LANE
    r = lax.rem(shift, LANE)
    turn = lax.rem(LANE - r, LANE)
    lane = lax.broadcasted_iota(jnp.int32, (16, LANE), 1)
    keep = lane < (LANE - r)
    def body(i, _):
        low = x_ref[pl.ds(q + i * 16, 16), :]
        high = x_ref[pl.ds(q + i * 16 + 1, 16), :]
        val = jnp.where(keep, pltpu.roll(low, turn, 1), pltpu.roll(high, turn, 1))
        out_ref[pl.ds(pl.multiple_of(out_base + i * 16, 16), 16), :] = val.astype(out_ref.dtype)
        return 0
    lax.fori_loop(lo // 16, hi // 16, body, 0, unroll=2 if (hi - lo) % 32 == 0 else 1)

def widen(dst_ref, dst_base, src_ref, rows):
    step = 248 if rows % 248 == 0 else 8
    for i in range(rows // step):
        dst_ref[dst_base + i * step:dst_base + (i + 1) * step, :] = src_ref[i * step:(i + 1) * step, :].astype(F32)

def convert_unit(src_ref, base, w_ref, krow, cols, scr):
    groups = UNIT // (16 * cols)
    def body(g, _):
        scr[0:16 * cols, :] = src_ref[pl.ds(pl.multiple_of(base + g * 16 * cols, 16), 16 * cols), :].astype(F32)
        for cc in range(cols):
            v = scr[pl.ds(cc, 16, stride=cols), :]
            w_ref[pl.ds(pl.multiple_of(krow + g * 16, 16), 16), cc * LANE:(cc + 1) * LANE] = v.astype(BF16)
        return 0
    lax.fori_loop(0, groups, body, 0)


def start_gather(g):
    n, Z, geo, me, z = g.n, g.Z, g.geo, g.me, g.z
    RL, RC = geo.RL, geo.RC
    nxt = lax.rem(me + 1, n)
    bar = pltpu.get_barrier_semaphore()
    far = lax.rem(me + n + 2 * g.core - 1, n)
    for dev in (g.sib, g.first, g.second, far):
        pl.semaphore_signal(bar, inc=1, device_id=(dev,), device_id_type=MESH)
    @pl.when(z > 0)
    def _(): pl.semaphore_signal(bar, inc=1, device_id=(me - 8,), device_id_type=MESH)
    @pl.when(z < Z - 1)
    def _(): pl.semaphore_signal(bar, inc=1, device_id=(me + 8,), device_id_type=MESH)
    widen(g.xlf, geo.HL, g.xl, geo.XL)
    widen(g.xcf, geo.HC, g.xc, geo.XC)
    HA, HB = 80, 32
    lshift, cshift = geo.HL * LANE - geo.dl * me, geo.HC * LANE - geo.dc * me
    realign(g.gl, me * RL, HA, RL, g.xlf, lshift)
    realign(g.gc, me * RC, HB, RC, g.xcf, cshift)
    pl.semaphore_wait(bar, 4 + jnp.where(z > 0, 1, 0) + jnp.where(z < Z - 1, 1, 0))
    halo = pltpu.make_async_remote_copy(src_ref=g.hb, dst_ref=g.hr, send_sem=g.hsem.at[0], recv_sem=g.hsem.at[1], device_id=(nxt,), device_id_type=MESH)
    halo.start()
    halo.wait()
    g.xlf[0:geo.HL, :] = g.hr[0:geo.HL, :].astype(F32)
    g.xcf[0:geo.HC, :] = g.hr[geo.HL:geo.HL + geo.HC, :].astype(F32)
    realign(g.gl, me * RL, 0, HA, g.xlf, lshift)
    realign(g.gc, me * RC, 0, HB, g.xcf, cshift)
    @pl.when(me == n - 1)
    def _():
        g.tail[...] = g.hb[...]


def gather_weights(g):
    n, Z, geo, me, z = g.n, g.Z, g.geo, g.me, g.z
    RL, RC = geo.RL, geo.RC
    sib, first, second, last = g.sib, g.first, g.second, n - 1
    size, place = (RL, RC), (g.gl, g.gc)
    def copy(k, src, dev, slot):
        ref = place[k].at[pl.ds(pl.multiple_of(src * size[k], 16), size[k])]
        return pltpu.make_async_remote_copy(src_ref=ref, dst_ref=ref, send_sem=g.ssem.at[k, slot], recv_sem=g.rsem.at[k, src], device_id=(dev,), device_id_type=MESH)
    def tail_copy(dev, slot):
        return pltpu.make_async_remote_copy(src_ref=g.tail, dst_ref=g.tail, send_sem=g.tsem.at[slot], recv_sem=g.tsem.at[5], device_id=(dev,), device_id_type=MESH)
    UP, DN, FI, SE, SI = 0, Z, 2 * Z, 3 * Z, 5 * Z
    def both(k, src, dev, slot, tslot, act):
        act(copy(k, src, dev, slot))
        if k == 0:
            @pl.when(src == last)
            def _(): act(tail_copy(dev, tslot))
    def send(k, src, dev, slot, tslot): both(k, src, dev, slot, tslot, lambda c: c.start())
    def await_recv(k, src): both(k, src, sib, 0, 0, lambda c: c.wait_recv())
    def drain(k, src, dev, slot, tslot): both(k, src, dev, slot, tslot, lambda c: c.wait_send())
    def valid(dz): return jnp.logical_and(z + dz >= 0, z + dz < Z)
    def src_of(dz, f, s): return me + 8 * dz + f * (first - me) + s * (second - me)
    def column(k, dz, act):
        src = src_of(dz, 0, 0)
        zi = z + dz
        if dz >= 0:
            @pl.when(z > 0)
            def _(): act(k, src, me - 8, DN + zi, 0)
        if dz <= 0:
            @pl.when(z < Z - 1)
            def _(): act(k, src, me + 8, UP + zi, 1)
        act(k, src, first, FI + zi, 2)
        act(k, src, second, SE + zi, 3)
        act(k, src, sib, SI + zi, 4)
    def firsts(k, dz, act):
        src = src_of(dz, 1, 0)
        act(k, src, second, SE + Z + z + dz, 3)
        act(k, src, sib, SI + Z + z + dz, 4)
    def seconds(k, dz, f, act):
        act(k, src_of(dz, f, 1), sib, SI + (2 + f) * Z + z + dz, 4)
    def convert(k, dz):
        for f in (0, 1):
            for s in (0, 1):
                src = src_of(dz, f, s)
                await_recv(k, src + sib - me)
                chip = src // 2
                if k == 1:
                    for i in range(2 * RC // UNIT):
                        t = chip * (2 * RC // UNIT) + i
                        convert_unit(g.gc, t * UNIT, g.wc, t * 192, 6, g.scr)
                    continue
                for i in range(2 * RL // UNIT):
                    t = chip * (2 * RL // UNIT) + i
                    base = t * UNIT
                    @pl.when(t < 12)
                    def _(): convert_unit(g.gl, base, g.wqkv, t * 64, 18, g.scr)
                    @pl.when(jnp.logical_and(t >= 12, t < 16))
                    def _(): convert_unit(g.gl, base, g.wo, (t - 12) * 192, 6, g.scr)
                    @pl.when(jnp.logical_and(t >= 16, t < 32))
                    def _(): convert_unit(g.gl, base, g.w1, (t - 16) * 48, 24, g.scr)
                    @pl.when(t >= 32)
                    def _(): convert_unit(g.gl, base, g.w2, (t - 32) * 192, 6, g.scr)
    def guarded(level, fn):
        for dz in ([0] if level == 0 else [level, -level] if level < Z else []):
            @pl.when(valid(dz))
            def _(): fn(dz)
    def e1(k, level):
        def fn(dz):
            if dz != 0: await_recv(k, src_of(dz, 0, 0))
            column(k, dz, send)
        guarded(level, fn)
    def e2(k, level):
        def fn(dz):
            await_recv(k, src_of(dz, 1, 0))
            firsts(k, dz, send)
            await_recv(k, src_of(dz, 0, 1))
            seconds(k, dz, 0, send)
        guarded(level, fn)
    def e4(k, level):
        def fn(dz):
            await_recv(k, src_of(dz, 1, 1))
            seconds(k, dz, 1, send)
        guarded(level, fn)
    def conv(k, level): guarded(level, lambda dz: convert(k, dz))
    def finish(k):
        def fn(dz):
            column(k, dz, drain)
            firsts(k, dz, drain)
            seconds(k, dz, 0, drain)
            seconds(k, dz, 1, drain)
        for level in range(Z): guarded(level, fn)
    return SimpleNamespace(e1=e1, e2=e2, e4=e4, conv=conv, finish=finish)


PART = 576


RING = 4


class Scatter:
    def __init__(self, g, steps, jobs):
        self.g = g
        self.size = (g.geo.RL, g.geo.RC)
        self.own = (g.gl, g.gc)
        self.jobs = [j for it in jobs for j in it]
        self.started, self.granted, self.waiting = set(), set(), []
        self.opened = self.closed = 0

    def target(self, zt, f, s):
        g = self.g
        return g.me + 8 * (zt - g.z) + f * (g.first - g.me) + s * (g.second - g.me)

    def other(self, zt, f, s): return self.target(zt, f, s) + self.g.sib - self.g.me

    def rows(self, k, t, p):
        return pl.ds(pl.multiple_of(t * self.size[k] + p * PART, 16), PART)

    def sem(self, k, p):
        return p if k == 0 else self.size[0] // PART + p

    def move(self, src, dst, send, recv, i, index, dev):
        return pltpu.make_async_remote_copy(src_ref=src, dst_ref=dst, send_sem=send.at[i, index], recv_sem=recv.at[i, index], device_id=(dev,), device_id_type=MESH)

    def at(self, k, p, t): return self.own[k].at[self.rows(k, t, p)]

    def to_sib(self, k, p, t):
        g = self.g
        return self.move(self.at(k, p, t), g.from_sib[k].at[self.rows(k, t // 2, p)], g.s_sib, g.r_sib, self.sem(k, p), t // 2, g.sib)

    def to_second(self, k, p, zt, f):
        g = self.g
        t = self.target(zt, f, 1)
        return self.move(self.at(k, p, t), self.at(k, p, t + g.sib - g.me), g.s_second, g.r_second, self.sem(k, p), 2 * zt + f, g.second)

    def to_first(self, k, p, zt):
        g = self.g
        t = self.target(zt, 1, 0)
        return self.move(self.at(k, p, t), self.at(k, p, t + g.second - g.me + g.sib - g.me), g.s_first, g.r_first, self.sem(k, p), zt, g.first)

    def down(self, k, p, zt):
        g = self.g
        return self.move(self.at(k, p, self.target(zt, 0, 0)), self.at(k, p, self.other(zt, 1, 1)), g.s_down, g.r_down, self.sem(k, p), zt, g.me - 8)

    def up(self, k, p, zt, land):
        g = self.g
        dst = (g.below_l, g.below_c)[k].at[pl.ds(p * PART, PART)] if land else self.at(k, p, self.other(zt, 1, 1))
        return self.move(self.at(k, p, self.target(zt, 0, 0)), dst, g.s_up, g.r_up, self.sem(k, p), zt, g.me + 8)

    def p0(self, k, p, zt):
        for f in (0, 1):
            for s in (0, 1):
                self.to_sib(k, p, self.other(zt, f, s)).start()
        self.started.add((k, p, zt))
        self.waiting.append((k, p, zt))

    def credit(self, which, dev):
        pl.semaphore_signal(self.g.credit.at[which], inc=1, device_id=(dev,), device_id_type=MESH)

    def grant(self, k, p, zt):
        g = self.g
        z, Z, me = g.z, g.Z, g.me
        for f in (0, 1):
            for s in (0, 1):
                self.to_sib(k, p, self.other(zt, f, s)).wait_send()
        self.credit(0, g.second)
        self.credit(1, g.first)
        if zt < Z - 1:
            @pl.when(jnp.logical_and(z >= zt, z < Z - 1))
            def _(): self.credit(2, me + 8)
        if zt > 1:
            @pl.when(jnp.logical_and(z < zt, z > 0))
            def _(): self.credit(3, me - 8)
        self.granted.add((k, p, zt))

    def grant_all(self):
        for st in self.waiting: self.grant(*st)
        self.waiting = []

    def spend(self, which): pl.semaphore_wait(self.g.credit.at[which], 1)

    def place(self, job):
        kind, (k, p, zt), x = job
        z, Z = self.g.z, self.g.Z
        if kind == "second": return None, self.target(zt, x, 1)
        if kind == "first": return None, self.target(zt, 1, 0)
        if kind == "last": return z == zt, self.target(zt, 0, 0)
        return z == (x[0] if x[1] else Z - 1 - x[0]), self.target(zt, 0, 0)

    def describe(self, job):
        kind, (k, p, zt), x = job
        g = self.g
        z, Z, me = g.z, g.Z, g.me
        if kind == "second":
            def send():
                if x == 1: self.spend(0)
                self.to_second(k, p, zt, x).start()
            return [], [], None, send
        if kind == "first":
            def send():
                self.spend(1)
                self.to_first(k, p, zt).start()
            return [self.to_second(k, p, zt, 1)], [self.at(k, p, self.other(zt, 1, 0))], None, send
        waits = [self.to_second(k, p, zt, 0), self.to_first(k, p, zt)]
        lands = [self.at(k, p, self.other(zt, 0, 0)), self.at(k, p, self.other(zt, 0, 1))]
        far = self.at(k, p, self.other(zt, 1, 1))
        if kind == "last":
            if zt < Z - 1:
                waits.append(self.down(k, p, zt))
                lands.append(far)
            if zt > 0:
                waits.append(self.up(k, p, zt, True))
                lands.append((g.below_l, g.below_c)[k].at[pl.ds(p * PART, PART)])
            return waits, lands, (g.xlf, g.xcf)[k], None
        hop, upward = x
        if hop > 0:
            waits.append(self.up(k, p, zt, False) if upward else self.down(k, p, zt))
            lands.append(far)
        here = hop if upward else Z - 1 - hop
        def send():
            if upward:
                if here + 1 < zt: self.spend(3)
                self.up(k, p, zt, here + 1 == zt).start()
            else:
                self.spend(2)
                self.down(k, p, zt).start()
        return waits, lands, None, send

    def guard(self, cond, fn):
        if cond is None: fn()
        else: pl.when(cond)(fn)

    def fetch(self, job, t, slot):
        g, (k, p, zt) = self.g, job[1]
        return pltpu.make_async_copy(g.from_sib[k].at[self.rows(k, t // 2, p)], g.tmp.at[slot], g.fsem.at[slot])

    def open(self, i):
        job = self.jobs[i]
        cond, t = self.place(job)
        def fn():
            self.to_sib(*job[1][:2], t).wait_recv()
            self.fetch(job, t, i % RING).start()
        self.guard(cond, fn)

    def close(self, i):
        g, job, slot = self.g, self.jobs[i], i % RING
        k, p, zt = job[1]
        cond, t = self.place(job)
        def fn():
            waits, lands, out, send = self.describe(job)
            for cp in waits: cp.wait_recv()
            self.fetch(job, t, slot).wait()
            mine = self.at(k, p, t)
            def body(b, _):
                r = pl.ds(pl.multiple_of(b * 16, 16), 16)
                acc = mine[r, :].astype(F32) + g.tmp[slot, r, :].astype(F32)
                for land in lands: acc = acc + land[r, :].astype(F32)
                if out is None: mine[r, :] = acc.astype(BF16)
                else: out[pl.ds(pl.multiple_of(p * PART + b * 16, 16), 16), :] = acc
                return 0
            lax.fori_loop(0, PART // 16, body, 0, unroll=4)
            if send is not None: send()
        self.guard(cond, fn)

    def run(self, count):
        for _ in range(count):
            i = self.closed
            step = self.jobs[i][1]
            if step not in self.granted: self.grant_all()
            while self.opened < len(self.jobs) and self.opened < i + RING and self.jobs[self.opened][1] in self.started:
                self.open(self.opened)
                self.opened += 1
            self.close(i)
            self.closed += 1

    def finish(self, k, p, zt):
        g = self.g
        for f in (0, 1): self.to_second(k, p, zt, f).wait_send()
        self.to_first(k, p, zt).wait_send()
        @pl.when(g.z > zt)
        def _(): self.down(k, p, zt).wait_send()
        @pl.when(g.z < zt)
        def _(): self.up(k, p, zt, False).wait_send()


def plan_jobs(Z, steps, l2, l3, hop_lag, last_lag):
    n = len(steps)
    rounds = [[] for _ in range(n + l3 + hop_lag * Z + last_lag + 1)]
    for i, (k, p, zt) in enumerate(steps):
        st = steps[i]
        rounds[i] += [("second", st, 1), ("second", st, 0)]
        rounds[i + l2].append(("first", st, None))
    for i, st in enumerate(steps):
        zt = st[2]
        for hop in range(zt): rounds[i + l3 + hop_lag * hop].append(("line", st, (hop, True)))
        for hop in range(Z - 1 - zt): rounds[i + l3 + hop_lag * hop].append(("line", st, (hop, False)))
    for i, st in enumerate(steps):
        rounds[i + l3 + hop_lag * max(st[2], Z - 1 - st[2]) + last_lag].append(("last", st, None))
    order = {"second": 0, "first": 1, "line": 2, "last": 3}
    return [sorted(r, key=lambda j: order[j[0]]) for r in rounds]


def reduce_vectors(g):
    Z, me, z = g.Z, g.me, g.z
    core = lax.rem(me, 2)
    bx, by = lax.rem(me // 2, 2), lax.rem(me // 4, 2)
    def cp(slot, dev):
        return pltpu.make_async_remote_copy(src_ref=g.vgrad, dst_ref=g.vland.at[slot], send_sem=g.vsem.at[0], recv_sem=g.vsem.at[1 + slot], device_id=(dev,), device_id_type=MESH)
    def take(slot):
        cp(slot, g.sib).wait_recv()
        g.vgrad[...] = g.vgrad[...] + g.vland[slot]
    def give(slot, dev):
        c = cp(slot, dev)
        c.start()
        c.wait_send()
    on = core == 1
    def stage0():
        @pl.when(jnp.logical_not(on))
        def _(): give(0, g.sib)
        @pl.when(on)
        def _(): take(0)
    def stage1():
        @pl.when(jnp.logical_and(on, bx == 0))
        def _(): give(1, g.second)
        @pl.when(jnp.logical_and(on, bx == 1))
        def _(): take(1)
    def stage2():
        @pl.when(jnp.logical_and(on, jnp.logical_and(bx == 1, by == 0)))
        def _(): give(2, g.first)
        @pl.when(jnp.logical_and(on, jnp.logical_and(bx == 1, by == 1)))
        def _(): take(2)
    def stage3():
        @pl.when(jnp.logical_and(on, jnp.logical_and(bx == 1, by == 1)))
        def _():
            @pl.when(z > 0)
            def _(): take(3)
            @pl.when(z < Z - 1)
            def _(): give(3, me + 8)
    return stage0, stage1, stage2, stage3


def place_gradients(g):
    n, geo, me = g.n, g.geo, g.me
    prv = lax.rem(me + n - 1, n)
    HL, HC = geo.HL, geo.HC
    g.fs[0:HL, :] = g.xlf[0:HL, :]
    g.fs[HL:HL + HC, :] = g.xcf[0:HC, :]
    cp = pltpu.make_async_remote_copy(src_ref=g.fs, dst_ref=g.fr, send_sem=g.hsem.at[2], recv_sem=g.hsem.at[3], device_id=(prv,), device_id_type=MESH)
    cp.start()
    cp.wait()
    edge = me == n - 1
    g.xlf[geo.RL:geo.RL + HL, :] = jnp.where(edge, g.vgrad[0:HL, :], g.fr[0:HL, :])
    skip = VBC - HL
    g.xcf[geo.RC:geo.RC + HC - skip, :] = jnp.where(edge, g.vgrad[VBC:HL + HC, :], g.fr[HL:HL + HC - skip, :])
    realign(g.outl, 0, 0, geo.XL // 16 * 16 + 16, g.xlf, geo.dl * me)
    realign(g.outc, 0, 0, geo.XC // 16 * 16 + 16, g.xcf, geo.dc * me)


def local_layout():
    return ((D, 3 * D), (D, D), (D, FF), (FF, D), (FF,)) + ((D,),) * 8


def conv_layout():
    return ((RATE * D, D), (D,), (D,), (D,))


def unpack(packed, layout):
    offset = 0
    pieces = []
    for extent in layout:
        length = math.prod(extent)
        pieces.append(packed[offset : offset + length].reshape(extent))
        offset = offset + length
    return pieces


def normalize_parts(values):
    average = jnp.mean(values, axis=-1, keepdims=True)
    centred = values - average
    spread = jnp.mean(centred * centred, axis=-1, keepdims=True)
    scaling = lax.rsqrt(spread + EPSILON)
    return (centred * scaling, scaling)


def normal_back(grad_normed, normed, scaling):
    first_mean = jnp.mean(grad_normed, axis=-1, keepdims=True)
    second_mean = jnp.mean(grad_normed * normed, axis=-1, keepdims=True)
    return scaling * (grad_normed - first_mean - normed * second_mean)


def product(left, right):
    return jnp.dot(left, right, preferred_element_type=jnp.float32)


def rows_inner(left, right):
    return lax.dot_general(
        left, right, (((0,), (0,)), ((), ())), preferred_element_type=jnp.float32
    )


def times_transpose(left, right):
    return lax.dot_general(
        left, right, (((1,), (1,)), ((), ())), preferred_element_type=jnp.float32
    )


def gelu_exact(values):
    return jax.nn.gelu(values, approximate=False)


def gelu_grad(values, upstream):
    return jax.vjp(gelu_exact, values)[1](upstream)[0]


def window_scores(projected, segments_block):
    row_count = projected.shape[0]
    windows = row_count // WINDOW
    heads_view = projected.reshape(windows, WINDOW, 3, HEADS, HEAD_SIZE)
    queries = heads_view[:, :, 0]
    keys_all = heads_view[:, :, 1]
    values = heads_view[:, :, 2]
    scores = jnp.einsum(
        "bqhe,bkhe->bhqk", queries, keys_all, preferred_element_type=jnp.float32
    ) * HEAD_SIZE ** (-0.5)
    grouped = segments_block.reshape(windows, WINDOW)
    allowed = grouped[:, None, :, None] == grouped[:, None, None, :]
    return (jnp.where(allowed, scores, -1e30), queries, keys_all, values)


def forward_pass(characters_block, segments_block, local_weights, conv_weights):
    (
        qkv_weight,
        out_weight,
        in_weight,
        down_weight,
        in_bias,
        gain_one,
        shift_one,
        query_bias,
        value_bias,
        out_bias,
        gain_two,
        shift_two,
        down_bias,
    ) = local_weights
    conv_weight, conv_bias, gain_three, shift_three = conv_weights
    row_count = characters_block.shape[0]
    inputs = characters_block.astype(jnp.float32)
    norm_one, scale_one = normalize_parts(inputs)
    normed = (norm_one * gain_one + shift_one).astype(jnp.bfloat16)
    proj_bias = jnp.concatenate([query_bias, jnp.zeros_like(query_bias), value_bias])
    projected = (product(normed, qkv_weight) + proj_bias).astype(jnp.bfloat16)
    scores, queries, keys_all, values = window_scores(projected, segments_block)
    largest = jnp.max(scores, axis=-1, keepdims=True)
    raised = jnp.exp(scores - largest)
    totals = jnp.sum(raised, axis=-1, keepdims=True)
    log_totals = largest + jnp.log(totals)
    weights = (raised / totals).astype(jnp.bfloat16)
    attended = jnp.einsum("bhqk,bkhe->bqhe", weights, values, preferred_element_type=jnp.float32)
    context = attended.reshape(row_count, D).astype(jnp.bfloat16)
    after_attention = inputs + product(context, out_weight) + out_bias
    norm_two, scale_two = normalize_parts(after_attention)
    middle = (norm_two * gain_two + shift_two).astype(jnp.bfloat16)
    pre_act = product(middle, in_weight) + in_bias
    hidden = gelu_exact(pre_act).astype(jnp.bfloat16)
    after_feed = after_attention + product(hidden, down_weight) + down_bias
    grouped_rows = after_feed.astype(jnp.bfloat16).reshape(row_count // RATE, RATE * D)
    conv_pre = product(grouped_rows, conv_weight) + conv_bias
    norm_three, scale_three = normalize_parts(gelu_exact(conv_pre))
    molecules = (norm_three * gain_three + shift_three).astype(jnp.bfloat16)
    saved_state = (
        segments_block,
        norm_one,
        scale_one,
        normed,
        projected,
        log_totals,
        context,
        norm_two,
        scale_two,
        middle,
        pre_act,
        hidden,
        grouped_rows,
        conv_pre,
        norm_three,
        scale_three,
    )
    return (molecules, saved_state)


def backward_pass(cotangent_block, saved_state, local_weights, conv_weights):
    (
        qkv_weight,
        out_weight,
        in_weight,
        down_weight,
        in_bias,
        gain_one,
        shift_one,
        query_bias,
        value_bias,
        out_bias,
        gain_two,
        shift_two,
        down_bias,
    ) = local_weights
    conv_weight, conv_bias, gain_three, shift_three = conv_weights
    (
        segments_block,
        norm_one,
        scale_one,
        normed,
        projected,
        log_totals,
        context,
        norm_two,
        scale_two,
        middle,
        pre_act,
        hidden,
        grouped_rows,
        conv_pre,
        norm_three,
        scale_three,
    ) = saved_state
    row_count = normed.shape[0]
    windows = row_count // WINDOW
    upstream = cotangent_block.astype(jnp.float32)
    grad_gain_three = jnp.sum(upstream * norm_three, axis=0)
    grad_shift_three = jnp.sum(upstream, axis=0)
    grad_activated = normal_back(upstream * gain_three, norm_three, scale_three)
    grad_conv_pre = gelu_grad(conv_pre, grad_activated).astype(jnp.bfloat16)
    grad_conv_bias = jnp.sum(grad_conv_pre.astype(jnp.float32), axis=0)
    grad_conv_weight = rows_inner(grouped_rows, grad_conv_pre)
    grad_feed = times_transpose(grad_conv_pre, conv_weight).reshape(row_count, D)
    grad_down_bias = jnp.sum(grad_feed, axis=0)
    grad_branch = grad_feed.astype(jnp.bfloat16)
    grad_down_weight = rows_inner(hidden, grad_branch)
    grad_hidden = times_transpose(grad_branch, down_weight)
    grad_pre = gelu_grad(pre_act, grad_hidden).astype(jnp.bfloat16)
    grad_in_bias = jnp.sum(grad_pre.astype(jnp.float32), axis=0)
    grad_in_weight = rows_inner(middle, grad_pre)
    grad_middle = times_transpose(grad_pre, in_weight)
    grad_gain_two = jnp.sum(grad_middle * norm_two, axis=0)
    grad_shift_two = jnp.sum(grad_middle, axis=0)
    grad_attention = grad_feed + normal_back(grad_middle * gain_two, norm_two, scale_two)
    grad_out_bias = jnp.sum(grad_attention, axis=0)
    grad_attn_out = grad_attention.astype(jnp.bfloat16)
    grad_out_weight = rows_inner(context, grad_attn_out)
    grad_context = times_transpose(grad_attn_out, out_weight).astype(jnp.bfloat16)
    grad_heads = grad_context.reshape(windows, WINDOW, HEADS, HEAD_SIZE)
    scores, queries, keys_all, values = window_scores(projected, segments_block)
    probs = jnp.exp(scores - log_totals)
    weights = probs.astype(jnp.bfloat16)
    grad_weights = jnp.einsum(
        "bqhe,bkhe->bhqk", grad_heads, values, preferred_element_type=jnp.float32
    )
    row_terms = jnp.sum(probs * grad_weights, axis=-1, keepdims=True)
    grad_scores = (probs * (grad_weights - row_terms)).astype(jnp.bfloat16)
    grad_queries = jnp.einsum(
        "bhqk,bkhe->bqhe", grad_scores, keys_all, preferred_element_type=jnp.float32
    ) * HEAD_SIZE ** (-0.5)
    grad_keys = jnp.einsum(
        "bhqk,bqhe->bkhe", grad_scores, queries, preferred_element_type=jnp.float32
    ) * HEAD_SIZE ** (-0.5)
    grad_values = jnp.einsum(
        "bhqk,bqhe->bkhe", weights, grad_heads, preferred_element_type=jnp.float32
    )
    grad_proj = (
        jnp.stack([grad_queries, grad_keys, grad_values], axis=2)
        .reshape(row_count, 3 * D)
        .astype(jnp.bfloat16)
    )
    proj_sums = jnp.sum(grad_proj.astype(jnp.float32), axis=0)
    grad_query_bias = proj_sums[:D]
    grad_value_bias = proj_sums[2 * D :]
    grad_qkv_weight = rows_inner(normed, grad_proj)
    grad_normed = times_transpose(grad_proj, qkv_weight)
    grad_gain_one = jnp.sum(grad_normed * norm_one, axis=0)
    grad_shift_one = jnp.sum(grad_normed, axis=0)
    grad_inputs = grad_attention + normal_back(grad_normed * gain_one, norm_one, scale_one)
    local_grad = jnp.concatenate(
        [
            grad_qkv_weight.reshape(-1),
            grad_out_weight.reshape(-1),
            grad_in_weight.reshape(-1),
            grad_down_weight.reshape(-1),
            grad_in_bias,
            grad_gain_one,
            grad_shift_one,
            grad_query_bias,
            grad_value_bias,
            grad_out_bias,
            grad_gain_two,
            grad_shift_two,
            grad_down_bias,
        ]
    )
    conv_grad = jnp.concatenate(
        [grad_conv_weight.reshape(-1), grad_conv_bias, grad_gain_three, grad_shift_three]
    )
    return (grad_inputs, local_grad, conv_grad)


def plain_device(characters, segment_ids, cotangent, local_params, conv_params):
    devices = lax.axis_size("fsdp")
    local_shard = local_params.shape[0]
    conv_shard = conv_params.shape[0]
    local_pad = local_shard * devices - LOCAL_COUNT
    conv_pad = conv_shard * devices - CONV_COUNT
    local_total = jnp.zeros((1, local_shard), jnp.float32)
    conv_total = jnp.zeros((1, conv_shard), jnp.float32)
    molecule_list = []
    gradient_list = []
    for micro_index in range(MICRO):
        local_full, conv_full = (
            lax.all_gather(local_params, "fsdp", axis=0, tiled=True),
            lax.all_gather(conv_params, "fsdp", axis=0, tiled=True),
        )
        molecules, saved_state = forward_pass(
            characters[micro_index],
            segment_ids[micro_index],
            unpack(local_full, local_layout()),
            unpack(conv_full, conv_layout()),
        )
        local_full, conv_full = (
            lax.all_gather(local_params, "fsdp", axis=0, tiled=True),
            lax.all_gather(conv_params, "fsdp", axis=0, tiled=True),
        )
        grad_inputs, local_grad, conv_grad = backward_pass(
            cotangent[micro_index],
            saved_state,
            unpack(local_full, local_layout()),
            unpack(conv_full, conv_layout()),
        )
        local_table = jnp.concatenate([local_grad, jnp.zeros((local_pad,), jnp.float32)]).reshape(
            devices, local_shard
        )
        conv_table = jnp.concatenate([conv_grad, jnp.zeros((conv_pad,), jnp.float32)]).reshape(
            devices, conv_shard
        )
        local_part, conv_part = (
            lax.psum_scatter(local_table, "fsdp", scatter_dimension=0, tiled=True),
            lax.psum_scatter(conv_table, "fsdp", scatter_dimension=0, tiled=True),
        )
        local_total = local_total + local_part
        conv_total = conv_total + conv_part
        molecule_list.append(molecules)
        gradient_list.append(grad_inputs)
    return (
        jnp.stack(molecule_list),
        jnp.stack(gradient_list),
        local_total.reshape(-1),
        conv_total.reshape(-1),
    )


def fused_kernel(geo, rows, in_names, out_names, scratch_names, *refs):
    n_in, n_out = len(in_names), len(out_names)
    every = dict(zip(list(in_names) + list(out_names) + list(scratch_names), refs))
    me, core, z, sib, first, second = where_am_i()
    g = SimpleNamespace(n=geo.n, Z=geo.Z, geo=geo, me=me, core=core, z=z, sib=sib, first=first, second=second, rows=rows, mols=rows // RATE, **every)
    g.from_sib = (every["from_sib_l"], every["from_sib_c"])
    program(g)


def program(g):
    Z = g.Z
    start_gather(g)
    ag = gather_weights(g)
    ag.e1(0, 0)
    for k in range(Z):
        ag.e1(0, k + 1)
        ag.e2(0, k)
        if k == Z - 1: ag.e1(1, 0)
        if k:
            ag.e4(0, k - 1)
            ag.conv(0, k - 1)
    ag.e4(0, Z - 1)
    ag.conv(0, Z - 1)
    g.vecs[...] = g.tail[...].astype(F32)
    ev = []
    for k in range(Z):
        ev.append(lambda k=k: (ag.e1(1, k + 1), ag.e2(1, k)))
        ev.append(lambda k=k: (ag.e4(1, k - 1), ag.conv(1, k - 1)) if k else None)
    pieces = [lambda: forward_norm(g), lambda: forward_qkv(g, 0, 5), lambda: forward_qkv(g, 5, 9), lambda: forward_attention(g), lambda: forward_out(g),
              lambda: forward_up(g, 0, 4), lambda: forward_up(g, 4, 8), lambda: forward_up(g, 8, 12)]
    for i in range(max(len(ev), len(pieces))):
        if i < len(pieces): pieces[i]()
        if i < len(ev): ev[i]()
    forward_down(g)
    ag.e4(1, Z - 1)
    ag.conv(1, Z - 1)
    forward_conv(g)
    ag.finish(0)
    ag.finish(1)
    NL, NC = g.geo.RL // PART, g.geo.RC // PART
    conv_steps = [(1, p, zt) for zt in reversed(range(Z)) for p in range(NC)]
    layer_steps = [(0, p, zt) for zt in reversed(range(Z)) for p in range(NL)]
    steps = conv_steps + layer_steps
    jobs = plan_jobs(Z, steps, *LAGS)
    sc = Scatter(g, steps, jobs)
    grad_conv_weight(g)
    for st in conv_steps: sc.p0(*st)
    def send_planes(lo, hi):
        sc.grant_all()
        for st in layer_steps:
            if lo <= st[2] < hi: sc.p0(*st)
    vec_stages = reduce_vectors(g)
    plane = 8 * g.geo.RL
    def plane_of(row): return -(-row // plane)
    q3, q2, q1 = plane_of(W2_ROW), plane_of(W1_ROW), plane_of(O_ROW)
    work = [
        lambda: (back_conv(g), grad_down_weight(g, 0, 6)),
        lambda: (grad_down_weight(g, 6, 12), send_planes(q3, Z)),
        lambda: back_down(g, 0, 6),
        lambda: back_down(g, 6, 12),
        lambda: grad_up_weight(g, 0, 3),
        lambda: (grad_up_weight(g, 3, 6), send_planes(q2, q3)),
        lambda: back_up(g),
        lambda: (grad_out_weight(g), send_planes(q1, q2), back_out(g)),
        lambda: back_attention(g, 0, 2),
        lambda: back_attention(g, 2, 4),
        lambda: back_attention(g, 4, 6),
        lambda: (grad_qkv_weight(g), send_planes(0, q1)),
        lambda: (back_qkv(g), pltpu.make_async_copy(g.dc, g.cg, g.osem.at[0]).start(), vec_stages[0]()),
        lambda: vec_stages[1](),
        lambda: vec_stages[2](),
        lambda: vec_stages[3](),
    ]
    for i in range(max(len(jobs), len(work))):
        if i < len(work): work[i]()
        if i < len(jobs): sc.run(len(jobs[i]))
    place_gradients(g)
    for st in steps: sc.finish(*st)
    pltpu.make_async_copy(g.dc, g.cg, g.osem.at[0]).wait()


LAGS = (2, 4, 2, 3)


def fused(n, characters, segment_ids, cotangent, local_params, conv_params):
    geo = Geo(n, local_params.shape[0], conv_params.shape[0])
    micro, span, _ = characters.shape
    rows = micro * span
    x = characters.reshape(rows, D)
    cot = cotangent.reshape(rows // RATE, D)
    segc = segment_ids.reshape(rows, 1)
    segr = segment_ids.reshape(rows // WINDOW, WINDOW)
    xl = jnp.pad(local_params, (0, geo.XL * LANE - local_params.shape[0])).reshape(geo.XL, LANE)
    xc = jnp.pad(conv_params, (0, geo.XC * LANE - conv_params.shape[0])).reshape(geo.XC, LANE)
    hb = jnp.concatenate([local_params[-geo.HL * LANE:], conv_params[-geo.HC * LANE:]]).reshape(geo.HL + geo.HC, LANE)
    V = pl.BlockSpec(memory_space=pltpu.VMEM)
    A = pl.BlockSpec(memory_space=pl.ANY)
    S = jax.ShapeDtypeStruct
    Z, H = geo.Z, geo.HL + geo.HC
    ins = dict(x=x, segc=segc, segr=segr, cot=cot, xl=xl, xc=xc, hb=hb)
    outs = dict(mol=(V, S((rows // RATE, D), BF16)), cg=(A, S((rows, D), F32)), outl=(V, S((geo.XL // 16 * 16 + 16, LANE), F32)), outc=(V, S((geo.XC // 16 * 16 + 16, LANE), F32)))
    for name, count in (("from_sib", n // 2),):
        outs[name + "_l"] = (A, S((count * geo.RL, LANE), BF16))
        outs[name + "_c"] = (A, S((count * geo.RC, LANE), BF16))
    W = pltpu.VMEM
    DMA = pltpu.SemaphoreType.DMA
    sc = state_shapes(rows)
    sc.update(wqkv=W((D, 3 * D), BF16), wo=W((D, D), BF16), w1=W((D, FF), BF16), w2=W((FF, D), BF16), wc=W((FF, D), BF16))
    sc.update(gl=W((n * geo.RL, LANE), BF16), gc=W((n * geo.RC, LANE), BF16), hr=W((H, LANE), BF16), tail=W((H, LANE), BF16),
              xlf=W((geo.HL + geo.XL + 32, LANE), F32), xcf=W((geo.HC + geo.XC + 32, LANE), F32), vgrad=W((H, LANE), F32), vland=W((4, H, LANE), F32),
              fs=W((H, LANE), F32), fr=W((H, LANE), F32), tmp=W((RING, PART, LANE), BF16), below_l=W((geo.RL, LANE), BF16), below_c=W((geo.RC, LANE), BF16))
    parts = (geo.RL + geo.RC) // PART
    sc.update(rsem=DMA((2, n)), ssem=DMA((2, 9 * Z)), hsem=DMA((4,)), tsem=DMA((6,)), osem=DMA((1,)), vsem=DMA((5,)), fsem=DMA((RING,)), credit=pltpu.SemaphoreType.REGULAR((4,)),
              r_sib=DMA((parts, n // 2)), s_sib=DMA((parts, n // 2)), r_second=DMA((parts, 2 * Z)), s_second=DMA((parts, 2 * Z)),
              r_first=DMA((parts, Z)), s_first=DMA((parts, Z)), r_up=DMA((parts, Z)), s_up=DMA((parts, Z)), r_down=DMA((parts, Z)), s_down=DMA((parts, Z)))
    res = pl.pallas_call(
        functools.partial(fused_kernel, geo, rows, list(ins), list(outs), list(sc)),
        out_shape=[s for _, s in outs.values()],
        in_specs=[V] * len(ins),
        out_specs=[b for b, _ in outs.values()],
        scratch_shapes=list(sc.values()),
        compiler_params=pltpu.CompilerParams(collective_id=0, has_side_effects=True, vmem_limit_bytes=64 << 20),
        name="layer",
    )(*ins.values())
    mol, cg, outl, outc = res[:4]
    return (mol.reshape(micro, span // RATE, D), cg.reshape(micro, span, D), outl.reshape(-1)[:local_params.shape[0]], outc.reshape(-1)[:conv_params.shape[0]])


def on_device(characters, segment_ids, cotangent, local_params, conv_params):
    n = lax.axis_size("fsdp")
    rows = characters.shape[0] * characters.shape[1]
    whole = n % 8 == 0 and (2 * 72 * D) % (n * UNIT) == 0 and (2 * 24 * D) % (n * UNIT) == 0
    exact = local_params.shape[0] * n == LOCAL_COUNT and conv_params.shape[0] * n == CONV_COUNT
    if whole and exact and rows == 4 * WINDOW:
        return fused(n, characters, segment_ids, cotangent, local_params, conv_params)
    return plain_device(characters, segment_ids, cotangent, local_params, conv_params)


def solution(mesh):
    return jax.shard_map(
        on_device,
        mesh=mesh,
        in_specs=(P(None, "fsdp", None), P(None, "fsdp"), P(None, "fsdp", None), P("fsdp"), P("fsdp")),
        out_specs=(P(None, "fsdp", None), P(None, "fsdp", None), P("fsdp"), P("fsdp")),
        check_vma=False,
    )
```

```python
import functools
import math
from types import SimpleNamespace

import jax
import jax.numpy as jnp
from jax import lax
from jax.experimental import pallas as pl
from jax.experimental.pallas import tpu as pltpu
from jax.sharding import PartitionSpec as P

MESH = pl.DeviceIdType.MESH
F32, BF16 = jnp.float32, jnp.bfloat16
D, FF, HEADS, WINDOW, RATE, MICRO, HEAD_SIZE = 768, 3072, 12, 128, 4, 2, 64
LOCAL_COUNT, CONV_COUNT = 7087104, 2361600
LANE = 128
UNIT = 1152
EPS = EPSILON = 1e-05


DC = D // LANE
FC = FF // LANE
VB1, VG1, VS1, VBQ, VBV, VBO, VG2, VS2, VB2 = 0, 24, 30, 36, 42, 48, 54, 60, 66
VBC, VG3, VS3 = 78, 84, 90
QKV_ROW, O_ROW, W1_ROW, W2_ROW = 0, 18 * D, 24 * D, 48 * D

def nn(a, b): return jnp.dot(a, b, preferred_element_type=F32)
def nt(a, b): return lax.dot_general(a, b, (((1,), (1,)), ((), ())), preferred_element_type=F32)
def tn(a, b): return lax.dot_general(a, b, (((0,), (0,)), ((), ())), preferred_element_type=F32)

def loop(n, fn, unroll=1):
    def body(i, _):
        fn(i)
        return 0
    lax.fori_loop(0, n, body, 0, unroll=unroll)

def span(lo, hi, n, fn, unroll=1):
    hi = n if hi is None else hi
    def body(i, _):
        fn(i)
        return 0
    lax.fori_loop(lo, hi, body, 0, unroll=unroll)

def at(i, size): return pl.ds(pl.multiple_of(i * size, size), size)

def vec(r, row, blocks=DC):
    return jnp.concatenate([r.vecs[row + i:row + i + 1, :] for i in range(blocks)], axis=1)

def put(r, row, value):
    for i in range(value.shape[1] // LANE):
        r.vgrad[row + i:row + i + 1, :] = value[:, i * LANE:(i + 1) * LANE]

def add_to(r, row, value):
    for i in range(value.shape[1] // LANE):
        r.vgrad[row + i:row + i + 1, :] += value[:, i * LANE:(i + 1) * LANE]

def normal(v):
    mean = jnp.mean(v, axis=-1, keepdims=True)
    cen = v - mean
    var = jnp.mean(cen * cen, axis=-1, keepdims=True)
    s = lax.rsqrt(var + EPS)
    return cen * s, s

def normal_back(dn, nrm, s):
    return s * (dn - jnp.mean(dn, axis=-1, keepdims=True) - nrm * jnp.mean(dn * nrm, axis=-1, keepdims=True))

def colsum(v): return jnp.sum(v, axis=0, keepdims=True)

def gelu_both(h):
    cdf = 0.5 + 0.5 * lax.erf(h * (0.5 ** 0.5))
    pdf = jnp.exp(-0.5 * h * h) * (1.0 / math.sqrt(2 * math.pi))
    return h * cdf, cdf + h * pdf

RB = 64
def forward_norm(r):
    g1, s1 = vec(r, VG1), vec(r, VS1)
    def f(i):
        nrm, _ = normal(r.x[at(i, RB), :].astype(F32))
        r.a[at(i, RB), :] = (nrm * g1 + s1).astype(BF16)
    loop(r.rows // RB, f, 2)

def forward_qkv(r, lo=0, hi=9):
    bias = jnp.concatenate([vec(r, VBQ), jnp.zeros((1, D), F32), vec(r, VBV)], axis=1)
    for i in range(18):
        r.bias[i:i + 1, :] = bias[:, i * LANE:(i + 1) * LANE]
    def f(i):
        b = jnp.concatenate([r.bias[pl.ds(2 * i, 1), :], r.bias[pl.ds(2 * i + 1, 1), :]], axis=1)
        r.P[:, at(i, 256)] = (nn(r.a[...], r.wqkv[:, at(i, 256)]) + b).astype(BF16)
    span(lo, hi, 9, f, 3)

def halves(v):
    lo = lax.broadcasted_iota(jnp.int32, v.shape, 1) < 64
    w = v.astype(F32)
    z = jnp.zeros_like(w)
    return jnp.concatenate([jnp.where(lo, w, z), jnp.where(lo, z, w)], axis=0).astype(BF16)

def pick(v):
    lo = lax.broadcasted_iota(jnp.int32, (WINDOW, LANE), 1) < 64
    return jnp.where(lo, v[:WINDOW], v[WINDOW:])

def heads_of(r, i):
    w = i // DC
    hp = lax.rem(i, DC)
    rows = at(w, WINDOW)
    return w, rows, at(hp, LANE), at(hp + DC, LANE), at(hp + 2 * DC, LANE)

def same_segment(r):
    per = r.seg.shape[1] // WINDOW
    for w in range(r.rows // WINDOW):
        ids = r.seg[w // per:w // per + 1, w % per * WINDOW:(w % per + 1) * WINDOW].astype(F32)
        wide = jnp.broadcast_to(ids, (WINDOW, WINDOW))
        r.same[w] = (wide == wide.T).astype(F32)

def forward_attention(r, lo=0, hi=24):
    def f(i):
        w, rows, cq, ck, cv = heads_of(r, i)
        q2 = halves(r.P[rows, cq])
        s = nt(q2, r.P[rows, ck]) * 0.125
        same = r.same[w]
        same2 = jnp.concatenate([same, same], axis=0) > 0.5
        s = jnp.where(same2, s, -1e30)
        e = jnp.exp(s - jnp.max(s, axis=-1, keepdims=True))
        p = (e / jnp.sum(e, axis=-1, keepdims=True)).astype(BF16)
        r.p[i] = p
        r.ctx[rows, cq] = pick(nn(p, r.P[rows, cv])).astype(BF16)
    span(lo, hi, 24, f, 4)

def forward_out(r):
    bo = vec(r, VBO)
    for i in range(3):
        c = slice(i * 256, (i + 1) * 256)
        r.y1[:, c] = r.x[:, c].astype(F32) + nn(r.ctx[...], r.wo[:, c]) + bo[:, c]
    g2, s2 = vec(r, VG2), vec(r, VS2)
    def f(i):
        nrm, _ = normal(r.y1[at(i, RB), :])
        r.c[at(i, RB), :] = (nrm * g2 + s2).astype(BF16)
    loop(r.rows // RB, f, 2)

def forward_up(r, lo=0, hi=12):
    def f(i):
        b = jnp.concatenate([r.vecs[pl.ds(VB1 + 2 * i, 1), :], r.vecs[pl.ds(VB1 + 2 * i + 1, 1), :]], axis=1)
        h = nn(r.c[...], r.w1[:, at(i, 256)]) + b
        hid, slope = gelu_both(h)
        r.hid[:, at(i, 256)] = hid.astype(BF16)
        r.slope[:, at(i, 256)] = slope.astype(BF16)
    span(lo, hi, 12, f, 2)

def forward_down(r):
    b2 = vec(r, VB2)
    for i in range(3):
        c = slice(i * 256, (i + 1) * 256)
        v = r.y1[:, c] + nn(r.hid[...], r.w2[:, c]) + b2[:, c]
        r.ys[2 * i] = v[:, :LANE]
        r.ys[2 * i + 1] = v[:, LANE:]
    for j in range(RATE):
        for c in range(DC):
            r.u[j * r.mols:(j + 1) * r.mols, c * LANE:(c + 1) * LANE] = r.ys[c, pl.ds(j, r.mols, stride=RATE), :].astype(BF16)

def forward_conv(r):
    z = vec(r, VBC)
    for j in range(RATE):
        z = z + nn(r.u[j * r.mols:(j + 1) * r.mols, :], r.wc[j * D:(j + 1) * D, :])
    w, slope = gelu_both(z)
    nrm, s = normal(w)
    r.mol[...] = (nrm * vec(r, VG3) + vec(r, VS3)).astype(BF16)
    t = r.cot[...].astype(F32)
    put(r, VG3, colsum(t * nrm))
    put(r, VS3, colsum(t))
    dw = normal_back(t * vec(r, VG3), nrm, s)
    dz = (dw * slope).astype(BF16)
    r.dz[...] = dz
    put(r, VBC, colsum(dz.astype(F32)))

def emit_flat(r, dst, row0, tile, base=0):
    k, m = tile.shape[0], tile.shape[1] // LANE
    for c in range(m):
        r.scr[pl.ds(base + c, k, stride=m), :] = tile[:, c * LANE:(c + 1) * LANE]
    dst[pl.ds(pl.multiple_of(row0, 16), k * m), :] = r.scr[base:base + k * m, :].astype(BF16)

def emit_pair(r, dst, row0, lhs, rhs):
    tiles = [tn(lhs(h), rhs) for h in (0, 1)]
    for h in (0, 1): emit_flat(r, dst, row0 + h * 256 * DC, tiles[h], h * 256 * DC)

def grad_conv_weight(r, j):
    for i in range(3):
        emit_flat(r, r.gc, (j * D + i * 256) * DC, tn(r.u[j * r.mols:(j + 1) * r.mols, i * 256:(i + 1) * 256], r.dz[...]), i % 2 * 256 * DC)

def back_conv(r):
    for j in range(RATE):
        v = nt(r.dz[...], r.wc[j * D:(j + 1) * D, :])
        for c in range(DC):
            r.ys[c, pl.ds(j, r.mols, stride=RATE), :] = v[:, c * LANE:(c + 1) * LANE]
    for c in range(DC):
        v = r.ys[c]
        r.u[:, c * LANE:(c + 1) * LANE] = v.astype(BF16)
        put(r, VB2 + c, colsum(v))

def grad_down_weight(r, lo=0, hi=12):
    span(lo // 2, hi // 2, 6, lambda i: emit_pair(r, r.gl, W2_ROW + i * 512 * DC, lambda h: r.hid[:, pl.ds(pl.multiple_of(i * 512 + h * 256, 256), 256)], r.u[...]))

def back_down(r, lo=0, hi=12):
    def f(i):
        cols = [at(2 * i + h, 256) for h in (0, 1)]
        slopes = [r.slope[:, c] for c in cols]
        outs = [(nt(r.u[...], r.w2[c, :]) * s.astype(F32)).astype(BF16) for c, s in zip(cols, slopes)]
        for h, (c, dh) in enumerate(zip(cols, outs)):
            r.slope[:, c] = dh
            s = colsum(dh.astype(F32))
            r.vgrad[pl.ds(VB1 + 4 * i + 2 * h, 1), :] = s[:, :LANE]
            r.vgrad[pl.ds(VB1 + 4 * i + 2 * h + 1, 1), :] = s[:, LANE:]
    span(lo // 2, hi // 2, 6, f)

def grad_up_weight(r, lo=0, hi=6):
    span(lo, hi, 6, lambda i: emit_flat(r, r.gl, W1_ROW + i * 128 * FC, tn(r.c[:, at(i, 128)], r.slope[...])))

def fold(v):
    out = v[0:8]
    for i in range(1, v.shape[0] // 8):
        out = out + v[i * 8:(i + 1) * 8]
    return out

def row_sums(r, fn, count):
    def body(i, acc):
        return tuple(a + fold(v) for a, v in zip(acc, fn(at(i, RB))))
    acc = lax.fori_loop(0, r.rows // RB, body, tuple(jnp.zeros((8, D), F32) for _ in range(count)), unroll=2)
    return [colsum(a) for a in acc]

def back_up(r):
    for i in range(3):
        r.dc[:, i * 256:(i + 1) * 256] = nt(r.slope[...], r.w1[i * 256:(i + 1) * 256, :])
    g2 = vec(r, VG2)
    def f(rows):
        dc = r.dc[rows, :]
        nrm, s = normal(r.y1[rows, :])
        dy2 = jnp.concatenate([r.ys[c, rows, :] for c in range(DC)], axis=1)
        dy1 = dy2 + normal_back(dc * g2, nrm, s)
        r.dc[rows, :] = dy1
        r.u[rows, :] = dy1.astype(BF16)
        return dc * nrm, dc, dy1
    sums = row_sums(r, f, 3)
    put(r, VG2, sums[0])
    put(r, VS2, sums[1])
    put(r, VBO, sums[2])

def grad_out_weight(r):
    for i in range(3):
        emit_flat(r, r.gl, O_ROW + i * 256 * DC, tn(r.ctx[:, i * 256:(i + 1) * 256], r.u[...]), i % 2 * 256 * DC)

def back_out(r):
    for i in range(3):
        r.c[:, i * 256:(i + 1) * 256] = nt(r.u[...], r.wo[i * 256:(i + 1) * 256, :]).astype(BF16)

AG = 6
def back_attention(r, lo=0, hi=None):
    def f(i):
        where = [heads_of(r, i * AG + j) for j in range(AG)]
        loads = [(r.c[rows, cq], r.P[rows, cq], r.P[rows, ck], r.P[rows, cv], r.p[i * AG + j]) for j, (w, rows, cq, ck, cv) in enumerate(where)]
        outs = []
        for do, q, k, v, pb in loads:
            do2, q2 = halves(do), halves(q)
            p = pb.astype(F32)
            dp = nt(do2, v)
            ds = (p * (dp - jnp.sum(p * dp, axis=-1, keepdims=True))).astype(BF16)
            outs.append((pick(nn(ds, k)) * 0.125, tn(ds, q2) * 0.125, tn(pb, do2)))
        for (w, rows, cq, ck, cv), (dq, dk, dv) in zip(where, outs):
            r.P[rows, cq] = dq.astype(BF16)
            r.P[rows, ck] = dk.astype(BF16)
            r.P[rows, cv] = dv.astype(BF16)
    span(lo, hi, r.rows // WINDOW * DC // AG, f)

def grad_qkv_weight(r):
    for c in range(DC):
        r.vgrad[VBQ + c:VBQ + c + 1, :] = colsum(r.P[:, c * LANE:(c + 1) * LANE].astype(F32))
        r.vgrad[VBV + c:VBV + c + 1, :] = colsum(r.P[:, 2 * D + c * LANE:2 * D + (c + 1) * LANE].astype(F32))
    loop(6, lambda i: emit_flat(r, r.gl, QKV_ROW + i * 128 * 18, tn(r.a[:, at(i, 128)], r.P[...])))

def back_qkv(r):
    for i in range(3):
        r.y1[:, i * 256:(i + 1) * 256] = nt(r.P[...], r.wqkv[i * 256:(i + 1) * 256, :])
    g1 = vec(r, VG1)
    def f(rows):
        da = r.y1[rows, :]
        nrm, s = normal(r.x[rows, :].astype(F32))
        r.dc[rows, :] = r.dc[rows, :] + normal_back(da * g1, nrm, s)
        return da * nrm, da
    sums = row_sums(r, f, 2)
    put(r, VG1, sums[0])
    put(r, VS1, sums[1])

def state_shapes(rows):
    mols = rows // RATE
    V = pltpu.VMEM
    return dict(
        same=V((rows // WINDOW, WINDOW, WINDOW), F32), a=V((rows, D), BF16), P=V((rows, 3 * D), BF16), p=V((rows // WINDOW * DC, 2 * WINDOW, LANE), BF16),
        ctx=V((rows, D), BF16), y1=V((rows, D), F32), c=V((rows, D), BF16), slope=V((rows, FF), BF16), hid=V((rows, FF), BF16),
        ys=V((DC, rows, LANE), F32), u=V((rows, D), BF16), dz=V((mols, D), BF16), dc=V((rows, D), F32),
        scr=V((128 * FC, LANE), F32), bias=V((24, LANE), F32), vecs=V((96, LANE), F32))


class Geo:
    def __init__(self, n, local_shard, conv_shard):
        self.n = n
        self.local_shard, self.conv_shard = local_shard, conv_shard
        self.Z = n // 8
        self.RL = (12 * D * D) // LANE // n
        self.RC = (4 * D * D) // LANE // n
        self.dl = local_shard - self.RL * LANE
        self.dc = conv_shard - self.RC * LANE
        self.HL = -(-(self.dl * n) // (8 * LANE)) * 8
        self.HC = -(-(self.dc * n) // (8 * LANE)) * 8
        self.XL = -(-local_shard // (8 * LANE)) * 8
        self.XC = -(-conv_shard // (8 * LANE)) * 8

def where_am_i():
    me = lax.axis_index("fsdp")
    core = lax.rem(me, 2)
    bx = lax.rem(me // 2, 2)
    by = lax.rem(me // 4, 2)
    z = me // 8
    sib = me + 1 - 2 * core
    xn = me + 2 - 4 * bx
    yn = me + 4 - 8 * by
    first = xn + core * (yn - xn)
    second = yn + core * (xn - yn)
    return me, core, z, sib, first, second

def realign(out_ref, out_base, lo, hi, x_ref, shift, step=16):
    q = shift // LANE
    r = lax.rem(shift, LANE)
    turn = lax.rem(LANE - r, LANE)
    lane = lax.broadcasted_iota(jnp.int32, (step, LANE), 1)
    keep = lane < (LANE - r)
    def body(i, _):
        low = x_ref[pl.ds(q + i * step, step), :]
        high = x_ref[pl.ds(q + i * step + 1, step), :]
        val = jnp.where(keep, pltpu.roll(low, turn, 1), pltpu.roll(high, turn, 1))
        out_ref[pl.ds(pl.multiple_of(out_base + i * step, step), step), :] = val.astype(out_ref.dtype)
        return 0
    many = max(u for u in (1, 2, 3, 4, 5, 6, 8) if (hi - lo) // step % u == 0)
    lax.fori_loop(lo // step, hi // step, body, 0, unroll=many)

def widen(dst_ref, dst_base, src_ref, rows):
    step = 248 if rows % 248 == 0 else 8
    for i in range(rows // step):
        dst_ref[dst_base + i * step:dst_base + (i + 1) * step, :] = src_ref[i * step:(i + 1) * step, :].astype(F32)

def convert_unit(src_ref, base, w_ref, krow, cols, scr):
    groups = UNIT // (16 * cols)
    def body(g, _):
        scr[0:16 * cols, :] = src_ref[pl.ds(pl.multiple_of(base + g * 16 * cols, 16), 16 * cols), :].astype(F32)
        for cc in range(cols):
            v = scr[pl.ds(cc, 16, stride=cols), :]
            w_ref[pl.ds(pl.multiple_of(krow + g * 16, 16), 16), cc * LANE:(cc + 1) * LANE] = v.astype(BF16)
        return 0
    lax.fori_loop(0, groups, body, 0)


def start_gather(g):
    n, Z, geo, me, z = g.n, g.Z, g.geo, g.me, g.z
    RL, RC = geo.RL, geo.RC
    nxt = lax.rem(me + 1, n)
    bar = pltpu.get_barrier_semaphore()
    far = lax.rem(me + n + 2 * g.core - 1, n)
    for dev in (g.sib, g.first, g.second, far):
        pl.semaphore_signal(bar, inc=1, device_id=(dev,), device_id_type=MESH)
    @pl.when(z > 0)
    def _(): pl.semaphore_signal(bar, inc=1, device_id=(me - 8,), device_id_type=MESH)
    @pl.when(z < Z - 1)
    def _(): pl.semaphore_signal(bar, inc=1, device_id=(me + 8,), device_id_type=MESH)
    widen(g.xlf, geo.HL, g.xl, geo.XL)
    widen(g.xcf, geo.HC, g.xc, geo.XC)
    realign(g.fs, 0, 0, geo.HL, g.xlf, geo.local_shard, 8)
    realign(g.fs, geo.HL, 0, geo.HC, g.xcf, geo.conv_shard, 8)
    g.hb[...] = g.fs[...].astype(BF16)
    HA, HB = 96, 96
    lshift, cshift = geo.HL * LANE - geo.dl * me, geo.HC * LANE - geo.dc * me
    realign(g.gl, me * RL, HA, RL, g.xlf, lshift)
    realign(g.gc, me * RC, HB, RC, g.xcf, cshift)
    pl.semaphore_wait(bar, 4 + jnp.where(z > 0, 1, 0) + jnp.where(z < Z - 1, 1, 0))
    halo = pltpu.make_async_remote_copy(src_ref=g.hb, dst_ref=g.hr, send_sem=g.hsem.at[0], recv_sem=g.hsem.at[1], device_id=(nxt,), device_id_type=MESH)
    halo.start()
    halo.wait()
    g.xlf[0:geo.HL, :] = g.hr[0:geo.HL, :].astype(F32)
    g.xcf[0:geo.HC, :] = g.hr[geo.HL:geo.HL + geo.HC, :].astype(F32)
    realign(g.gl, me * RL, 0, HA, g.xlf, lshift)
    realign(g.gc, me * RC, 0, HB, g.xcf, cshift)
    @pl.when(me == n - 1)
    def _():
        g.tail[...] = g.hb[...]


def gather_table(g):
    Z, me, z = g.Z, g.me, g.z
    bx, by = lax.rem(me // 2, 2), lax.rem(me // 4, 2)
    one = g.core == 1
    def copy(slot, dev):
        return pltpu.make_async_remote_copy(src_ref=g.tail, dst_ref=g.tail, send_sem=g.tsem.at[slot], recv_sem=g.tsem.at[4], device_id=(dev,), device_id_type=MESH)
    right = jnp.logical_and(one, bx == 1)
    corner = jnp.logical_and(right, by == 1)
    sends = ((0, me - 8, jnp.logical_and(corner, z > 0)), (1, g.first, corner), (2, g.second, right), (3, g.sib, one))
    @pl.when(me != g.n - 1)
    def _(): copy(0, g.sib).wait_recv()
    for slot, dev, there in sends:
        @pl.when(there)
        def _(): copy(slot, dev).start()
    g.vecs[...] = g.tail[...].astype(F32)
    def finish():
        for slot, dev, there in sends:
            @pl.when(there)
            def _(): copy(slot, dev).wait_send()
    return finish


class Gather:
    def __init__(self, g, parts):
        self.g = g
        self.parts = parts
        self.size = (g.geo.RL, g.geo.RC)
        self.place = (g.gl, g.gc)

    def source(self, dz, f, s):
        g = self.g
        return g.me + 8 * dz + f * (g.first - g.me) + s * (g.second - g.me)

    def copy(self, k, p, src, dev, slot):
        g = self.g
        rows = self.size[k] // self.parts[k]
        i = p if k == 0 else self.parts[0] + p
        ref = self.place[k].at[pl.ds(pl.multiple_of(src * self.size[k] + p * rows, 16), rows)]
        return pltpu.make_async_remote_copy(src_ref=ref, dst_ref=ref, send_sem=g.ssem.at[i, slot], recv_sem=g.rsem.at[i, src], device_id=(dev,), device_id_type=MESH)

    def sends(self, o, k, p, dz):
        g, z, Z = self.g, self.g.z, self.g.Z
        f, s = {1: (0, 0), 2: (1, 0), 3: (0, 1), 4: (1, 1)}[o]
        src, zi = self.source(dz, f, s), z + dz
        out = []
        if k == 1:
            if dz >= 0: out.append((lambda: self.copy(k, p, src, g.me - 8, (o - 1) * Z + zi), z > 0))
            if dz <= 0: out.append((lambda: self.copy(k, p, src, g.me + 8, (o + 3) * Z + zi), z < Z - 1))
            if dz == 0 and o == 1: out.append((lambda: self.copy(k, p, src, g.first, 8 * Z), None))
            if dz == 0 and o <= 2: out.append((lambda: self.copy(k, p, src, g.second, 8 * Z + o), None))
            out.append((lambda: self.copy(k, p, src, g.sib, (8 + o) * Z + zi), None))
            return src, out
        if o == 1:
            if dz >= 0: out.append((lambda: self.copy(k, p, src, g.me - 8, zi), z > 0))
            if dz <= 0: out.append((lambda: self.copy(k, p, src, g.me + 8, Z + zi), z < Z - 1))
            out.append((lambda: self.copy(k, p, src, g.first, 2 * Z + zi), None))
        if o <= 2: out.append((lambda: self.copy(k, p, src, g.second, (2 + o) * Z + zi), None))
        out.append((lambda: self.copy(k, p, src, g.sib, (4 + o) * Z + zi), None))
        return src, out

    def guard(self, cond, fn):
        if cond is None: fn()
        else: pl.when(cond)(fn)

    def valid(self, dz, fn):
        z, Z = self.g.z, self.g.Z
        self.guard(None if dz == 0 else jnp.logical_and(z + dz >= 0, z + dz < Z), fn)

    def event(self, o, k, p, dz):
        def fn():
            src, sends = self.sends(o, k, p, dz)
            if o > 1 or dz != 0: self.copy(k, p, src, self.g.sib, 0).wait_recv()
            for cp, there in sends: self.guard(there, lambda cp=cp: cp().start())
        self.valid(dz, fn)

    def drain(self, o, k, p, dz):
        def fn():
            for cp, there in self.sends(o, k, p, dz)[1]: self.guard(there, lambda cp=cp: cp().wait_send())
        self.valid(dz, fn)

    def convert(self, k, dz):
        g = self.g
        per = 2 * self.size[k] // UNIT
        def fn():
            def chip_body(c, _):
                src = self.source(dz, c // 2, lax.rem(c, 2))
                for p in range(self.parts[k]): self.copy(k, p, src + g.sib - g.me, g.sib, 0).wait_recv()
                def unit(i, _):
                    t = (src // 2) * per + i
                    base = t * UNIT
                    if k == 1: convert_unit(g.gc, base, g.wc, t * 192, 6, g.scr)
                    else:
                        @pl.when(t < 12)
                        def _(): convert_unit(g.gl, base, g.wqkv, t * 64, 18, g.scr)
                        @pl.when(jnp.logical_and(t >= 12, t < 16))
                        def _(): convert_unit(g.gl, base, g.wo, (t - 12) * 192, 6, g.scr)
                        @pl.when(jnp.logical_and(t >= 16, t < 32))
                        def _(): convert_unit(g.gl, base, g.w1, (t - 16) * 48, 24, g.scr)
                        @pl.when(t >= 32)
                        def _(): convert_unit(g.gl, base, g.w2, (t - 32) * 192, 6, g.scr)
                    return 0
                lax.fori_loop(0, per, unit, 0)
                return 0
            lax.fori_loop(0, 4, chip_body, 0)
        self.valid(dz, fn)


PART = 576
RING = 4


class Scatter:
    def __init__(self, g, jobs):
        self.g = g
        self.size = (g.geo.RL, g.geo.RC)
        self.own = (g.gl, g.gc)
        self.jobs = jobs
        self.started, self.granted, self.waiting = set(), set(), []
        self.opened = self.closed = 0

    def target(self, zt, f, s):
        g = self.g
        return g.me + 8 * (zt - g.z) + f * (g.first - g.me) + s * (g.second - g.me)

    def other(self, zt, f, s): return self.target(zt, f, s) + self.g.sib - self.g.me

    def rows(self, k, t, p):
        return pl.ds(pl.multiple_of(t * self.size[k] + p * PART, 16), PART)

    def sem(self, k, p):
        return p if k == 0 else self.size[0] // PART + p

    def move(self, src, dst, send, recv, i, index, dev):
        return pltpu.make_async_remote_copy(src_ref=src, dst_ref=dst, send_sem=send.at[i, index], recv_sem=recv.at[i, index], device_id=(dev,), device_id_type=MESH)

    def at(self, k, p, t): return self.own[k].at[self.rows(k, t, p)]

    def to_sib(self, k, p, t):
        g = self.g
        return self.move(self.at(k, p, t), g.from_sib[k].at[self.rows(k, t // 2, p)], g.s_sib, g.r_sib, self.sem(k, p), t // 2, g.sib)

    def to_second(self, k, p, zt, f):
        g = self.g
        t = self.target(zt, f, 1)
        return self.move(self.at(k, p, t), self.at(k, p, t + g.sib - g.me), g.s_second, g.r_second, self.sem(k, p), 2 * zt + f, g.second)

    def to_first(self, k, p, zt):
        g = self.g
        t = self.target(zt, 1, 0)
        return self.move(self.at(k, p, t), self.at(k, p, t + g.second - g.me + g.sib - g.me), g.s_first, g.r_first, self.sem(k, p), zt, g.first)

    def down(self, k, p, zt):
        g = self.g
        return self.move(self.at(k, p, self.target(zt, 0, 0)), self.at(k, p, self.other(zt, 1, 1)), g.s_down, g.r_down, self.sem(k, p), zt, g.me - 8)

    def up(self, k, p, zt, land):
        g = self.g
        dst = (g.below_l, g.below_c)[k].at[pl.ds(p * PART, PART)] if land else self.at(k, p, self.other(zt, 1, 1))
        return self.move(self.at(k, p, self.target(zt, 0, 0)), dst, g.s_up, g.r_up, self.sem(k, p), zt, g.me + 8)

    def p0(self, k, p, zt):
        for f in (0, 1):
            for s in (0, 1):
                self.to_sib(k, p, self.other(zt, f, s)).start()
        self.started.add((k, p, zt))
        self.waiting.append((k, p, zt))

    def ticket(self, which, k, p, zt): return self.g.credit.at[which, self.sem(k, p) * self.g.Z + zt]

    def credit(self, which, k, p, zt, dev):
        pl.semaphore_signal(self.ticket(which, k, p, zt), inc=1, device_id=(dev,), device_id_type=MESH)

    def grant(self, k, p, zt):
        g = self.g
        z, Z, me = g.z, g.Z, g.me
        for f in (0, 1):
            for s in (0, 1):
                self.to_sib(k, p, self.other(zt, f, s)).wait_send()
        self.credit(0, k, p, zt, g.second)
        self.credit(1, k, p, zt, g.second)
        self.credit(2, k, p, zt, g.first)
        if zt < Z - 1:
            @pl.when(jnp.logical_and(z >= zt, z < Z - 1))
            def _(): self.credit(3, k, p, zt, me + 8)
        if zt > 1:
            @pl.when(jnp.logical_and(z < zt, z > 0))
            def _(): self.credit(4, k, p, zt, me - 8)
        self.granted.add((k, p, zt))

    def grant_all(self):
        for st in self.waiting: self.grant(*st)
        self.waiting = []

    def spend(self, which, k, p, zt): pl.semaphore_wait(self.ticket(which, k, p, zt), 1)

    def place(self, job):
        kind, (k, p, zt), x = job
        z, Z = self.g.z, self.g.Z
        if kind == "second": return None, self.target(zt, x, 1)
        if kind == "first": return None, self.target(zt, 1, 0)
        if kind == "last": return z == zt, self.target(zt, 0, 0)
        return z == (x[0] if x[1] else Z - 1 - x[0]), self.target(zt, 0, 0)

    def describe(self, job):
        kind, (k, p, zt), x = job
        g = self.g
        z, Z, me = g.z, g.Z, g.me
        if kind == "second":
            def send():
                self.spend(x, k, p, zt)
                self.to_second(k, p, zt, x).start()
            return [], [], None, send
        if kind == "first":
            def send():
                self.spend(2, k, p, zt)
                self.to_first(k, p, zt).start()
            return [self.to_second(k, p, zt, 1)], [self.at(k, p, self.other(zt, 1, 0))], None, send
        waits = [self.to_second(k, p, zt, 0), self.to_first(k, p, zt)]
        lands = [self.at(k, p, self.other(zt, 0, 0)), self.at(k, p, self.other(zt, 0, 1))]
        far = self.at(k, p, self.other(zt, 1, 1))
        if kind == "last":
            if zt < Z - 1:
                waits.append(self.down(k, p, zt))
                lands.append(far)
            if zt > 0:
                waits.append(self.up(k, p, zt, True))
                lands.append((g.below_l, g.below_c)[k].at[pl.ds(p * PART, PART)])
            return waits, lands, (g.xlf, g.xcf)[k], None
        hop, upward = x
        if hop > 0:
            waits.append(self.up(k, p, zt, False) if upward else self.down(k, p, zt))
            lands.append(far)
        here = hop if upward else Z - 1 - hop
        def send():
            if upward:
                if here + 1 < zt: self.spend(4, k, p, zt)
                self.up(k, p, zt, here + 1 == zt).start()
            else:
                self.spend(3, k, p, zt)
                self.down(k, p, zt).start()
        return waits, lands, None, send

    def guard(self, cond, fn):
        if cond is None: fn()
        else: pl.when(cond)(fn)

    def fetch(self, job, t, slot):
        g, (k, p, zt) = self.g, job[1]
        return pltpu.make_async_copy(g.from_sib[k].at[self.rows(k, t // 2, p)], g.tmp.at[slot], g.fsem.at[slot])

    def open(self, i):
        job = self.jobs[i]
        cond, t = self.place(job)
        def fn():
            self.to_sib(*job[1][:2], t).wait_recv()
            self.fetch(job, t, i % RING).start()
        self.guard(cond, fn)

    def close(self, i):
        g, job, slot = self.g, self.jobs[i], i % RING
        k, p, zt = job[1]
        cond, t = self.place(job)
        def fn():
            waits, lands, out, send = self.describe(job)
            for cp in waits: cp.wait_recv()
            self.fetch(job, t, slot).wait()
            mine = self.at(k, p, t)
            def body(b, _):
                r = pl.ds(pl.multiple_of(b * 16, 16), 16)
                acc = mine[r, :].astype(F32) + g.tmp[slot, r, :].astype(F32)
                for land in lands: acc = acc + land[r, :].astype(F32)
                if out is None: mine[r, :] = acc.astype(BF16)
                else: out[pl.ds(pl.multiple_of(p * PART + b * 16, 16), 16), :] = acc
                return 0
            lax.fori_loop(0, PART // 16, body, 0, unroll=4)
            if send is not None: send()
        self.guard(cond, fn)

    def run(self):
        i = self.closed
        step = self.jobs[i][1]
        if step not in self.granted: self.grant_all()
        while self.opened < len(self.jobs) and self.opened < i + RING and self.jobs[self.opened][1] in self.started:
            self.open(self.opened)
            self.opened += 1
        self.close(i)
        self.closed += 1

    def finish(self, k, p, zt):
        g = self.g
        for f in (0, 1): self.to_second(k, p, zt, f).wait_send()
        self.to_first(k, p, zt).wait_send()
        @pl.when(g.z > zt)
        def _(): self.down(k, p, zt).wait_send()
        @pl.when(g.z < zt)
        def _(): self.up(k, p, zt, False).wait_send()


def reduce_vectors(g):
    Z, me, z = g.Z, g.me, g.z
    core = lax.rem(me, 2)
    bx, by = lax.rem(me // 2, 2), lax.rem(me // 4, 2)
    def cp(slot, dev):
        return pltpu.make_async_remote_copy(src_ref=g.vgrad, dst_ref=g.vland.at[slot], send_sem=g.vsem.at[0], recv_sem=g.vsem.at[1 + slot], device_id=(dev,), device_id_type=MESH)
    def take(slot):
        cp(slot, g.sib).wait_recv()
        g.vgrad[...] = g.vgrad[...] + g.vland[slot]
    def give(slot, dev):
        c = cp(slot, dev)
        c.start()
        c.wait_send()
    on = core == 1
    def stage0():
        @pl.when(jnp.logical_not(on))
        def _(): give(0, g.sib)
        @pl.when(on)
        def _(): take(0)
    def stage1():
        @pl.when(jnp.logical_and(on, bx == 0))
        def _(): give(1, g.second)
        @pl.when(jnp.logical_and(on, bx == 1))
        def _(): take(1)
    def stage2():
        @pl.when(jnp.logical_and(on, jnp.logical_and(bx == 1, by == 0)))
        def _(): give(2, g.first)
        @pl.when(jnp.logical_and(on, jnp.logical_and(bx == 1, by == 1)))
        def _(): take(2)
    def stage3():
        @pl.when(jnp.logical_and(on, jnp.logical_and(bx == 1, by == 1)))
        def _():
            @pl.when(z > 0)
            def _(): take(3)
            @pl.when(z < Z - 1)
            def _(): give(3, me + 8)
    return stage0, stage1, stage2, stage3


def place_gradients(g):
    n, geo, me = g.n, g.geo, g.me
    prv = lax.rem(me + n - 1, n)
    edge = me == n - 1
    HL, HC = geo.HL, geo.HC
    skip = VBC - HL
    vectors = ((0, HL, HL), (VBC, HL + HC, HC - skip))
    def part(k):
        x, out, rows, drift = ((g.xlf, g.outl, geo.RL, geo.dl), (g.xcf, g.outc, geo.RC, geo.dc))[k]
        first, last = (0, HL) if k == 0 else (HL, HL + HC)
        cp = pltpu.make_async_remote_copy(src_ref=g.fs.at[pl.ds(first, last - first)], dst_ref=g.fr.at[pl.ds(first, last - first)],
                                          send_sem=g.hsem.at[2 + 2 * k], recv_sem=g.hsem.at[3 + 2 * k], device_id=(prv,), device_id_type=MESH)
        def begin():
            g.fs[first:last, :] = x[0:last - first, :]
            cp.start()
        split = (rows - 96) // 96 * 96
        def middle(): realign(out, 0, 0, split, x, drift * me)
        def end():
            cp.wait()
            lo, hi, count = vectors[k]
            x[rows:rows + count, :] = jnp.where(edge, g.vgrad[lo:hi, :], g.fr[first:first + count, :])
            realign(out, 0, split, out.shape[0], x, drift * me)
        return begin, middle, end
    return part(0), part(1)


PLANES = 4
LAYER_PARTS = 1
GATHER = (
    (1, 1, 0, 0), (1, 0, 0, 0), (1, 0, 0, -1), (3, 0, 0, 0), (2, 1, 0, 0), (2, 0, 0, 0), (1, 0, 0, 1), (4, 1, 0, 0), (1, 0, 0, 2), (3, 1, 0, 0),
    (1, 0, 0, -2), (2, 0, 0, -1), (3, 1, 0, 1), (4, 0, 0, 0), (2, 0, 0, 1), (4, 1, 0, -1), (3, 1, 0, -1), (1, 0, 0, 3), (4, 1, 0, 1), (2, 1, 0, 1),
    (3, 0, 0, -1), (1, 0, 0, -3), (1, 1, 0, 1), (5, 0, 0), (2, 1, 0, -1), (0, 0), (3, 0, 0, 1), (1, 1, 0, -1), (3, 0, 0, 2), (5, 1, 0), (2, 0, 0, -2),
    (4, 0, 0, -1), (5, 1, 1), (2, 0, 0, 2), (3, 1, 0, 2), (5, 1, -1), (3, 0, 0, -2), (2, 0, 0, -3), (3, 0, 0, -3), (3, 1, 0, -2), (4, 1, 0, -2),
    (4, 0, 0, 1), (2, 1, 0, 2), (1, 1, 0, 2), (4, 1, 0, 2), (5, 0, -1), (2, 0, 0, 3), (4, 0, 0, -2), (1, 1, 0, -2), (2, 1, 0, -2), (4, 0, 0, -3),
    (5, 0, 1), (5, 0, -2), (5, 0, -3), (0, 1), (0, 2), (0, 3), (4, 0, 0, 2), (5, 1, -2), (5, 1, 2), (0, 4), (2, 1, 0, -3), (3, 0, 0, 3), (4, 0, 0, 3),
    (0, 5), (5, 0, 2), (1, 1, 0, 3), (0, 6), (3, 1, 0, 3), (4, 1, 0, 3), (0, 7), (2, 1, 0, 3), (1, 1, 0, -3), (4, 1, 0, -3), (3, 1, 0, -3), (0, 8),
    (5, 0, 3), (0, 9), (5, 1, -3), (5, 1, 3), (0, 10),
)
SCATTER = (
    (1, 1, 0, 3, 0), (1, 1, 0, 2, 1), (1, 1, 0, 3, 1), (1, 1, 0, 0, 1), (1, 1, 0, 1, 1), (0, 0), (0, 1), (1, 0, 1, 3, 1), (1, 0, 0, 3, 1),
    (1, 0, 1, 3, 0), (1, 1, 0, 2, 0), (0, 2), (1, 1, 0, 1, 0), (2, 1, 0, 2, 0), (2, 1, 0, 1, 0), (0, 3), (0, 4), (2, 0, 0, 3, 0), (1, 1, 0, 0, 0),
    (0, 5), (1, 0, 0, 2, 0), (1, 0, 0, 2, 1), (1, 0, 2, 2, 0), (2, 1, 0, 3, 0), (0, 6), (2, 1, 0, 0, 0), (1, 0, 2, 2, 1), (3, 1, 0, 2, (0, True)),
    (3, 1, 0, 1, (0, True)), (0, 7), (1, 0, 0, 3, 0), (1, 0, 2, 3, 1), (2, 0, 0, 2, 0), (1, 0, 2, 3, 0), (0, 8), (3, 1, 0, 3, (0, True)), (0, 9),
    (1, 0, 1, 2, 1), (0, 10), (3, 1, 0, 2, (0, False)), (2, 0, 2, 2, 0), (3, 1, 0, 2, (1, True)), (3, 0, 0, 3, (0, True)), (2, 0, 1, 3, 0),
    (1, 0, 1, 2, 0), (2, 0, 2, 3, 0), (0, 11), (3, 0, 0, 3, (1, True)), (3, 1, 0, 0, (0, False)), (2, 0, 1, 2, 0), (0, 12), (1, 0, 0, 0, 1),
    (3, 0, 0, 3, (2, True)), (3, 0, 2, 2, (0, False)), (3, 0, 2, 3, (0, True)), (1, 0, 0, 0, 0), (4, 1, 0, 2, 0), (1, 0, 1, 1, 1),
    (3, 1, 0, 3, (1, True)), (3, 1, 0, 1, (0, False)), (1, 0, 2, 0, 1), (3, 0, 1, 2, (0, False)), (3, 0, 0, 2, (0, False)), (3, 1, 0, 0, (1, False)),
    (2, 0, 0, 0, 0), (3, 0, 0, 2, (0, True)), (3, 0, 1, 3, (0, True)), (3, 0, 2, 3, (1, True)), (1, 0, 1, 0, 1), (3, 0, 2, 2, (0, True)),
    (1, 0, 2, 0, 0), (3, 0, 1, 2, (0, True)), (0, 13), (3, 0, 0, 2, (1, True)), (2, 0, 2, 0, 0), (1, 0, 1, 0, 0), (3, 0, 0, 0, (0, False)),
    (3, 0, 1, 3, (1, True)), (3, 1, 0, 3, (2, True)), (3, 1, 0, 0, (2, False)), (1, 0, 0, 1, 1), (1, 0, 0, 1, 0), (3, 0, 0, 0, (2, False)),
    (3, 0, 2, 0, (0, False)), (3, 0, 1, 2, (1, True)), (3, 1, 0, 1, (1, False)), (3, 0, 0, 0, (1, False)), (2, 0, 1, 0, 0), (0, 14),
    (3, 0, 2, 3, (2, True)), (2, 0, 0, 1, 0), (1, 0, 2, 1, 1), (3, 0, 1, 0, (0, False)), (3, 0, 2, 0, (2, False)), (1, 0, 1, 1, 0), (4, 1, 0, 1, 0),
    (3, 0, 2, 2, (1, True)), (3, 0, 2, 0, (1, False)), (3, 0, 1, 3, (2, True)), (3, 0, 1, 0, (1, False)), (3, 0, 1, 0, (2, False)), (2, 0, 1, 1, 0),
    (0, 15), (3, 0, 0, 1, (0, False)), (4, 0, 2, 3, 0), (2, 0, 2, 1, 0), (3, 0, 1, 1, (0, True)), (1, 0, 2, 1, 0), (3, 0, 1, 1, (0, False)),
    (3, 0, 0, 1, (1, False)), (4, 0, 0, 3, 0), (3, 0, 0, 1, (0, True)), (0, 16), (4, 0, 0, 2, 0), (4, 1, 0, 3, 0), (4, 0, 1, 1, 0),
    (3, 0, 2, 1, (0, True)), (3, 0, 1, 1, (1, False)), (4, 0, 0, 1, 0), (3, 0, 2, 1, (0, False)), (3, 0, 2, 1, (1, False)), (4, 0, 1, 2, 0),
    (4, 0, 1, 0, 0), (4, 0, 2, 1, 0), (4, 0, 0, 0, 0), (4, 1, 0, 0, 0), (4, 0, 2, 2, 0), (4, 0, 1, 3, 0), (4, 0, 2, 0, 0),
)


def local_layout():
    return ((D, 3 * D), (D, D), (D, FF), (FF, D), (FF,)) + ((D,),) * 8


def conv_layout():
    return ((RATE * D, D), (D,), (D,), (D,))


def unpack(packed, layout):
    offset = 0
    pieces = []
    for extent in layout:
        length = math.prod(extent)
        pieces.append(packed[offset : offset + length].reshape(extent))
        offset = offset + length
    return pieces


def normalize_parts(values):
    average = jnp.mean(values, axis=-1, keepdims=True)
    centred = values - average
    spread = jnp.mean(centred * centred, axis=-1, keepdims=True)
    scaling = lax.rsqrt(spread + EPSILON)
    return (centred * scaling, scaling)


def normal_back(grad_normed, normed, scaling):
    first_mean = jnp.mean(grad_normed, axis=-1, keepdims=True)
    second_mean = jnp.mean(grad_normed * normed, axis=-1, keepdims=True)
    return scaling * (grad_normed - first_mean - normed * second_mean)


def product(left, right):
    return jnp.dot(left, right, preferred_element_type=jnp.float32)


def rows_inner(left, right):
    return lax.dot_general(
        left, right, (((0,), (0,)), ((), ())), preferred_element_type=jnp.float32
    )


def times_transpose(left, right):
    return lax.dot_general(
        left, right, (((1,), (1,)), ((), ())), preferred_element_type=jnp.float32
    )


def gelu_exact(values):
    return jax.nn.gelu(values, approximate=False)


def gelu_grad(values, upstream):
    return jax.vjp(gelu_exact, values)[1](upstream)[0]


def window_scores(projected, segments_block):
    row_count = projected.shape[0]
    windows = row_count // WINDOW
    heads_view = projected.reshape(windows, WINDOW, 3, HEADS, HEAD_SIZE)
    queries = heads_view[:, :, 0]
    keys_all = heads_view[:, :, 1]
    values = heads_view[:, :, 2]
    scores = jnp.einsum(
        "bqhe,bkhe->bhqk", queries, keys_all, preferred_element_type=jnp.float32
    ) * HEAD_SIZE ** (-0.5)
    grouped = segments_block.reshape(windows, WINDOW)
    allowed = grouped[:, None, :, None] == grouped[:, None, None, :]
    return (jnp.where(allowed, scores, -1e30), queries, keys_all, values)


def forward_pass(characters_block, segments_block, local_weights, conv_weights):
    (
        qkv_weight,
        out_weight,
        in_weight,
        down_weight,
        in_bias,
        gain_one,
        shift_one,
        query_bias,
        value_bias,
        out_bias,
        gain_two,
        shift_two,
        down_bias,
    ) = local_weights
    conv_weight, conv_bias, gain_three, shift_three = conv_weights
    row_count = characters_block.shape[0]
    inputs = characters_block.astype(jnp.float32)
    norm_one, scale_one = normalize_parts(inputs)
    normed = (norm_one * gain_one + shift_one).astype(jnp.bfloat16)
    proj_bias = jnp.concatenate([query_bias, jnp.zeros_like(query_bias), value_bias])
    projected = (product(normed, qkv_weight) + proj_bias).astype(jnp.bfloat16)
    scores, queries, keys_all, values = window_scores(projected, segments_block)
    largest = jnp.max(scores, axis=-1, keepdims=True)
    raised = jnp.exp(scores - largest)
    totals = jnp.sum(raised, axis=-1, keepdims=True)
    log_totals = largest + jnp.log(totals)
    weights = (raised / totals).astype(jnp.bfloat16)
    attended = jnp.einsum("bhqk,bkhe->bqhe", weights, values, preferred_element_type=jnp.float32)
    context = attended.reshape(row_count, D).astype(jnp.bfloat16)
    after_attention = inputs + product(context, out_weight) + out_bias
    norm_two, scale_two = normalize_parts(after_attention)
    middle = (norm_two * gain_two + shift_two).astype(jnp.bfloat16)
    pre_act = product(middle, in_weight) + in_bias
    hidden = gelu_exact(pre_act).astype(jnp.bfloat16)
    after_feed = after_attention + product(hidden, down_weight) + down_bias
    grouped_rows = after_feed.astype(jnp.bfloat16).reshape(row_count // RATE, RATE * D)
    conv_pre = product(grouped_rows, conv_weight) + conv_bias
    norm_three, scale_three = normalize_parts(gelu_exact(conv_pre))
    molecules = (norm_three * gain_three + shift_three).astype(jnp.bfloat16)
    saved_state = (
        segments_block,
        norm_one,
        scale_one,
        normed,
        projected,
        log_totals,
        context,
        norm_two,
        scale_two,
        middle,
        pre_act,
        hidden,
        grouped_rows,
        conv_pre,
        norm_three,
        scale_three,
    )
    return (molecules, saved_state)


def backward_pass(cotangent_block, saved_state, local_weights, conv_weights):
    (
        qkv_weight,
        out_weight,
        in_weight,
        down_weight,
        in_bias,
        gain_one,
        shift_one,
        query_bias,
        value_bias,
        out_bias,
        gain_two,
        shift_two,
        down_bias,
    ) = local_weights
    conv_weight, conv_bias, gain_three, shift_three = conv_weights
    (
        segments_block,
        norm_one,
        scale_one,
        normed,
        projected,
        log_totals,
        context,
        norm_two,
        scale_two,
        middle,
        pre_act,
        hidden,
        grouped_rows,
        conv_pre,
        norm_three,
        scale_three,
    ) = saved_state
    row_count = normed.shape[0]
    windows = row_count // WINDOW
    upstream = cotangent_block.astype(jnp.float32)
    grad_gain_three = jnp.sum(upstream * norm_three, axis=0)
    grad_shift_three = jnp.sum(upstream, axis=0)
    grad_activated = normal_back(upstream * gain_three, norm_three, scale_three)
    grad_conv_pre = gelu_grad(conv_pre, grad_activated).astype(jnp.bfloat16)
    grad_conv_bias = jnp.sum(grad_conv_pre.astype(jnp.float32), axis=0)
    grad_conv_weight = rows_inner(grouped_rows, grad_conv_pre)
    grad_feed = times_transpose(grad_conv_pre, conv_weight).reshape(row_count, D)
    grad_down_bias = jnp.sum(grad_feed, axis=0)
    grad_branch = grad_feed.astype(jnp.bfloat16)
    grad_down_weight = rows_inner(hidden, grad_branch)
    grad_hidden = times_transpose(grad_branch, down_weight)
    grad_pre = gelu_grad(pre_act, grad_hidden).astype(jnp.bfloat16)
    grad_in_bias = jnp.sum(grad_pre.astype(jnp.float32), axis=0)
    grad_in_weight = rows_inner(middle, grad_pre)
    grad_middle = times_transpose(grad_pre, in_weight)
    grad_gain_two = jnp.sum(grad_middle * norm_two, axis=0)
    grad_shift_two = jnp.sum(grad_middle, axis=0)
    grad_attention = grad_feed + normal_back(grad_middle * gain_two, norm_two, scale_two)
    grad_out_bias = jnp.sum(grad_attention, axis=0)
    grad_attn_out = grad_attention.astype(jnp.bfloat16)
    grad_out_weight = rows_inner(context, grad_attn_out)
    grad_context = times_transpose(grad_attn_out, out_weight).astype(jnp.bfloat16)
    grad_heads = grad_context.reshape(windows, WINDOW, HEADS, HEAD_SIZE)
    scores, queries, keys_all, values = window_scores(projected, segments_block)
    probs = jnp.exp(scores - log_totals)
    weights = probs.astype(jnp.bfloat16)
    grad_weights = jnp.einsum(
        "bqhe,bkhe->bhqk", grad_heads, values, preferred_element_type=jnp.float32
    )
    row_terms = jnp.sum(probs * grad_weights, axis=-1, keepdims=True)
    grad_scores = (probs * (grad_weights - row_terms)).astype(jnp.bfloat16)
    grad_queries = jnp.einsum(
        "bhqk,bkhe->bqhe", grad_scores, keys_all, preferred_element_type=jnp.float32
    ) * HEAD_SIZE ** (-0.5)
    grad_keys = jnp.einsum(
        "bhqk,bqhe->bkhe", grad_scores, queries, preferred_element_type=jnp.float32
    ) * HEAD_SIZE ** (-0.5)
    grad_values = jnp.einsum(
        "bhqk,bqhe->bkhe", weights, grad_heads, preferred_element_type=jnp.float32
    )
    grad_proj = (
        jnp.stack([grad_queries, grad_keys, grad_values], axis=2)
        .reshape(row_count, 3 * D)
        .astype(jnp.bfloat16)
    )
    proj_sums = jnp.sum(grad_proj.astype(jnp.float32), axis=0)
    grad_query_bias = proj_sums[:D]
    grad_value_bias = proj_sums[2 * D :]
    grad_qkv_weight = rows_inner(normed, grad_proj)
    grad_normed = times_transpose(grad_proj, qkv_weight)
    grad_gain_one = jnp.sum(grad_normed * norm_one, axis=0)
    grad_shift_one = jnp.sum(grad_normed, axis=0)
    grad_inputs = grad_attention + normal_back(grad_normed * gain_one, norm_one, scale_one)
    local_grad = jnp.concatenate(
        [
            grad_qkv_weight.reshape(-1),
            grad_out_weight.reshape(-1),
            grad_in_weight.reshape(-1),
            grad_down_weight.reshape(-1),
            grad_in_bias,
            grad_gain_one,
            grad_shift_one,
            grad_query_bias,
            grad_value_bias,
            grad_out_bias,
            grad_gain_two,
            grad_shift_two,
            grad_down_bias,
        ]
    )
    conv_grad = jnp.concatenate(
        [grad_conv_weight.reshape(-1), grad_conv_bias, grad_gain_three, grad_shift_three]
    )
    return (grad_inputs, local_grad, conv_grad)


def plain_device(characters, segment_ids, cotangent, local_params, conv_params):
    devices = lax.axis_size("fsdp")
    local_shard = local_params.shape[0]
    conv_shard = conv_params.shape[0]
    local_pad = local_shard * devices - LOCAL_COUNT
    conv_pad = conv_shard * devices - CONV_COUNT
    local_total = jnp.zeros((1, local_shard), jnp.float32)
    conv_total = jnp.zeros((1, conv_shard), jnp.float32)
    molecule_list = []
    gradient_list = []
    for micro_index in range(MICRO):
        local_full, conv_full = (
            lax.all_gather(local_params, "fsdp", axis=0, tiled=True),
            lax.all_gather(conv_params, "fsdp", axis=0, tiled=True),
        )
        molecules, saved_state = forward_pass(
            characters[micro_index],
            segment_ids[micro_index],
            unpack(local_full, local_layout()),
            unpack(conv_full, conv_layout()),
        )
        local_full, conv_full = (
            lax.all_gather(local_params, "fsdp", axis=0, tiled=True),
            lax.all_gather(conv_params, "fsdp", axis=0, tiled=True),
        )
        grad_inputs, local_grad, conv_grad = backward_pass(
            cotangent[micro_index],
            saved_state,
            unpack(local_full, local_layout()),
            unpack(conv_full, conv_layout()),
        )
        local_table = jnp.concatenate([local_grad, jnp.zeros((local_pad,), jnp.float32)]).reshape(
            devices, local_shard
        )
        conv_table = jnp.concatenate([conv_grad, jnp.zeros((conv_pad,), jnp.float32)]).reshape(
            devices, conv_shard
        )
        local_part, conv_part = (
            lax.psum_scatter(local_table, "fsdp", scatter_dimension=0, tiled=True),
            lax.psum_scatter(conv_table, "fsdp", scatter_dimension=0, tiled=True),
        )
        local_total = local_total + local_part
        conv_total = conv_total + conv_part
        molecule_list.append(molecules)
        gradient_list.append(grad_inputs)
    return (
        jnp.stack(molecule_list),
        jnp.stack(gradient_list),
        local_total.reshape(-1),
        conv_total.reshape(-1),
    )


def fused_kernel(geo, rows, in_names, out_names, scratch_names, *refs):
    n_in, n_out = len(in_names), len(out_names)
    every = dict(zip(list(in_names) + list(out_names) + list(scratch_names), refs))
    me, core, z, sib, first, second = where_am_i()
    g = SimpleNamespace(n=geo.n, Z=geo.Z, geo=geo, me=me, core=core, z=z, sib=sib, first=first, second=second, rows=rows, mols=rows // RATE, **every)
    g.from_sib = (every["from_sib_l"], every["from_sib_c"])
    program(g)


def program(g):
    Z = g.Z
    start_gather(g)
    ag = Gather(g, (LAYER_PARTS, 1))
    own = [e for e in GATHER if e[0] == 1 and e[1] == 0 and e[3] == 0]
    for e in own: ag.event(*e)
    table = gather_table(g)
    forward = [
        lambda: (same_segment(g), forward_norm(g)), lambda: forward_qkv(g, 0, 6), lambda: forward_qkv(g, 6, 9),
        lambda: forward_attention(g, 0, 12), lambda: forward_attention(g, 12, 24), lambda: forward_out(g),
        lambda: forward_up(g, 0, 4), lambda: forward_up(g, 4, 8), lambda: forward_up(g, 8, 12), lambda: forward_down(g), lambda: forward_conv(g)]
    for e in GATHER:
        if e[0] == 0: forward[e[1]]()
        elif e[0] == 5: ag.convert(*e[1:])
        elif e not in own: ag.event(*e)
    for e in GATHER:
        if 1 <= e[0] <= 4: ag.drain(*e)
    table()
    NL, NC = g.geo.RL // PART, g.geo.RC // PART
    conv_steps = [(1, p, zt) for zt in reversed(range(Z)) for p in range(NC)]
    layer_steps = [(0, p, zt) for zt in reversed(range(Z)) for p in range(NL)]
    names = {1: "second", 2: "first", 3: "line", 4: "last"}
    jobs = [(names[e[0]], e[1:4], e[4]) for e in SCATTER if e[0]]
    sc = Scatter(g, jobs)
    for zt in reversed(range(Z)):
        grad_conv_weight(g, zt)
        for st in conv_steps:
            if st[2] == zt: sc.p0(*st)
    def send_planes(lo, hi):
        sc.grant_all()
        for st in layer_steps:
            if lo <= st[2] < hi: sc.p0(*st)
    vec_stages = reduce_vectors(g)
    plane = 8 * g.geo.RL
    def plane_of(row): return -(-row // plane)
    q3, q2, q1 = plane_of(W2_ROW), plane_of(W1_ROW), plane_of(O_ROW)
    backward = [
        lambda: (back_conv(g), grad_down_weight(g, 0, 6)),
        lambda: (grad_down_weight(g, 6, 12), send_planes(q3, Z)),
        lambda: back_down(g, 0, 6),
        lambda: back_down(g, 6, 12),
        lambda: grad_up_weight(g, 0, 3),
        lambda: (grad_up_weight(g, 3, 6), send_planes(q2, q3)),
        lambda: back_up(g),
        lambda: (grad_out_weight(g), send_planes(q1, q2), back_out(g)),
        lambda: back_attention(g, 0, 1),
        lambda: back_attention(g, 1, 2),
        lambda: back_attention(g, 2, 3),
        lambda: back_attention(g, 3, 4),
        lambda: (grad_qkv_weight(g), send_planes(0, q1)),
        lambda: (back_qkv(g), pltpu.make_async_copy(g.dc, g.cg, g.osem.at[0]).start(), vec_stages[0]()),
        lambda: vec_stages[1](),
        lambda: vec_stages[2](),
        lambda: vec_stages[3](),
    ]
    for e in SCATTER:
        if e[0] == 0: backward[e[1]]()
        else: sc.run()
    layer, conv = place_gradients(g)
    layer[0]()
    conv[0]()
    layer[1]()
    conv[1]()
    layer[2]()
    conv[2]()
    for st in conv_steps + layer_steps: sc.finish(*st)
    pltpu.make_async_copy(g.dc, g.cg, g.osem.at[0]).wait()


def fused(n, characters, segment_ids, cotangent, local_params, conv_params):
    geo = Geo(n, local_params.shape[0], conv_params.shape[0])
    micro, span, _ = characters.shape
    rows = micro * span
    x = characters.reshape(rows, D)
    cot = cotangent.reshape(rows // RATE, D)
    xl = jnp.pad(local_params, (0, geo.XL * LANE - local_params.shape[0])).reshape(geo.XL, LANE)
    xc = jnp.pad(conv_params, (0, geo.XC * LANE - conv_params.shape[0])).reshape(geo.XC, LANE)
    V = pl.BlockSpec(memory_space=pltpu.VMEM)
    A = pl.BlockSpec(memory_space=pl.ANY)
    S = jax.ShapeDtypeStruct
    Z, H = geo.Z, geo.HL + geo.HC
    ins = dict(x=x, seg=segment_ids, cot=cot, xl=xl, xc=xc)
    outs = dict(mol=(V, S((rows // RATE, D), BF16)), cg=(A, S((rows, D), F32)), outl=(V, S((-(-geo.XL // 96) * 96, LANE), F32)), outc=(V, S((-(-geo.XC // 96) * 96, LANE), F32)))
    for name, count in (("from_sib", n // 2),):
        outs[name + "_l"] = (A, S((count * geo.RL, LANE), BF16))
        outs[name + "_c"] = (A, S((count * geo.RC, LANE), BF16))
    W = pltpu.VMEM
    DMA = pltpu.SemaphoreType.DMA
    sc = state_shapes(rows)
    sc.update(wqkv=W((D, 3 * D), BF16), wo=W((D, D), BF16), w1=W((D, FF), BF16), w2=W((FF, D), BF16), wc=W((FF, D), BF16))
    sc.update(gl=W((n * geo.RL, LANE), BF16), gc=W((n * geo.RC, LANE), BF16), hb=W((H, LANE), BF16), hr=W((H, LANE), BF16), tail=W((H, LANE), BF16),
              xlf=W((geo.HL + -(-geo.XL // 96) * 96 + 32, LANE), F32), xcf=W((geo.HC + -(-geo.XC // 96) * 96 + 32, LANE), F32), vgrad=W((H, LANE), F32), vland=W((4, H, LANE), F32),
              fs=W((H, LANE), F32), fr=W((H, LANE), F32), tmp=W((RING, PART, LANE), BF16), below_l=W((geo.RL, LANE), BF16), below_c=W((geo.RC, LANE), BF16))
    parts = (geo.RL + geo.RC) // PART
    sc.update(rsem=DMA((LAYER_PARTS + 1, n)), ssem=DMA((LAYER_PARTS + 1, 13 * Z)), hsem=DMA((6,)), tsem=DMA((5,)), osem=DMA((1,)), vsem=DMA((5,)), fsem=DMA((RING,)), credit=pltpu.SemaphoreType.REGULAR((5, (geo.RL + geo.RC) // PART * Z)),
              r_sib=DMA((parts, n // 2)), s_sib=DMA((parts, n // 2)), r_second=DMA((parts, 2 * Z)), s_second=DMA((parts, 2 * Z)),
              r_first=DMA((parts, Z)), s_first=DMA((parts, Z)), r_up=DMA((parts, Z)), s_up=DMA((parts, Z)), r_down=DMA((parts, Z)), s_down=DMA((parts, Z)))
    res = pl.pallas_call(
        functools.partial(fused_kernel, geo, rows, list(ins), list(outs), list(sc)),
        out_shape=[s for _, s in outs.values()],
        in_specs=[V] * len(ins),
        out_specs=[b for b, _ in outs.values()],
        scratch_shapes=list(sc.values()),
        compiler_params=pltpu.CompilerParams(collective_id=0, has_side_effects=True, vmem_limit_bytes=64 << 20),
        name="layer",
    )(*ins.values())
    mol, cg, outl, outc = res[:4]
    return (mol.reshape(micro, span // RATE, D), cg.reshape(micro, span, D), outl.reshape(-1)[:local_params.shape[0]], outc.reshape(-1)[:conv_params.shape[0]])


def on_device(characters, segment_ids, cotangent, local_params, conv_params):
    n = lax.axis_size("fsdp")
    rows = characters.shape[0] * characters.shape[1]
    whole = n // 8 == PLANES and n % 8 == 0 and (2 * 72 * D) % (n * UNIT) == 0 and (2 * 24 * D) % (n * UNIT) == 0
    exact = local_params.shape[0] * n == LOCAL_COUNT and conv_params.shape[0] * n == CONV_COUNT
    if whole and exact and rows == 4 * WINDOW:
        return fused(n, characters, segment_ids, cotangent, local_params, conv_params)
    return plain_device(characters, segment_ids, cotangent, local_params, conv_params)


def solution(mesh):
    return jax.shard_map(
        on_device,
        mesh=mesh,
        in_specs=(P(None, "fsdp", None), P(None, "fsdp"), P(None, "fsdp", None), P("fsdp"), P("fsdp")),
        out_specs=(P(None, "fsdp", None), P(None, "fsdp", None), P("fsdp"), P("fsdp")),
        check_vma=False,
    )
```

```python
import functools
import math
from types import SimpleNamespace

import jax
import jax.numpy as jnp
from jax import lax
from jax.experimental import pallas as pl
from jax.experimental.pallas import tpu as pltpu
from jax.sharding import PartitionSpec as P

MESH = pl.DeviceIdType.MESH
F32, BF16 = jnp.float32, jnp.bfloat16
D, FF, HEADS, WINDOW, RATE, MICRO, HEAD_SIZE = 768, 3072, 12, 128, 4, 2, 64
LOCAL_COUNT, CONV_COUNT = 7087104, 2361600
LANE = 128
UNIT = 1152
EPS = EPSILON = 1e-05


DC = D // LANE
FC = FF // LANE
VB1, VG1, VS1, VBQ, VBV, VBO, VG2, VS2, VB2 = 0, 24, 30, 36, 42, 48, 54, 60, 66
VBC, VG3, VS3 = 78, 84, 90
QKV_ROW, O_ROW, W1_ROW, W2_ROW = 0, 18 * D, 24 * D, 48 * D

def nn(a, b): return jnp.dot(a, b, preferred_element_type=F32)
def nt(a, b): return lax.dot_general(a, b, (((1,), (1,)), ((), ())), preferred_element_type=F32)
def tn(a, b): return lax.dot_general(a, b, (((0,), (0,)), ((), ())), preferred_element_type=F32)

def loop(n, fn, unroll=1):
    def body(i, _):
        fn(i)
        return 0
    lax.fori_loop(0, n, body, 0, unroll=unroll)

def span(lo, hi, n, fn, unroll=1):
    hi = n if hi is None else hi
    def body(i, _):
        fn(i)
        return 0
    lax.fori_loop(lo, hi, body, 0, unroll=unroll)

def at(i, size): return pl.ds(pl.multiple_of(i * size, size), size)

def vec(r, row, blocks=DC):
    return jnp.concatenate([r.vecs[row + i:row + i + 1, :] for i in range(blocks)], axis=1)

def put(r, row, value):
    for i in range(value.shape[1] // LANE):
        r.vgrad[row + i:row + i + 1, :] = value[:, i * LANE:(i + 1) * LANE]

def add_to(r, row, value):
    for i in range(value.shape[1] // LANE):
        r.vgrad[row + i:row + i + 1, :] += value[:, i * LANE:(i + 1) * LANE]

def normal(v):
    mean = jnp.mean(v, axis=-1, keepdims=True)
    cen = v - mean
    var = jnp.mean(cen * cen, axis=-1, keepdims=True)
    s = lax.rsqrt(var + EPS)
    return cen * s, s

def normal_back(dn, nrm, s):
    return s * (dn - jnp.mean(dn, axis=-1, keepdims=True) - nrm * jnp.mean(dn * nrm, axis=-1, keepdims=True))

def colsum(v): return jnp.sum(v, axis=0, keepdims=True)

def gelu_both(h):
    cdf = 0.5 + 0.5 * lax.erf(h * (0.5 ** 0.5))
    pdf = jnp.exp(-0.5 * h * h) * (1.0 / math.sqrt(2 * math.pi))
    return h * cdf, cdf + h * pdf

RB = 64
def forward_norm(r):
    g1, s1 = vec(r, VG1), vec(r, VS1)
    def f(i):
        nrm, _ = normal(r.x[at(i, RB), :].astype(F32))
        r.a[at(i, RB), :] = (nrm * g1 + s1).astype(BF16)
    loop(r.rows // RB, f, 2)

def forward_qkv(r, lo=0, hi=9):
    bias = jnp.concatenate([vec(r, VBQ), jnp.zeros((1, D), F32), vec(r, VBV)], axis=1)
    for i in range(18):
        r.bias[i:i + 1, :] = bias[:, i * LANE:(i + 1) * LANE]
    def f(i):
        b = jnp.concatenate([r.bias[pl.ds(2 * i, 1), :], r.bias[pl.ds(2 * i + 1, 1), :]], axis=1)
        r.P[:, at(i, 256)] = (nn(r.a[...], r.wqkv[:, at(i, 256)]) + b).astype(BF16)
    span(lo, hi, 9, f, 3)

def halves(v):
    lo = lax.broadcasted_iota(jnp.int32, v.shape, 1) < 64
    w = v.astype(F32)
    z = jnp.zeros_like(w)
    return jnp.concatenate([jnp.where(lo, w, z), jnp.where(lo, z, w)], axis=0).astype(BF16)

def pick(v):
    lo = lax.broadcasted_iota(jnp.int32, (WINDOW, LANE), 1) < 64
    return jnp.where(lo, v[:WINDOW], v[WINDOW:])

def heads_of(r, i):
    w = i // DC
    hp = lax.rem(i, DC)
    rows = at(w, WINDOW)
    return w, rows, at(hp, LANE), at(hp + DC, LANE), at(hp + 2 * DC, LANE)

def same_segment(r):
    per = r.seg.shape[1] // WINDOW
    for w in range(r.rows // WINDOW):
        ids = r.seg[w // per:w // per + 1, w % per * WINDOW:(w % per + 1) * WINDOW].astype(F32)
        wide = jnp.broadcast_to(ids, (WINDOW, WINDOW))
        r.same[w] = (wide == wide.T).astype(F32)

def forward_attention(r, lo=0, hi=24):
    def f(i):
        w, rows, cq, ck, cv = heads_of(r, i)
        q2 = halves(r.P[rows, cq])
        s = nt(q2, r.P[rows, ck]) * 0.125
        same = r.same[w]
        same2 = jnp.concatenate([same, same], axis=0) > 0.5
        s = jnp.where(same2, s, -1e30)
        e = jnp.exp(s - jnp.max(s, axis=-1, keepdims=True))
        p = (e / jnp.sum(e, axis=-1, keepdims=True)).astype(BF16)
        r.p[i] = p
        r.ctx[rows, cq] = pick(nn(p, r.P[rows, cv])).astype(BF16)
    span(lo, hi, 24, f, 4)

def forward_out(r):
    bo = vec(r, VBO)
    for i in range(3):
        c = slice(i * 256, (i + 1) * 256)
        r.y1[:, c] = r.x[:, c].astype(F32) + nn(r.ctx[...], r.wo[:, c]) + bo[:, c]
    g2, s2 = vec(r, VG2), vec(r, VS2)
    def f(i):
        nrm, _ = normal(r.y1[at(i, RB), :])
        r.c[at(i, RB), :] = (nrm * g2 + s2).astype(BF16)
    loop(r.rows // RB, f, 2)

def forward_up(r, lo=0, hi=12):
    def f(i):
        b = jnp.concatenate([r.vecs[pl.ds(VB1 + 2 * i, 1), :], r.vecs[pl.ds(VB1 + 2 * i + 1, 1), :]], axis=1)
        h = nn(r.c[...], r.w1[:, at(i, 256)]) + b
        hid, slope = gelu_both(h)
        r.hid[:, at(i, 256)] = hid.astype(BF16)
        r.slope[:, at(i, 256)] = slope.astype(BF16)
    span(lo, hi, 12, f, 2)

def forward_down(r):
    b2 = vec(r, VB2)
    for i in range(3):
        c = slice(i * 256, (i + 1) * 256)
        v = r.y1[:, c] + nn(r.hid[...], r.w2[:, c]) + b2[:, c]
        r.ys[2 * i] = v[:, :LANE]
        r.ys[2 * i + 1] = v[:, LANE:]
    for j in range(RATE):
        for c in range(DC):
            r.u[j * r.mols:(j + 1) * r.mols, c * LANE:(c + 1) * LANE] = r.ys[c, pl.ds(j, r.mols, stride=RATE), :].astype(BF16)

def forward_conv(r):
    z = vec(r, VBC)
    for j in range(RATE):
        z = z + nn(r.u[j * r.mols:(j + 1) * r.mols, :], r.wc[j * D:(j + 1) * D, :])
    w, slope = gelu_both(z)
    nrm, s = normal(w)
    r.mol[...] = (nrm * vec(r, VG3) + vec(r, VS3)).astype(BF16)
    t = r.cot[...].astype(F32)
    put(r, VG3, colsum(t * nrm))
    put(r, VS3, colsum(t))
    dw = normal_back(t * vec(r, VG3), nrm, s)
    dz = (dw * slope).astype(BF16)
    r.dz[...] = dz
    put(r, VBC, colsum(dz.astype(F32)))

def emit_flat(r, dst, row0, tile, base=0):
    k, m = tile.shape[0], tile.shape[1] // LANE
    for c in range(m):
        r.scr[pl.ds(base + c, k, stride=m), :] = tile[:, c * LANE:(c + 1) * LANE]
    dst[pl.ds(pl.multiple_of(row0, 16), k * m), :] = r.scr[base:base + k * m, :].astype(BF16)

def emit_pair(r, dst, row0, lhs, rhs):
    tiles = [tn(lhs(h), rhs) for h in (0, 1)]
    for h in (0, 1): emit_flat(r, dst, row0 + h * 256 * DC, tiles[h], h * 256 * DC)

def grad_conv_weight(r, j):
    for i in range(3):
        emit_flat(r, r.gc, (j * D + i * 256) * DC, tn(r.u[j * r.mols:(j + 1) * r.mols, i * 256:(i + 1) * 256], r.dz[...]), i % 2 * 256 * DC)

def back_conv(r):
    for j in range(RATE):
        v = nt(r.dz[...], r.wc[j * D:(j + 1) * D, :])
        for c in range(DC):
            r.ys[c, pl.ds(j, r.mols, stride=RATE), :] = v[:, c * LANE:(c + 1) * LANE]
    for c in range(DC):
        v = r.ys[c]
        r.u[:, c * LANE:(c + 1) * LANE] = v.astype(BF16)
        put(r, VB2 + c, colsum(v))

def grad_down_weight(r, lo=0, hi=12):
    span(lo // 2, hi // 2, 6, lambda i: emit_pair(r, r.gl, W2_ROW + i * 512 * DC, lambda h: r.hid[:, pl.ds(pl.multiple_of(i * 512 + h * 256, 256), 256)], r.u[...]))

def back_down(r, lo=0, hi=12):
    def f(i):
        cols = [at(2 * i + h, 256) for h in (0, 1)]
        slopes = [r.slope[:, c] for c in cols]
        outs = [(nt(r.u[...], r.w2[c, :]) * s.astype(F32)).astype(BF16) for c, s in zip(cols, slopes)]
        for h, (c, dh) in enumerate(zip(cols, outs)):
            r.slope[:, c] = dh
            s = colsum(dh.astype(F32))
            r.vgrad[pl.ds(VB1 + 4 * i + 2 * h, 1), :] = s[:, :LANE]
            r.vgrad[pl.ds(VB1 + 4 * i + 2 * h + 1, 1), :] = s[:, LANE:]
    span(lo // 2, hi // 2, 6, f)

def grad_up_weight(r, lo=0, hi=6):
    span(lo, hi, 6, lambda i: emit_flat(r, r.gl, W1_ROW + i * 128 * FC, tn(r.c[:, at(i, 128)], r.slope[...])))

def fold(v):
    out = v[0:8]
    for i in range(1, v.shape[0] // 8):
        out = out + v[i * 8:(i + 1) * 8]
    return out

def row_sums(r, fn, count):
    def body(i, acc):
        return tuple(a + fold(v) for a, v in zip(acc, fn(at(i, RB))))
    acc = lax.fori_loop(0, r.rows // RB, body, tuple(jnp.zeros((8, D), F32) for _ in range(count)), unroll=2)
    return [colsum(a) for a in acc]

def back_up(r):
    for i in range(3):
        r.dc[:, i * 256:(i + 1) * 256] = nt(r.slope[...], r.w1[i * 256:(i + 1) * 256, :])
    g2 = vec(r, VG2)
    def f(rows):
        dc = r.dc[rows, :]
        nrm, s = normal(r.y1[rows, :])
        dy2 = jnp.concatenate([r.ys[c, rows, :] for c in range(DC)], axis=1)
        dy1 = dy2 + normal_back(dc * g2, nrm, s)
        r.dc[rows, :] = dy1
        r.u[rows, :] = dy1.astype(BF16)
        return dc * nrm, dc, dy1
    sums = row_sums(r, f, 3)
    put(r, VG2, sums[0])
    put(r, VS2, sums[1])
    put(r, VBO, sums[2])

def grad_out_weight(r):
    for i in range(3):
        emit_flat(r, r.gl, O_ROW + i * 256 * DC, tn(r.ctx[:, i * 256:(i + 1) * 256], r.u[...]), i % 2 * 256 * DC)

def back_out(r):
    for i in range(3):
        r.c[:, i * 256:(i + 1) * 256] = nt(r.u[...], r.wo[i * 256:(i + 1) * 256, :]).astype(BF16)

AG = 6
def back_attention(r, lo=0, hi=None):
    def f(i):
        where = [heads_of(r, i * AG + j) for j in range(AG)]
        loads = [(r.c[rows, cq], r.P[rows, cq], r.P[rows, ck], r.P[rows, cv], r.p[i * AG + j]) for j, (w, rows, cq, ck, cv) in enumerate(where)]
        outs = []
        for do, q, k, v, pb in loads:
            do2, q2 = halves(do), halves(q)
            p = pb.astype(F32)
            dp = nt(do2, v)
            ds = (p * (dp - jnp.sum(p * dp, axis=-1, keepdims=True))).astype(BF16)
            outs.append((pick(nn(ds, k)) * 0.125, tn(ds, q2) * 0.125, tn(pb, do2)))
        for (w, rows, cq, ck, cv), (dq, dk, dv) in zip(where, outs):
            r.P[rows, cq] = dq.astype(BF16)
            r.P[rows, ck] = dk.astype(BF16)
            r.P[rows, cv] = dv.astype(BF16)
    span(lo, hi, r.rows // WINDOW * DC // AG, f)

def grad_qkv_weight(r):
    for c in range(DC):
        r.vgrad[VBQ + c:VBQ + c + 1, :] = colsum(r.P[:, c * LANE:(c + 1) * LANE].astype(F32))
        r.vgrad[VBV + c:VBV + c + 1, :] = colsum(r.P[:, 2 * D + c * LANE:2 * D + (c + 1) * LANE].astype(F32))
    loop(6, lambda i: emit_flat(r, r.gl, QKV_ROW + i * 128 * 18, tn(r.a[:, at(i, 128)], r.P[...])))

def back_qkv(r):
    for i in range(3):
        r.y1[:, i * 256:(i + 1) * 256] = nt(r.P[...], r.wqkv[i * 256:(i + 1) * 256, :])
    g1 = vec(r, VG1)
    def f(rows):
        da = r.y1[rows, :]
        nrm, s = normal(r.x[rows, :].astype(F32))
        r.dc[rows, :] = r.dc[rows, :] + normal_back(da * g1, nrm, s)
        return da * nrm, da
    sums = row_sums(r, f, 2)
    put(r, VG1, sums[0])
    put(r, VS1, sums[1])

def state_shapes(rows):
    mols = rows // RATE
    V = pltpu.VMEM
    return dict(
        same=V((rows // WINDOW, WINDOW, WINDOW), F32), a=V((rows, D), BF16), P=V((rows, 3 * D), BF16), p=V((rows // WINDOW * DC, 2 * WINDOW, LANE), BF16),
        ctx=V((rows, D), BF16), y1=V((rows, D), F32), c=V((rows, D), BF16), slope=V((rows, FF), BF16), hid=V((rows, FF), BF16),
        ys=V((DC, rows, LANE), F32), u=V((rows, D), BF16), dz=V((mols, D), BF16), dc=V((rows, D), F32),
        scr=V((128 * FC, LANE), F32), bias=V((24, LANE), F32), vecs=V((96, LANE), F32))


class Geo:
    def __init__(self, n, local_shard, conv_shard):
        self.n = n
        self.local_shard, self.conv_shard = local_shard, conv_shard
        self.Z = n // 8
        self.RL = (12 * D * D) // LANE // n
        self.RC = (4 * D * D) // LANE // n
        self.dl = local_shard - self.RL * LANE
        self.dc = conv_shard - self.RC * LANE
        self.HL = -(-(self.dl * n) // (8 * LANE)) * 8
        self.HC = -(-(self.dc * n) // (8 * LANE)) * 8
        self.XL = -(-local_shard // (8 * LANE)) * 8
        self.XC = -(-conv_shard // (8 * LANE)) * 8

def where_am_i():
    me = lax.axis_index("fsdp")
    core = lax.rem(me, 2)
    bx = lax.rem(me // 2, 2)
    by = lax.rem(me // 4, 2)
    z = me // 8
    sib = me + 1 - 2 * core
    xn = me + 2 - 4 * bx
    yn = me + 4 - 8 * by
    first = xn + core * (yn - xn)
    second = yn + core * (xn - yn)
    return me, core, z, sib, first, second

def realign(out_ref, out_base, lo, hi, x_ref, shift, step=16):
    q = shift // LANE
    r = lax.rem(shift, LANE)
    turn = lax.rem(LANE - r, LANE)
    lane = lax.broadcasted_iota(jnp.int32, (step, LANE), 1)
    keep = lane < (LANE - r)
    def body(i, _):
        low = x_ref[pl.ds(q + i * step, step), :]
        high = x_ref[pl.ds(q + i * step + 1, step), :]
        val = jnp.where(keep, pltpu.roll(low, turn, 1), pltpu.roll(high, turn, 1))
        out_ref[pl.ds(pl.multiple_of(out_base + i * step, step), step), :] = val.astype(out_ref.dtype)
        return 0
    many = max(u for u in (1, 2, 3, 4, 5, 6, 8) if (hi - lo) // step % u == 0)
    lax.fori_loop(lo // step, hi // step, body, 0, unroll=many)

def widen(dst_ref, dst_base, src_ref, rows):
    step = 248 if rows % 248 == 0 else 8
    for i in range(rows // step):
        dst_ref[dst_base + i * step:dst_base + (i + 1) * step, :] = src_ref[i * step:(i + 1) * step, :].astype(F32)

def convert_unit(src_ref, base, w_ref, krow, cols, scr):
    groups = UNIT // (16 * cols)
    def body(g, _):
        scr[0:16 * cols, :] = src_ref[pl.ds(pl.multiple_of(base + g * 16 * cols, 16), 16 * cols), :].astype(F32)
        for cc in range(cols):
            v = scr[pl.ds(cc, 16, stride=cols), :]
            w_ref[pl.ds(pl.multiple_of(krow + g * 16, 16), 16), cc * LANE:(cc + 1) * LANE] = v.astype(BF16)
        return 0
    lax.fori_loop(0, groups, body, 0)


def start_gather(g):
    n, Z, geo, me, z = g.n, g.Z, g.geo, g.me, g.z
    RL, RC = geo.RL, geo.RC
    nxt = lax.rem(me + 1, n)
    bar = pltpu.get_barrier_semaphore()
    far = lax.rem(me + n + 2 * g.core - 1, n)
    for dev in (g.sib, g.first, g.second, far):
        pl.semaphore_signal(bar, inc=1, device_id=(dev,), device_id_type=MESH)
    @pl.when(z > 0)
    def _(): pl.semaphore_signal(bar, inc=1, device_id=(me - 8,), device_id_type=MESH)
    @pl.when(z < Z - 1)
    def _(): pl.semaphore_signal(bar, inc=1, device_id=(me + 8,), device_id_type=MESH)
    widen(g.xlf, geo.HL, g.xl, geo.XL)
    widen(g.xcf, geo.HC, g.xc, geo.XC)
    realign(g.fs, 0, 0, geo.HL, g.xlf, geo.local_shard, 8)
    realign(g.fs, geo.HL, 0, geo.HC, g.xcf, geo.conv_shard, 8)
    g.hb[...] = g.fs[...].astype(BF16)
    HA, HB = 96, 96
    lshift, cshift = geo.HL * LANE - geo.dl * me, geo.HC * LANE - geo.dc * me
    realign(g.gl, me * RL, HA, RL, g.xlf, lshift)
    realign(g.gc, me * RC, HB, RC, g.xcf, cshift)
    pl.semaphore_wait(bar, 4 + jnp.where(z > 0, 1, 0) + jnp.where(z < Z - 1, 1, 0))
    halo = pltpu.make_async_remote_copy(src_ref=g.hb, dst_ref=g.hr, send_sem=g.hsem.at[0], recv_sem=g.hsem.at[1], device_id=(nxt,), device_id_type=MESH)
    halo.start()
    halo.wait()
    g.xlf[0:geo.HL, :] = g.hr[0:geo.HL, :].astype(F32)
    g.xcf[0:geo.HC, :] = g.hr[geo.HL:geo.HL + geo.HC, :].astype(F32)
    realign(g.gl, me * RL, 0, HA, g.xlf, lshift)
    realign(g.gc, me * RC, 0, HB, g.xcf, cshift)
    @pl.when(me == n - 1)
    def _():
        g.tail[...] = g.hb[...]


def gather_table(g):
    Z, me, z = g.Z, g.me, g.z
    bx, by = lax.rem(me // 2, 2), lax.rem(me // 4, 2)
    one = g.core == 1
    def copy(slot, dev):
        return pltpu.make_async_remote_copy(src_ref=g.tail, dst_ref=g.tail, send_sem=g.tsem.at[slot], recv_sem=g.tsem.at[4], device_id=(dev,), device_id_type=MESH)
    right = jnp.logical_and(one, bx == 1)
    corner = jnp.logical_and(right, by == 1)
    sends = ((0, me - 8, jnp.logical_and(corner, z > 0)), (1, g.first, corner), (2, g.second, right), (3, g.sib, one))
    @pl.when(me != g.n - 1)
    def _(): copy(0, g.sib).wait_recv()
    for slot, dev, there in sends:
        @pl.when(there)
        def _(): copy(slot, dev).start()
    g.vecs[...] = g.tail[...].astype(F32)
    def finish():
        for slot, dev, there in sends:
            @pl.when(there)
            def _(): copy(slot, dev).wait_send()
    return finish


class Gather:
    def __init__(self, g, parts):
        self.g = g
        self.parts = parts
        self.size = (g.geo.RL, g.geo.RC)
        self.place = (g.gl, g.gc)

    def source(self, dz, f, s):
        g = self.g
        return g.me + 8 * dz + f * (g.first - g.me) + s * (g.second - g.me)

    def copy(self, k, p, src, dev, slot):
        g = self.g
        rows = self.size[k] // self.parts[k]
        i = p if k == 0 else self.parts[0] + p
        ref = self.place[k].at[pl.ds(pl.multiple_of(src * self.size[k] + p * rows, 16), rows)]
        return pltpu.make_async_remote_copy(src_ref=ref, dst_ref=ref, send_sem=g.ssem.at[i, slot], recv_sem=g.rsem.at[i, src], device_id=(dev,), device_id_type=MESH)

    def sends(self, o, k, p, dz):
        g, z, Z = self.g, self.g.z, self.g.Z
        f, s = {1: (0, 0), 2: (1, 0), 3: (0, 1), 4: (1, 1)}[o]
        src, zi = self.source(dz, f, s), z + dz
        out = []
        if k == 1:
            if dz >= 0: out.append((lambda: self.copy(k, p, src, g.me - 8, (o - 1) * Z + zi), z > 0))
            if dz <= 0: out.append((lambda: self.copy(k, p, src, g.me + 8, (o + 3) * Z + zi), z < Z - 1))
            if dz == 0 and o == 1: out.append((lambda: self.copy(k, p, src, g.first, 8 * Z), None))
            if dz == 0 and o <= 2: out.append((lambda: self.copy(k, p, src, g.second, 8 * Z + o), None))
            out.append((lambda: self.copy(k, p, src, g.sib, (8 + o) * Z + zi), None))
            return src, out
        if o == 1:
            if dz >= 0: out.append((lambda: self.copy(k, p, src, g.me - 8, zi), z > 0))
            if dz <= 0: out.append((lambda: self.copy(k, p, src, g.me + 8, Z + zi), z < Z - 1))
            out.append((lambda: self.copy(k, p, src, g.first, 2 * Z + zi), None))
        if o <= 2: out.append((lambda: self.copy(k, p, src, g.second, (2 + o) * Z + zi), None))
        out.append((lambda: self.copy(k, p, src, g.sib, (4 + o) * Z + zi), None))
        return src, out

    def guard(self, cond, fn):
        if cond is None: fn()
        else: pl.when(cond)(fn)

    def valid(self, dz, fn):
        z, Z = self.g.z, self.g.Z
        self.guard(None if dz == 0 else jnp.logical_and(z + dz >= 0, z + dz < Z), fn)

    def event(self, o, k, p, dz):
        def fn():
            src, sends = self.sends(o, k, p, dz)
            if o > 1 or dz != 0: self.copy(k, p, src, self.g.sib, 0).wait_recv()
            for cp, there in sends: self.guard(there, lambda cp=cp: cp().start())
        self.valid(dz, fn)

    def drain(self, o, k, p, dz):
        def fn():
            for cp, there in self.sends(o, k, p, dz)[1]: self.guard(there, lambda cp=cp: cp().wait_send())
        self.valid(dz, fn)

    def convert(self, k, dz):
        g = self.g
        per = 2 * self.size[k] // UNIT
        def fn():
            def chip_body(c, _):
                src = self.source(dz, c // 2, lax.rem(c, 2))
                for p in range(self.parts[k]): self.copy(k, p, src + g.sib - g.me, g.sib, 0).wait_recv()
                def unit(i, _):
                    t = (src // 2) * per + i
                    base = t * UNIT
                    if k == 1: convert_unit(g.gc, base, g.wc, t * 192, 6, g.scr)
                    else:
                        @pl.when(t < 12)
                        def _(): convert_unit(g.gl, base, g.wqkv, t * 64, 18, g.scr)
                        @pl.when(jnp.logical_and(t >= 12, t < 16))
                        def _(): convert_unit(g.gl, base, g.wo, (t - 12) * 192, 6, g.scr)
                        @pl.when(jnp.logical_and(t >= 16, t < 32))
                        def _(): convert_unit(g.gl, base, g.w1, (t - 16) * 48, 24, g.scr)
                        @pl.when(t >= 32)
                        def _(): convert_unit(g.gl, base, g.w2, (t - 32) * 192, 6, g.scr)
                    return 0
                lax.fori_loop(0, per, unit, 0)
                return 0
            lax.fori_loop(0, 4, chip_body, 0)
        self.valid(dz, fn)


PART = 576
RING = 4


class Scatter:
    def __init__(self, g, jobs):
        self.g = g
        self.size = (g.geo.RL, g.geo.RC)
        self.own = (g.gl, g.gc)
        self.jobs = jobs
        self.started, self.granted, self.waiting = set(), set(), []
        self.opened = self.closed = 0
        self.arrived = set()
        self.leads = {}
        for kind, step, x in jobs:
            if kind == "second": self.leads.setdefault(step, x)

    def target(self, zt, f, s):
        g = self.g
        return g.me + 8 * (zt - g.z) + f * (g.first - g.me) + s * (g.second - g.me)

    def other(self, zt, f, s): return self.target(zt, f, s) + self.g.sib - self.g.me

    def rows(self, k, t, p):
        return pl.ds(pl.multiple_of(t * self.size[k] + p * PART, 16), PART)

    def sem(self, k, p):
        return p if k == 0 else self.size[0] // PART + p

    def move(self, src, dst, send, recv, i, index, dev):
        return pltpu.make_async_remote_copy(src_ref=src, dst_ref=dst, send_sem=send.at[i, index], recv_sem=recv.at[i, index], device_id=(dev,), device_id_type=MESH)

    def at(self, k, p, t): return self.own[k].at[self.rows(k, t, p)]

    def to_sib(self, k, p, zt):
        g = self.g
        half, size, part = g.n // 2, self.size[k], pl.ds(p * PART, PART)
        src = self.own[k].reshape(half, 2, size, LANE).at[pl.ds(4 * zt, 4), 1 - g.core, part]
        dst = g.from_sib[k].reshape(half, size, LANE).at[pl.ds(4 * zt, 4), part]
        return self.move(src, dst, g.s_sib, g.r_sib, self.sem(k, p), zt, g.sib)

    def to_second(self, k, p, zt, f):
        g = self.g
        t = self.target(zt, f, 1)
        return self.move(self.at(k, p, t), self.at(k, p, t + g.sib - g.me), g.s_second, g.r_second, self.sem(k, p), 2 * zt + f, g.second)

    def to_first(self, k, p, zt):
        g = self.g
        t = self.target(zt, 1, 0)
        return self.move(self.at(k, p, t), self.at(k, p, t + g.second - g.me + g.sib - g.me), g.s_first, g.r_first, self.sem(k, p), zt, g.first)

    def down(self, k, p, zt):
        g = self.g
        return self.move(self.at(k, p, self.target(zt, 0, 0)), self.at(k, p, self.other(zt, 1, 1)), g.s_down, g.r_down, self.sem(k, p), zt, g.me - 8)

    def up(self, k, p, zt, land):
        g = self.g
        dst = (g.below_l, g.below_c)[k].at[pl.ds(p * PART, PART)] if land else self.at(k, p, self.other(zt, 1, 1))
        return self.move(self.at(k, p, self.target(zt, 0, 0)), dst, g.s_up, g.r_up, self.sem(k, p), zt, g.me + 8)

    def p0(self, k, p, zt):
        self.to_sib(k, p, zt).start()
        self.started.add((k, p, zt))
        self.waiting.append((k, p, zt))

    def ticket(self, which, k, p, zt): return self.g.credit.at[which, self.sem(k, p) * self.g.Z + zt]

    def credit(self, which, k, p, zt, dev):
        pl.semaphore_signal(self.ticket(which, k, p, zt), inc=1, device_id=(dev,), device_id_type=MESH)

    def grant(self, k, p, zt):
        g = self.g
        z, Z, me = g.z, g.Z, g.me
        self.to_sib(k, p, zt).wait_send()
        self.credit(0, k, p, zt, g.second)
        self.credit(1, k, p, zt, g.first)
        if zt < Z - 1:
            @pl.when(jnp.logical_and(z >= zt, z < Z - 1))
            def _(): self.credit(2, k, p, zt, me + 8)
        if zt > 1:
            @pl.when(jnp.logical_and(z < zt, z > 0))
            def _(): self.credit(3, k, p, zt, me - 8)
        self.granted.add((k, p, zt))

    def grant_all(self):
        for st in self.waiting: self.grant(*st)
        self.waiting = []

    def spend(self, which, k, p, zt): pl.semaphore_wait(self.ticket(which, k, p, zt), 1)

    def place(self, job):
        kind, (k, p, zt), x = job
        z, Z = self.g.z, self.g.Z
        if kind == "second": return None, self.target(zt, x, 1)
        if kind == "first": return None, self.target(zt, 1, 0)
        if kind == "last": return z == zt, self.target(zt, 0, 0)
        return z == (x[0] if x[1] else Z - 1 - x[0]), self.target(zt, 0, 0)

    def describe(self, job):
        kind, (k, p, zt), x = job
        g = self.g
        z, Z, me = g.z, g.Z, g.me
        if kind == "second":
            def send():
                if self.leads[k, p, zt] == x: self.spend(0, k, p, zt)
                self.to_second(k, p, zt, x).start()
            return [], [], None, send
        if kind == "first":
            def send():
                self.spend(1, k, p, zt)
                self.to_first(k, p, zt).start()
            return [self.to_second(k, p, zt, 1)], [self.at(k, p, self.other(zt, 1, 0))], None, send
        waits = [self.to_second(k, p, zt, 0), self.to_first(k, p, zt)]
        lands = [self.at(k, p, self.other(zt, 0, 0)), self.at(k, p, self.other(zt, 0, 1))]
        far = self.at(k, p, self.other(zt, 1, 1))
        if kind == "last":
            if zt < Z - 1:
                waits.append(self.down(k, p, zt))
                lands.append(far)
            if zt > 0:
                waits.append(self.up(k, p, zt, True))
                lands.append((g.below_l, g.below_c)[k].at[pl.ds(p * PART, PART)])
            return waits, lands, (g.xlf, g.xcf)[k], None
        hop, upward = x
        if hop > 0:
            waits.append(self.up(k, p, zt, False) if upward else self.down(k, p, zt))
            lands.append(far)
        here = hop if upward else Z - 1 - hop
        def send():
            if upward:
                if here + 1 < zt: self.spend(3, k, p, zt)
                self.up(k, p, zt, here + 1 == zt).start()
            else:
                self.spend(2, k, p, zt)
                self.down(k, p, zt).start()
        return waits, lands, None, send

    def guard(self, cond, fn):
        if cond is None: fn()
        else: pl.when(cond)(fn)

    def fetch(self, job, t, slot):
        g, (k, p, zt) = self.g, job[1]
        return pltpu.make_async_copy(g.from_sib[k].at[self.rows(k, t // 2, p)], g.tmp.at[slot], g.fsem.at[slot])

    def open(self, i):
        job = self.jobs[i]
        cond, t = self.place(job)
        if job[1] not in self.arrived:
            self.to_sib(*job[1]).wait_recv()
            self.arrived.add(job[1])
        self.guard(cond, lambda: self.fetch(job, t, i % RING).start())

    def close(self, i):
        g, job, slot = self.g, self.jobs[i], i % RING
        k, p, zt = job[1]
        cond, t = self.place(job)
        def fn():
            waits, lands, out, send = self.describe(job)
            for cp in waits: cp.wait_recv()
            self.fetch(job, t, slot).wait()
            mine = self.at(k, p, t)
            def body(b, _):
                r = pl.ds(pl.multiple_of(b * 16, 16), 16)
                acc = mine[r, :].astype(F32) + g.tmp[slot, r, :].astype(F32)
                for land in lands: acc = acc + land[r, :].astype(F32)
                if out is None: mine[r, :] = acc.astype(BF16)
                else: out[pl.ds(pl.multiple_of(p * PART + b * 16, 16), 16), :] = acc
                return 0
            lax.fori_loop(0, PART // 16, body, 0, unroll=4)
            if send is not None: send()
        self.guard(cond, fn)

    def run(self):
        i = self.closed
        step = self.jobs[i][1]
        if step not in self.granted: self.grant_all()
        while self.opened < len(self.jobs) and self.opened < i + RING and self.jobs[self.opened][1] in self.started:
            self.open(self.opened)
            self.opened += 1
        self.close(i)
        self.closed += 1

    def finish(self, k, p, zt):
        g = self.g
        for f in (0, 1): self.to_second(k, p, zt, f).wait_send()
        self.to_first(k, p, zt).wait_send()
        @pl.when(g.z > zt)
        def _(): self.down(k, p, zt).wait_send()
        @pl.when(g.z < zt)
        def _(): self.up(k, p, zt, False).wait_send()


def reduce_vectors(g):
    Z, me, z = g.Z, g.me, g.z
    core = lax.rem(me, 2)
    bx, by = lax.rem(me // 2, 2), lax.rem(me // 4, 2)
    def cp(slot, dev):
        return pltpu.make_async_remote_copy(src_ref=g.vgrad, dst_ref=g.vland.at[slot], send_sem=g.vsem.at[0], recv_sem=g.vsem.at[1 + slot], device_id=(dev,), device_id_type=MESH)
    def take(slot):
        cp(slot, g.sib).wait_recv()
        g.vgrad[...] = g.vgrad[...] + g.vland[slot]
    def give(slot, dev): cp(slot, dev).start()
    on = core == 1
    right = jnp.logical_and(on, bx == 1)
    corner = jnp.logical_and(right, by == 1)
    def stage(giver, taker, slot, dev):
        def fn():
            @pl.when(giver)
            def _(): give(slot, dev)
            @pl.when(taker)
            def _(): take(slot)
        return fn
    stages = [stage(jnp.logical_not(on), on, 0, g.sib), stage(jnp.logical_and(on, bx == 0), right, 1, g.second),
              stage(jnp.logical_and(right, by == 0), corner, 2, g.first)]
    stages += [stage(jnp.logical_and(corner, z == h), jnp.logical_and(corner, z == h + 1), 3, me + 8) for h in range(Z - 1)]
    def finish():
        @pl.when(me != g.n - 1)
        def _(): cp(0, g.sib).wait_send()
    return stages, finish


def place_gradients(g):
    n, geo, me = g.n, g.geo, g.me
    prv = lax.rem(me + n - 1, n)
    edge = me == n - 1
    HL, HC = geo.HL, geo.HC
    skip = VBC - HL
    vectors = ((0, HL, HL), (VBC, HL + HC, HC - skip))
    def part(k):
        x, out, rows, drift = ((g.xlf, g.outl, geo.RL, geo.dl), (g.xcf, g.outc, geo.RC, geo.dc))[k]
        first, last = (0, HL) if k == 0 else (HL, HL + HC)
        cp = pltpu.make_async_remote_copy(src_ref=g.fs.at[pl.ds(first, last - first)], dst_ref=g.fr.at[pl.ds(first, last - first)],
                                          send_sem=g.hsem.at[2 + 2 * k], recv_sem=g.hsem.at[3 + 2 * k], device_id=(prv,), device_id_type=MESH)
        def begin():
            g.fs[first:last, :] = x[0:last - first, :]
            cp.start()
        split = (rows - 96) // 96 * 96
        def middle(): realign(out, 0, 0, split, x, drift * me)
        def end():
            cp.wait()
            lo, hi, count = vectors[k]
            x[rows:rows + count, :] = jnp.where(edge, g.vgrad[lo:hi, :], g.fr[first:first + count, :])
            realign(out, 0, split, out.shape[0], x, drift * me)
        return begin, middle, end
    return part(0), part(1)


PLANES = 4
LAYER_PARTS = 1
GATHER = (
    (1, 1, 0, 0), (1, 0, 0, 0), (1, 0, 0, -1), (3, 0, 0, 0), (2, 1, 0, 0), (2, 0, 0, 0), (1, 0, 0, 1), (4, 1, 0, 0), (1, 0, 0, 2), (3, 1, 0, 0),
    (1, 0, 0, -2), (2, 0, 0, -1), (3, 1, 0, 1), (4, 0, 0, 0), (2, 0, 0, 1), (4, 1, 0, -1), (3, 1, 0, -1), (1, 0, 0, 3), (4, 1, 0, 1), (2, 1, 0, 1),
    (3, 0, 0, -1), (1, 0, 0, -3), (1, 1, 0, 1), (5, 0, 0), (2, 1, 0, -1), (0, 0), (3, 0, 0, 1), (1, 1, 0, -1), (3, 0, 0, 2), (5, 1, 0), (2, 0, 0, -2),
    (4, 0, 0, -1), (5, 1, 1), (2, 0, 0, 2), (3, 1, 0, 2), (5, 1, -1), (3, 0, 0, -2), (2, 0, 0, -3), (3, 0, 0, -3), (3, 1, 0, -2), (4, 1, 0, -2),
    (4, 0, 0, 1), (2, 1, 0, 2), (1, 1, 0, 2), (4, 1, 0, 2), (5, 0, -1), (2, 0, 0, 3), (4, 0, 0, -2), (1, 1, 0, -2), (2, 1, 0, -2), (4, 0, 0, -3),
    (5, 0, 1), (5, 0, -2), (5, 0, -3), (0, 1), (0, 2), (0, 3), (4, 0, 0, 2), (5, 1, -2), (5, 1, 2), (0, 4), (2, 1, 0, -3), (3, 0, 0, 3), (4, 0, 0, 3),
    (0, 5), (5, 0, 2), (1, 1, 0, 3), (0, 6), (3, 1, 0, 3), (4, 1, 0, 3), (0, 7), (2, 1, 0, 3), (1, 1, 0, -3), (4, 1, 0, -3), (3, 1, 0, -3), (0, 8),
    (5, 0, 3), (0, 9), (5, 1, -3), (5, 1, 3), (0, 10),
)
SCATTER = (
    (1, 1, 0, 3, 0), (1, 1, 0, 2, 1), (1, 1, 0, 3, 1), (1, 1, 0, 0, 1), (1, 1, 0, 1, 1), (0, 0), (0, 1), (1, 0, 1, 3, 1), (1, 0, 0, 3, 1),
    (1, 0, 1, 3, 0), (1, 1, 0, 2, 0), (0, 2), (1, 1, 0, 1, 0), (2, 1, 0, 2, 0), (2, 1, 0, 1, 0), (0, 3), (0, 4), (2, 0, 0, 3, 0), (1, 1, 0, 0, 0),
    (0, 5), (1, 0, 0, 2, 0), (1, 0, 0, 2, 1), (1, 0, 2, 2, 0), (2, 1, 0, 3, 0), (0, 6), (2, 1, 0, 0, 0), (1, 0, 2, 2, 1), (3, 1, 0, 2, (0, True)),
    (3, 1, 0, 1, (0, True)), (0, 7), (1, 0, 0, 3, 0), (1, 0, 2, 3, 1), (2, 0, 0, 2, 0), (1, 0, 2, 3, 0), (0, 8), (3, 1, 0, 3, (0, True)), (0, 9),
    (1, 0, 1, 2, 1), (0, 10), (3, 1, 0, 2, (0, False)), (2, 0, 2, 2, 0), (3, 1, 0, 2, (1, True)), (3, 0, 0, 3, (0, True)), (2, 0, 1, 3, 0),
    (1, 0, 1, 2, 0), (2, 0, 2, 3, 0), (0, 11), (3, 0, 0, 3, (1, True)), (3, 1, 0, 0, (0, False)), (2, 0, 1, 2, 0), (0, 12), (1, 0, 0, 0, 1),
    (3, 0, 0, 3, (2, True)), (3, 0, 2, 2, (0, False)), (3, 0, 2, 3, (0, True)), (1, 0, 0, 0, 0), (4, 1, 0, 2, 0), (1, 0, 1, 1, 1),
    (3, 1, 0, 3, (1, True)), (3, 1, 0, 1, (0, False)), (1, 0, 2, 0, 1), (3, 0, 1, 2, (0, False)), (3, 0, 0, 2, (0, False)), (3, 1, 0, 0, (1, False)),
    (2, 0, 0, 0, 0), (3, 0, 0, 2, (0, True)), (3, 0, 1, 3, (0, True)), (3, 0, 2, 3, (1, True)), (1, 0, 1, 0, 1), (3, 0, 2, 2, (0, True)),
    (1, 0, 2, 0, 0), (3, 0, 1, 2, (0, True)), (0, 13), (3, 0, 0, 2, (1, True)), (2, 0, 2, 0, 0), (1, 0, 1, 0, 0), (3, 0, 0, 0, (0, False)),
    (3, 0, 1, 3, (1, True)), (3, 1, 0, 3, (2, True)), (3, 1, 0, 0, (2, False)), (1, 0, 0, 1, 1), (1, 0, 0, 1, 0), (3, 0, 0, 0, (2, False)),
    (3, 0, 2, 0, (0, False)), (3, 0, 1, 2, (1, True)), (3, 1, 0, 1, (1, False)), (3, 0, 0, 0, (1, False)), (2, 0, 1, 0, 0), (0, 14),
    (3, 0, 2, 3, (2, True)), (2, 0, 0, 1, 0), (1, 0, 2, 1, 1), (3, 0, 1, 0, (0, False)), (3, 0, 2, 0, (2, False)), (1, 0, 1, 1, 0), (4, 1, 0, 1, 0),
    (3, 0, 2, 2, (1, True)), (3, 0, 2, 0, (1, False)), (3, 0, 1, 3, (2, True)), (3, 0, 1, 0, (1, False)), (3, 0, 1, 0, (2, False)), (2, 0, 1, 1, 0),
    (0, 15), (3, 0, 0, 1, (0, False)), (4, 0, 2, 3, 0), (2, 0, 2, 1, 0), (3, 0, 1, 1, (0, True)), (1, 0, 2, 1, 0), (3, 0, 1, 1, (0, False)),
    (3, 0, 0, 1, (1, False)), (4, 0, 0, 3, 0), (3, 0, 0, 1, (0, True)), (0, 16), (4, 0, 0, 2, 0), (4, 1, 0, 3, 0), (4, 0, 1, 1, 0),
    (3, 0, 2, 1, (0, True)), (3, 0, 1, 1, (1, False)), (4, 0, 0, 1, 0), (3, 0, 2, 1, (0, False)), (3, 0, 2, 1, (1, False)), (4, 0, 1, 2, 0),
    (4, 0, 1, 0, 0), (4, 0, 2, 1, 0), (4, 0, 0, 0, 0), (4, 1, 0, 0, 0), (4, 0, 2, 2, 0), (4, 0, 1, 3, 0), (4, 0, 2, 0, 0),
)


def local_layout():
    return ((D, 3 * D), (D, D), (D, FF), (FF, D), (FF,)) + ((D,),) * 8


def conv_layout():
    return ((RATE * D, D), (D,), (D,), (D,))


def unpack(packed, layout):
    offset = 0
    pieces = []
    for extent in layout:
        length = math.prod(extent)
        pieces.append(packed[offset : offset + length].reshape(extent))
        offset = offset + length
    return pieces


def normalize_parts(values):
    average = jnp.mean(values, axis=-1, keepdims=True)
    centred = values - average
    spread = jnp.mean(centred * centred, axis=-1, keepdims=True)
    scaling = lax.rsqrt(spread + EPSILON)
    return (centred * scaling, scaling)


def normal_back(grad_normed, normed, scaling):
    first_mean = jnp.mean(grad_normed, axis=-1, keepdims=True)
    second_mean = jnp.mean(grad_normed * normed, axis=-1, keepdims=True)
    return scaling * (grad_normed - first_mean - normed * second_mean)


def product(left, right):
    return jnp.dot(left, right, preferred_element_type=jnp.float32)


def rows_inner(left, right):
    return lax.dot_general(
        left, right, (((0,), (0,)), ((), ())), preferred_element_type=jnp.float32
    )


def times_transpose(left, right):
    return lax.dot_general(
        left, right, (((1,), (1,)), ((), ())), preferred_element_type=jnp.float32
    )


def gelu_exact(values):
    return jax.nn.gelu(values, approximate=False)


def gelu_grad(values, upstream):
    return jax.vjp(gelu_exact, values)[1](upstream)[0]


def window_scores(projected, segments_block):
    row_count = projected.shape[0]
    windows = row_count // WINDOW
    heads_view = projected.reshape(windows, WINDOW, 3, HEADS, HEAD_SIZE)
    queries = heads_view[:, :, 0]
    keys_all = heads_view[:, :, 1]
    values = heads_view[:, :, 2]
    scores = jnp.einsum(
        "bqhe,bkhe->bhqk", queries, keys_all, preferred_element_type=jnp.float32
    ) * HEAD_SIZE ** (-0.5)
    grouped = segments_block.reshape(windows, WINDOW)
    allowed = grouped[:, None, :, None] == grouped[:, None, None, :]
    return (jnp.where(allowed, scores, -1e30), queries, keys_all, values)


def forward_pass(characters_block, segments_block, local_weights, conv_weights):
    (
        qkv_weight,
        out_weight,
        in_weight,
        down_weight,
        in_bias,
        gain_one,
        shift_one,
        query_bias,
        value_bias,
        out_bias,
        gain_two,
        shift_two,
        down_bias,
    ) = local_weights
    conv_weight, conv_bias, gain_three, shift_three = conv_weights
    row_count = characters_block.shape[0]
    inputs = characters_block.astype(jnp.float32)
    norm_one, scale_one = normalize_parts(inputs)
    normed = (norm_one * gain_one + shift_one).astype(jnp.bfloat16)
    proj_bias = jnp.concatenate([query_bias, jnp.zeros_like(query_bias), value_bias])
    projected = (product(normed, qkv_weight) + proj_bias).astype(jnp.bfloat16)
    scores, queries, keys_all, values = window_scores(projected, segments_block)
    largest = jnp.max(scores, axis=-1, keepdims=True)
    raised = jnp.exp(scores - largest)
    totals = jnp.sum(raised, axis=-1, keepdims=True)
    log_totals = largest + jnp.log(totals)
    weights = (raised / totals).astype(jnp.bfloat16)
    attended = jnp.einsum("bhqk,bkhe->bqhe", weights, values, preferred_element_type=jnp.float32)
    context = attended.reshape(row_count, D).astype(jnp.bfloat16)
    after_attention = inputs + product(context, out_weight) + out_bias
    norm_two, scale_two = normalize_parts(after_attention)
    middle = (norm_two * gain_two + shift_two).astype(jnp.bfloat16)
    pre_act = product(middle, in_weight) + in_bias
    hidden = gelu_exact(pre_act).astype(jnp.bfloat16)
    after_feed = after_attention + product(hidden, down_weight) + down_bias
    grouped_rows = after_feed.astype(jnp.bfloat16).reshape(row_count // RATE, RATE * D)
    conv_pre = product(grouped_rows, conv_weight) + conv_bias
    norm_three, scale_three = normalize_parts(gelu_exact(conv_pre))
    molecules = (norm_three * gain_three + shift_three).astype(jnp.bfloat16)
    saved_state = (
        segments_block,
        norm_one,
        scale_one,
        normed,
        projected,
        log_totals,
        context,
        norm_two,
        scale_two,
        middle,
        pre_act,
        hidden,
        grouped_rows,
        conv_pre,
        norm_three,
        scale_three,
    )
    return (molecules, saved_state)


def backward_pass(cotangent_block, saved_state, local_weights, conv_weights):
    (
        qkv_weight,
        out_weight,
        in_weight,
        down_weight,
        in_bias,
        gain_one,
        shift_one,
        query_bias,
        value_bias,
        out_bias,
        gain_two,
        shift_two,
        down_bias,
    ) = local_weights
    conv_weight, conv_bias, gain_three, shift_three = conv_weights
    (
        segments_block,
        norm_one,
        scale_one,
        normed,
        projected,
        log_totals,
        context,
        norm_two,
        scale_two,
        middle,
        pre_act,
        hidden,
        grouped_rows,
        conv_pre,
        norm_three,
        scale_three,
    ) = saved_state
    row_count = normed.shape[0]
    windows = row_count // WINDOW
    upstream = cotangent_block.astype(jnp.float32)
    grad_gain_three = jnp.sum(upstream * norm_three, axis=0)
    grad_shift_three = jnp.sum(upstream, axis=0)
    grad_activated = normal_back(upstream * gain_three, norm_three, scale_three)
    grad_conv_pre = gelu_grad(conv_pre, grad_activated).astype(jnp.bfloat16)
    grad_conv_bias = jnp.sum(grad_conv_pre.astype(jnp.float32), axis=0)
    grad_conv_weight = rows_inner(grouped_rows, grad_conv_pre)
    grad_feed = times_transpose(grad_conv_pre, conv_weight).reshape(row_count, D)
    grad_down_bias = jnp.sum(grad_feed, axis=0)
    grad_branch = grad_feed.astype(jnp.bfloat16)
    grad_down_weight = rows_inner(hidden, grad_branch)
    grad_hidden = times_transpose(grad_branch, down_weight)
    grad_pre = gelu_grad(pre_act, grad_hidden).astype(jnp.bfloat16)
    grad_in_bias = jnp.sum(grad_pre.astype(jnp.float32), axis=0)
    grad_in_weight = rows_inner(middle, grad_pre)
    grad_middle = times_transpose(grad_pre, in_weight)
    grad_gain_two = jnp.sum(grad_middle * norm_two, axis=0)
    grad_shift_two = jnp.sum(grad_middle, axis=0)
    grad_attention = grad_feed + normal_back(grad_middle * gain_two, norm_two, scale_two)
    grad_out_bias = jnp.sum(grad_attention, axis=0)
    grad_attn_out = grad_attention.astype(jnp.bfloat16)
    grad_out_weight = rows_inner(context, grad_attn_out)
    grad_context = times_transpose(grad_attn_out, out_weight).astype(jnp.bfloat16)
    grad_heads = grad_context.reshape(windows, WINDOW, HEADS, HEAD_SIZE)
    scores, queries, keys_all, values = window_scores(projected, segments_block)
    probs = jnp.exp(scores - log_totals)
    weights = probs.astype(jnp.bfloat16)
    grad_weights = jnp.einsum(
        "bqhe,bkhe->bhqk", grad_heads, values, preferred_element_type=jnp.float32
    )
    row_terms = jnp.sum(probs * grad_weights, axis=-1, keepdims=True)
    grad_scores = (probs * (grad_weights - row_terms)).astype(jnp.bfloat16)
    grad_queries = jnp.einsum(
        "bhqk,bkhe->bqhe", grad_scores, keys_all, preferred_element_type=jnp.float32
    ) * HEAD_SIZE ** (-0.5)
    grad_keys = jnp.einsum(
        "bhqk,bqhe->bkhe", grad_scores, queries, preferred_element_type=jnp.float32
    ) * HEAD_SIZE ** (-0.5)
    grad_values = jnp.einsum(
        "bhqk,bqhe->bkhe", weights, grad_heads, preferred_element_type=jnp.float32
    )
    grad_proj = (
        jnp.stack([grad_queries, grad_keys, grad_values], axis=2)
        .reshape(row_count, 3 * D)
        .astype(jnp.bfloat16)
    )
    proj_sums = jnp.sum(grad_proj.astype(jnp.float32), axis=0)
    grad_query_bias = proj_sums[:D]
    grad_value_bias = proj_sums[2 * D :]
    grad_qkv_weight = rows_inner(normed, grad_proj)
    grad_normed = times_transpose(grad_proj, qkv_weight)
    grad_gain_one = jnp.sum(grad_normed * norm_one, axis=0)
    grad_shift_one = jnp.sum(grad_normed, axis=0)
    grad_inputs = grad_attention + normal_back(grad_normed * gain_one, norm_one, scale_one)
    local_grad = jnp.concatenate(
        [
            grad_qkv_weight.reshape(-1),
            grad_out_weight.reshape(-1),
            grad_in_weight.reshape(-1),
            grad_down_weight.reshape(-1),
            grad_in_bias,
            grad_gain_one,
            grad_shift_one,
            grad_query_bias,
            grad_value_bias,
            grad_out_bias,
            grad_gain_two,
            grad_shift_two,
            grad_down_bias,
        ]
    )
    conv_grad = jnp.concatenate(
        [grad_conv_weight.reshape(-1), grad_conv_bias, grad_gain_three, grad_shift_three]
    )
    return (grad_inputs, local_grad, conv_grad)


def plain_device(characters, segment_ids, cotangent, local_params, conv_params):
    devices = lax.axis_size("fsdp")
    local_shard = local_params.shape[0]
    conv_shard = conv_params.shape[0]
    local_pad = local_shard * devices - LOCAL_COUNT
    conv_pad = conv_shard * devices - CONV_COUNT
    local_total = jnp.zeros((1, local_shard), jnp.float32)
    conv_total = jnp.zeros((1, conv_shard), jnp.float32)
    molecule_list = []
    gradient_list = []
    for micro_index in range(MICRO):
        local_full, conv_full = (
            lax.all_gather(local_params, "fsdp", axis=0, tiled=True),
            lax.all_gather(conv_params, "fsdp", axis=0, tiled=True),
        )
        molecules, saved_state = forward_pass(
            characters[micro_index],
            segment_ids[micro_index],
            unpack(local_full, local_layout()),
            unpack(conv_full, conv_layout()),
        )
        local_full, conv_full = (
            lax.all_gather(local_params, "fsdp", axis=0, tiled=True),
            lax.all_gather(conv_params, "fsdp", axis=0, tiled=True),
        )
        grad_inputs, local_grad, conv_grad = backward_pass(
            cotangent[micro_index],
            saved_state,
            unpack(local_full, local_layout()),
            unpack(conv_full, conv_layout()),
        )
        local_table = jnp.concatenate([local_grad, jnp.zeros((local_pad,), jnp.float32)]).reshape(
            devices, local_shard
        )
        conv_table = jnp.concatenate([conv_grad, jnp.zeros((conv_pad,), jnp.float32)]).reshape(
            devices, conv_shard
        )
        local_part, conv_part = (
            lax.psum_scatter(local_table, "fsdp", scatter_dimension=0, tiled=True),
            lax.psum_scatter(conv_table, "fsdp", scatter_dimension=0, tiled=True),
        )
        local_total = local_total + local_part
        conv_total = conv_total + conv_part
        molecule_list.append(molecules)
        gradient_list.append(grad_inputs)
    return (
        jnp.stack(molecule_list),
        jnp.stack(gradient_list),
        local_total.reshape(-1),
        conv_total.reshape(-1),
    )


HOP_GAP = 8


def fused_kernel(geo, rows, in_names, out_names, scratch_names, *refs):
    n_in, n_out = len(in_names), len(out_names)
    every = dict(zip(list(in_names) + list(out_names) + list(scratch_names), refs))
    me, core, z, sib, first, second = where_am_i()
    g = SimpleNamespace(n=geo.n, Z=geo.Z, geo=geo, me=me, core=core, z=z, sib=sib, first=first, second=second, rows=rows, mols=rows // RATE, **every)
    g.from_sib = (every["from_sib_l"], every["from_sib_c"])
    program(g)


def program(g):
    Z = g.Z
    start_gather(g)
    ag = Gather(g, (LAYER_PARTS, 1))
    own = [e for e in GATHER if e[0] == 1 and e[1] == 0 and e[3] == 0]
    for e in own: ag.event(*e)
    table = gather_table(g)
    forward = [
        lambda: (same_segment(g), forward_norm(g)), lambda: forward_qkv(g, 0, 6), lambda: forward_qkv(g, 6, 9),
        lambda: forward_attention(g, 0, 12), lambda: forward_attention(g, 12, 24), lambda: forward_out(g),
        lambda: forward_up(g, 0, 4), lambda: forward_up(g, 4, 8), lambda: forward_up(g, 8, 12), lambda: forward_down(g), lambda: forward_conv(g)]
    for e in GATHER:
        if e[0] == 0: forward[e[1]]()
        elif e[0] == 5: ag.convert(*e[1:])
        elif e not in own: ag.event(*e)
    for e in GATHER:
        if 1 <= e[0] <= 4: ag.drain(*e)
    table()
    NL, NC = g.geo.RL // PART, g.geo.RC // PART
    conv_steps = [(1, p, zt) for zt in reversed(range(Z)) for p in range(NC)]
    layer_steps = [(0, p, zt) for zt in reversed(range(Z)) for p in range(NL)]
    names = {1: "second", 2: "first", 3: "line", 4: "last"}
    jobs = [(names[e[0]], e[1:4], e[4]) for e in SCATTER if e[0]]
    sc = Scatter(g, jobs)
    for zt in reversed(range(Z)):
        grad_conv_weight(g, zt)
        for st in conv_steps:
            if st[2] == zt: sc.p0(*st)
    def send_planes(lo, hi):
        sc.grant_all()
        for st in layer_steps:
            if lo <= st[2] < hi: sc.p0(*st)
    vec_stages, vec_finish = reduce_vectors(g)
    plane = 8 * g.geo.RL
    def plane_of(row): return -(-row // plane)
    q3, q2, q1 = plane_of(W2_ROW), plane_of(W1_ROW), plane_of(O_ROW)
    backward = [
        lambda: (back_conv(g), grad_down_weight(g, 0, 6)),
        lambda: (grad_down_weight(g, 6, 12), send_planes(q3, Z)),
        lambda: back_down(g, 0, 6),
        lambda: back_down(g, 6, 12),
        lambda: grad_up_weight(g, 0, 3),
        lambda: (grad_up_weight(g, 3, 6), send_planes(q2, q3)),
        lambda: back_up(g),
        lambda: (grad_out_weight(g), send_planes(q1, q2), back_out(g)),
        lambda: back_attention(g, 0, 1),
        lambda: back_attention(g, 1, 2),
        lambda: back_attention(g, 2, 3),
        lambda: back_attention(g, 3, 4),
        lambda: (grad_qkv_weight(g), send_planes(0, q1)),
        lambda: (back_qkv(g), pltpu.make_async_copy(g.dc, g.cg, g.osem.at[0]).start(), vec_stages[0]()),
        lambda: vec_stages[1](),
        lambda: vec_stages[2](),
        vec_stages[3],
    ]
    late = vec_stages[4:]
    for i, e in enumerate(SCATTER):
        if e[0] == 0: backward[e[1]]()
        else: sc.run()
        if late and i >= len(SCATTER) - 1 - HOP_GAP * (len(late) - 1): late.pop(0)()
    layer, conv = place_gradients(g)
    layer[0]()
    conv[0]()
    layer[1]()
    conv[1]()
    layer[2]()
    conv[2]()
    vec_finish()
    for st in conv_steps + layer_steps: sc.finish(*st)
    pltpu.make_async_copy(g.dc, g.cg, g.osem.at[0]).wait()


def fused(n, characters, segment_ids, cotangent, local_params, conv_params):
    geo = Geo(n, local_params.shape[0], conv_params.shape[0])
    micro, span, _ = characters.shape
    rows = micro * span
    x = characters.reshape(rows, D)
    cot = cotangent.reshape(rows // RATE, D)
    xl = jnp.pad(local_params, (0, geo.XL * LANE - local_params.shape[0])).reshape(geo.XL, LANE)
    xc = jnp.pad(conv_params, (0, geo.XC * LANE - conv_params.shape[0])).reshape(geo.XC, LANE)
    V = pl.BlockSpec(memory_space=pltpu.VMEM)
    A = pl.BlockSpec(memory_space=pl.ANY)
    S = jax.ShapeDtypeStruct
    Z, H = geo.Z, geo.HL + geo.HC
    ins = dict(x=x, seg=segment_ids, cot=cot, xl=xl, xc=xc)
    outs = dict(mol=(V, S((rows // RATE, D), BF16)), cg=(A, S((rows, D), F32)), outl=(V, S((-(-geo.XL // 96) * 96, LANE), F32)), outc=(V, S((-(-geo.XC // 96) * 96, LANE), F32)))
    for name, count in (("from_sib", n // 2),):
        outs[name + "_l"] = (A, S((count * geo.RL, LANE), BF16))
        outs[name + "_c"] = (A, S((count * geo.RC, LANE), BF16))
    W = pltpu.VMEM
    DMA = pltpu.SemaphoreType.DMA
    sc = state_shapes(rows)
    sc.update(wqkv=W((D, 3 * D), BF16), wo=W((D, D), BF16), w1=W((D, FF), BF16), w2=W((FF, D), BF16), wc=W((FF, D), BF16))
    sc.update(gl=W((n * geo.RL, LANE), BF16), gc=W((n * geo.RC, LANE), BF16), hb=W((H, LANE), BF16), hr=W((H, LANE), BF16), tail=W((H, LANE), BF16),
              xlf=W((geo.HL + -(-geo.XL // 96) * 96 + 32, LANE), F32), xcf=W((geo.HC + -(-geo.XC // 96) * 96 + 32, LANE), F32), vgrad=W((H, LANE), F32), vland=W((4, H, LANE), F32),
              fs=W((H, LANE), F32), fr=W((H, LANE), F32), tmp=W((RING, PART, LANE), BF16), below_l=W((geo.RL, LANE), BF16), below_c=W((geo.RC, LANE), BF16))
    parts = (geo.RL + geo.RC) // PART
    sc.update(rsem=DMA((LAYER_PARTS + 1, n)), ssem=DMA((LAYER_PARTS + 1, 13 * Z)), hsem=DMA((6,)), tsem=DMA((5,)), osem=DMA((1,)), vsem=DMA((5,)), fsem=DMA((RING,)), credit=pltpu.SemaphoreType.REGULAR((4, (geo.RL + geo.RC) // PART * Z)),
              r_sib=DMA((parts, Z)), s_sib=DMA((parts, Z)), r_second=DMA((parts, 2 * Z)), s_second=DMA((parts, 2 * Z)),
              r_first=DMA((parts, Z)), s_first=DMA((parts, Z)), r_up=DMA((parts, Z)), s_up=DMA((parts, Z)), r_down=DMA((parts, Z)), s_down=DMA((parts, Z)))
    res = pl.pallas_call(
        functools.partial(fused_kernel, geo, rows, list(ins), list(outs), list(sc)),
        out_shape=[s for _, s in outs.values()],
        in_specs=[V] * len(ins),
        out_specs=[b for b, _ in outs.values()],
        scratch_shapes=list(sc.values()),
        compiler_params=pltpu.CompilerParams(collective_id=0, has_side_effects=True, vmem_limit_bytes=64 << 20),
        name="layer",
    )(*ins.values())
    mol, cg, outl, outc = res[:4]
    return (mol.reshape(micro, span // RATE, D), cg.reshape(micro, span, D), outl.reshape(-1)[:local_params.shape[0]], outc.reshape(-1)[:conv_params.shape[0]])


def on_device(characters, segment_ids, cotangent, local_params, conv_params):
    n = lax.axis_size("fsdp")
    rows = characters.shape[0] * characters.shape[1]
    whole = n // 8 == PLANES and n % 8 == 0 and (2 * 72 * D) % (n * UNIT) == 0 and (2 * 24 * D) % (n * UNIT) == 0
    exact = local_params.shape[0] * n == LOCAL_COUNT and conv_params.shape[0] * n == CONV_COUNT
    if whole and exact and rows == 4 * WINDOW:
        return fused(n, characters, segment_ids, cotangent, local_params, conv_params)
    return plain_device(characters, segment_ids, cotangent, local_params, conv_params)


def solution(mesh):
    return jax.shard_map(
        on_device,
        mesh=mesh,
        in_specs=(P(None, "fsdp", None), P(None, "fsdp"), P(None, "fsdp", None), P("fsdp"), P("fsdp")),
        out_specs=(P(None, "fsdp", None), P(None, "fsdp", None), P("fsdp"), P("fsdp")),
        check_vma=False,
    )
```

```python
import functools
import math
from types import SimpleNamespace

import jax
import jax.numpy as jnp
from jax import lax
from jax.experimental import pallas as pl
from jax.experimental.pallas import tpu as pltpu
from jax.sharding import PartitionSpec as P

MESH = pl.DeviceIdType.MESH
F32, BF16 = jnp.float32, jnp.bfloat16
D, FF, HEADS, WINDOW, RATE, MICRO, HEAD_SIZE = 768, 3072, 12, 128, 4, 2, 64
LOCAL_COUNT, CONV_COUNT = 7087104, 2361600
LANE = 128
UNIT = 1152
EPS = EPSILON = 1e-05


DC = D // LANE
FC = FF // LANE
VB1, VG1, VS1, VBQ, VBV, VBO, VG2, VS2, VB2 = 0, 24, 30, 36, 42, 48, 54, 60, 66
VBC, VG3, VS3 = 78, 84, 90
QKV_ROW, O_ROW, W1_ROW, W2_ROW = 0, 18 * D, 24 * D, 48 * D

def nn(a, b): return jnp.dot(a, b, preferred_element_type=F32)
def nt(a, b): return lax.dot_general(a, b, (((1,), (1,)), ((), ())), preferred_element_type=F32)
def tn(a, b): return lax.dot_general(a, b, (((0,), (0,)), ((), ())), preferred_element_type=F32)

def loop(n, fn, unroll=1):
    def body(i, _):
        fn(i)
        return 0
    lax.fori_loop(0, n, body, 0, unroll=unroll)

def span(lo, hi, n, fn, unroll=1):
    hi = n if hi is None else hi
    def body(i, _):
        fn(i)
        return 0
    lax.fori_loop(lo, hi, body, 0, unroll=unroll)

def at(i, size): return pl.ds(pl.multiple_of(i * size, size), size)

def vec(r, row, blocks=DC):
    return jnp.concatenate([r.vecs[row + i:row + i + 1, :] for i in range(blocks)], axis=1)

def put(r, row, value):
    for i in range(value.shape[1] // LANE):
        r.vgrad[row + i:row + i + 1, :] = value[:, i * LANE:(i + 1) * LANE]

def add_to(r, row, value):
    for i in range(value.shape[1] // LANE):
        r.vgrad[row + i:row + i + 1, :] += value[:, i * LANE:(i + 1) * LANE]

def normal(v):
    mean = jnp.mean(v, axis=-1, keepdims=True)
    cen = v - mean
    var = jnp.mean(cen * cen, axis=-1, keepdims=True)
    s = lax.rsqrt(var + EPS)
    return cen * s, s

def normal_back(dn, nrm, s):
    return s * (dn - jnp.mean(dn, axis=-1, keepdims=True) - nrm * jnp.mean(dn * nrm, axis=-1, keepdims=True))

def colsum(v): return jnp.sum(v, axis=0, keepdims=True)

def gelu_both(h):
    cdf = 0.5 + 0.5 * lax.erf(h * (0.5 ** 0.5))
    pdf = jnp.exp(-0.5 * h * h) * (1.0 / math.sqrt(2 * math.pi))
    return h * cdf, cdf + h * pdf

RB = 64
def forward_norm(r):
    g1, s1 = vec(r, VG1), vec(r, VS1)
    def f(i):
        nrm, _ = normal(r.x[at(i, RB), :].astype(F32))
        r.a[at(i, RB), :] = (nrm * g1 + s1).astype(BF16)
    loop(r.rows // RB, f, 2)

def forward_qkv(r, lo=0, hi=9):
    bias = jnp.concatenate([vec(r, VBQ), jnp.zeros((1, D), F32), vec(r, VBV)], axis=1)
    for i in range(18):
        r.bias[i:i + 1, :] = bias[:, i * LANE:(i + 1) * LANE]
    def f(i):
        b = jnp.concatenate([r.bias[pl.ds(2 * i, 1), :], r.bias[pl.ds(2 * i + 1, 1), :]], axis=1)
        r.P[:, at(i, 256)] = (nn(r.a[...], r.wqkv[:, at(i, 256)]) + b).astype(BF16)
    span(lo, hi, 9, f, 3)

def halves(v):
    lo = lax.broadcasted_iota(jnp.int32, v.shape, 1) < 64
    w = v.astype(F32)
    z = jnp.zeros_like(w)
    return jnp.concatenate([jnp.where(lo, w, z), jnp.where(lo, z, w)], axis=0).astype(BF16)

def pick(v):
    lo = lax.broadcasted_iota(jnp.int32, (WINDOW, LANE), 1) < 64
    return jnp.where(lo, v[:WINDOW], v[WINDOW:])

def heads_of(r, i):
    w = i // DC
    hp = lax.rem(i, DC)
    rows = at(w, WINDOW)
    return w, rows, at(hp, LANE), at(hp + DC, LANE), at(hp + 2 * DC, LANE)

def same_segment(r):
    per = r.seg.shape[1] // WINDOW
    for w in range(r.rows // WINDOW):
        ids = r.seg[w // per:w // per + 1, w % per * WINDOW:(w % per + 1) * WINDOW].astype(F32)
        wide = jnp.broadcast_to(ids, (WINDOW, WINDOW))
        r.same[w] = (wide == wide.T).astype(F32)

def forward_attention(r, lo=0, hi=24):
    def f(i):
        w, rows, cq, ck, cv = heads_of(r, i)
        q2 = halves(r.P[rows, cq])
        s = nt(q2, r.P[rows, ck]) * 0.125
        same = r.same[w]
        same2 = jnp.concatenate([same, same], axis=0) > 0.5
        s = jnp.where(same2, s, -1e30)
        e = jnp.exp(s - jnp.max(s, axis=-1, keepdims=True))
        p = (e / jnp.sum(e, axis=-1, keepdims=True)).astype(BF16)
        r.p[i] = p
        r.ctx[rows, cq] = pick(nn(p, r.P[rows, cv])).astype(BF16)
    span(lo, hi, 24, f, 6)

def forward_out(r):
    bo = vec(r, VBO)
    for i in range(3):
        c = slice(i * 256, (i + 1) * 256)
        r.y1[:, c] = r.x[:, c].astype(F32) + nn(r.ctx[...], r.wo[:, c]) + bo[:, c]
    g2, s2 = vec(r, VG2), vec(r, VS2)
    def f(i):
        nrm, _ = normal(r.y1[at(i, RB), :])
        r.c[at(i, RB), :] = (nrm * g2 + s2).astype(BF16)
    loop(r.rows // RB, f, 2)

def forward_up(r, lo=0, hi=12):
    def f(i):
        b = jnp.concatenate([r.vecs[pl.ds(VB1 + 2 * i, 1), :], r.vecs[pl.ds(VB1 + 2 * i + 1, 1), :]], axis=1)
        h = nn(r.c[...], r.w1[:, at(i, 256)]) + b
        hid, slope = gelu_both(h)
        r.hid[:, at(i, 256)] = hid.astype(BF16)
        r.slope[:, at(i, 256)] = slope.astype(BF16)
    span(lo, hi, 12, f, 4)

def forward_down(r):
    b2 = vec(r, VB2)
    for i in range(3):
        c = slice(i * 256, (i + 1) * 256)
        v = r.y1[:, c] + nn(r.hid[...], r.w2[:, c]) + b2[:, c]
        r.ys[2 * i] = v[:, :LANE]
        r.ys[2 * i + 1] = v[:, LANE:]
    for j in range(RATE):
        for c in range(DC):
            r.u[j * r.mols:(j + 1) * r.mols, c * LANE:(c + 1) * LANE] = r.ys[c, pl.ds(j, r.mols, stride=RATE), :].astype(BF16)

def forward_conv(r):
    z = vec(r, VBC)
    for j in range(RATE):
        z = z + nn(r.u[j * r.mols:(j + 1) * r.mols, :], r.wc[j * D:(j + 1) * D, :])
    w, slope = gelu_both(z)
    nrm, s = normal(w)
    r.mol[...] = (nrm * vec(r, VG3) + vec(r, VS3)).astype(BF16)
    t = r.cot[...].astype(F32)
    put(r, VG3, colsum(t * nrm))
    put(r, VS3, colsum(t))
    dw = normal_back(t * vec(r, VG3), nrm, s)
    dz = (dw * slope).astype(BF16)
    r.dz[...] = dz
    put(r, VBC, colsum(dz.astype(F32)))

def emit_flat(r, dst, row0, tile, base=0):
    k, m = tile.shape[0], tile.shape[1] // LANE
    for c in range(m):
        r.scr[pl.ds(base + c, k, stride=m), :] = tile[:, c * LANE:(c + 1) * LANE]
    dst[pl.ds(pl.multiple_of(row0, 16), k * m), :] = r.scr[base:base + k * m, :].astype(BF16)

def emit_pair(r, dst, row0, lhs, rhs):
    tiles = [tn(lhs(h), rhs) for h in (0, 1)]
    for h in (0, 1): emit_flat(r, dst, row0 + h * 256 * DC, tiles[h], h * 256 * DC)

def grad_conv_weight(r, j):
    for i in range(3):
        emit_flat(r, r.gc, (j * D + i * 256) * DC, tn(r.u[j * r.mols:(j + 1) * r.mols, i * 256:(i + 1) * 256], r.dz[...]), i % 2 * 256 * DC)

def back_conv(r):
    for j in range(RATE):
        v = nt(r.dz[...], r.wc[j * D:(j + 1) * D, :])
        for c in range(DC):
            r.ys[c, pl.ds(j, r.mols, stride=RATE), :] = v[:, c * LANE:(c + 1) * LANE]
    for c in range(DC):
        v = r.ys[c]
        r.u[:, c * LANE:(c + 1) * LANE] = v.astype(BF16)
        put(r, VB2 + c, colsum(v))

def grad_down_weight(r, lo=0, hi=12):
    span(lo // 2, hi // 2, 6, lambda i: emit_pair(r, r.gl, W2_ROW + i * 512 * DC, lambda h: r.hid[:, pl.ds(pl.multiple_of(i * 512 + h * 256, 256), 256)], r.u[...]))

def back_down(r, lo=0, hi=12):
    def f(i):
        cols = [at(2 * i + h, 256) for h in (0, 1)]
        slopes = [r.slope[:, c] for c in cols]
        outs = [(nt(r.u[...], r.w2[c, :]) * s.astype(F32)).astype(BF16) for c, s in zip(cols, slopes)]
        for h, (c, dh) in enumerate(zip(cols, outs)):
            r.slope[:, c] = dh
            s = colsum(dh.astype(F32))
            r.vgrad[pl.ds(VB1 + 4 * i + 2 * h, 1), :] = s[:, :LANE]
            r.vgrad[pl.ds(VB1 + 4 * i + 2 * h + 1, 1), :] = s[:, LANE:]
    span(lo // 2, hi // 2, 6, f)

def grad_up_weight(r, lo=0, hi=6):
    span(lo, hi, 6, lambda i: emit_flat(r, r.gl, W1_ROW + i * 128 * FC, tn(r.c[:, at(i, 128)], r.slope[...])))

def fold(v):
    out = v[0:8]
    for i in range(1, v.shape[0] // 8):
        out = out + v[i * 8:(i + 1) * 8]
    return out

def row_sums(r, fn, count):
    def body(i, acc):
        return tuple(a + fold(v) for a, v in zip(acc, fn(at(i, RB))))
    acc = lax.fori_loop(0, r.rows // RB, body, tuple(jnp.zeros((8, D), F32) for _ in range(count)), unroll=2)
    return [colsum(a) for a in acc]

def back_up(r):
    for i in range(3):
        r.dc[:, i * 256:(i + 1) * 256] = nt(r.slope[...], r.w1[i * 256:(i + 1) * 256, :])
    g2 = vec(r, VG2)
    def f(rows):
        dc = r.dc[rows, :]
        nrm, s = normal(r.y1[rows, :])
        dy2 = jnp.concatenate([r.ys[c, rows, :] for c in range(DC)], axis=1)
        dy1 = dy2 + normal_back(dc * g2, nrm, s)
        r.dc[rows, :] = dy1
        r.u[rows, :] = dy1.astype(BF16)
        return dc * nrm, dc, dy1
    sums = row_sums(r, f, 3)
    put(r, VG2, sums[0])
    put(r, VS2, sums[1])
    put(r, VBO, sums[2])

def grad_out_weight(r):
    for i in range(3):
        emit_flat(r, r.gl, O_ROW + i * 256 * DC, tn(r.ctx[:, i * 256:(i + 1) * 256], r.u[...]), i % 2 * 256 * DC)

def back_out(r):
    for i in range(3):
        r.c[:, i * 256:(i + 1) * 256] = nt(r.u[...], r.wo[i * 256:(i + 1) * 256, :]).astype(BF16)

AG = 6
def back_attention(r, lo=0, hi=None):
    def f(i):
        where = [heads_of(r, i * AG + j) for j in range(AG)]
        loads = [(r.c[rows, cq], r.P[rows, cq], r.P[rows, ck], r.P[rows, cv], r.p[i * AG + j]) for j, (w, rows, cq, ck, cv) in enumerate(where)]
        outs = []
        for do, q, k, v, pb in loads:
            do2, q2 = halves(do), halves(q)
            p = pb.astype(F32)
            dp = nt(do2, v)
            ds = (p * (dp - jnp.sum(p * dp, axis=-1, keepdims=True))).astype(BF16)
            outs.append((pick(nn(ds, k)) * 0.125, tn(ds, q2) * 0.125, tn(pb, do2)))
        for (w, rows, cq, ck, cv), (dq, dk, dv) in zip(where, outs):
            r.P[rows, cq] = dq.astype(BF16)
            r.P[rows, ck] = dk.astype(BF16)
            r.P[rows, cv] = dv.astype(BF16)
    span(lo, hi, r.rows // WINDOW * DC // AG, f)

def grad_qkv_weight(r):
    for c in range(DC):
        r.vgrad[VBQ + c:VBQ + c + 1, :] = colsum(r.P[:, c * LANE:(c + 1) * LANE].astype(F32))
        r.vgrad[VBV + c:VBV + c + 1, :] = colsum(r.P[:, 2 * D + c * LANE:2 * D + (c + 1) * LANE].astype(F32))
    loop(6, lambda i: emit_flat(r, r.gl, QKV_ROW + i * 128 * 18, tn(r.a[:, at(i, 128)], r.P[...])))

def back_qkv(r):
    for i in range(3):
        r.y1[:, i * 256:(i + 1) * 256] = nt(r.P[...], r.wqkv[i * 256:(i + 1) * 256, :])
    g1 = vec(r, VG1)
    def f(rows):
        da = r.y1[rows, :]
        nrm, s = normal(r.x[rows, :].astype(F32))
        r.dc[rows, :] = r.dc[rows, :] + normal_back(da * g1, nrm, s)
        return da * nrm, da
    sums = row_sums(r, f, 2)
    put(r, VG1, sums[0])
    put(r, VS1, sums[1])

def state_shapes(rows):
    mols = rows // RATE
    V = pltpu.VMEM
    return dict(
        same=V((rows // WINDOW, WINDOW, WINDOW), F32), a=V((rows, D), BF16), P=V((rows, 3 * D), BF16), p=V((rows // WINDOW * DC, 2 * WINDOW, LANE), BF16),
        ctx=V((rows, D), BF16), y1=V((rows, D), F32), c=V((rows, D), BF16), slope=V((rows, FF), BF16), hid=V((rows, FF), BF16),
        ys=V((DC, rows, LANE), F32), u=V((rows, D), BF16), dz=V((mols, D), BF16), dc=V((rows, D), F32),
        scr=V((128 * FC, LANE), F32), bias=V((24, LANE), F32), vecs=V((96, LANE), F32))


class Geo:
    def __init__(self, n, local_shard, conv_shard):
        self.n = n
        self.local_shard, self.conv_shard = local_shard, conv_shard
        self.Z = n // 8
        self.RL = (12 * D * D) // LANE // n
        self.RC = (4 * D * D) // LANE // n
        self.dl = local_shard - self.RL * LANE
        self.dc = conv_shard - self.RC * LANE
        self.HL = -(-(self.dl * n) // (8 * LANE)) * 8
        self.HC = -(-(self.dc * n) // (8 * LANE)) * 8
        self.XL = -(-local_shard // (8 * LANE)) * 8
        self.XC = -(-conv_shard // (8 * LANE)) * 8

def where_am_i():
    me = lax.axis_index("fsdp")
    core = lax.rem(me, 2)
    bx = lax.rem(me // 2, 2)
    by = lax.rem(me // 4, 2)
    z = me // 8
    sib = me + 1 - 2 * core
    xn = me + 2 - 4 * bx
    yn = me + 4 - 8 * by
    first = xn + core * (yn - xn)
    second = yn + core * (xn - yn)
    return me, core, z, sib, first, second

def realign(out_ref, out_base, lo, hi, x_ref, shift, step=16):
    q = shift // LANE
    r = lax.rem(shift, LANE)
    turn = lax.rem(LANE - r, LANE)
    lane = lax.broadcasted_iota(jnp.int32, (step, LANE), 1)
    keep = lane < (LANE - r)
    def body(i, _):
        low = x_ref[pl.ds(q + i * step, step), :]
        high = x_ref[pl.ds(q + i * step + 1, step), :]
        val = jnp.where(keep, pltpu.roll(low, turn, 1), pltpu.roll(high, turn, 1))
        out_ref[pl.ds(pl.multiple_of(out_base + i * step, step), step), :] = val.astype(out_ref.dtype)
        return 0
    many = max(u for u in (1, 2, 3, 4, 5, 6, 8) if (hi - lo) // step % u == 0)
    lax.fori_loop(lo // step, hi // step, body, 0, unroll=many)

def widen(dst_ref, dst_base, src_ref, rows):
    step = 248 if rows % 248 == 0 else 8
    for i in range(rows // step):
        dst_ref[dst_base + i * step:dst_base + (i + 1) * step, :] = src_ref[i * step:(i + 1) * step, :].astype(F32)

def convert_unit(src_ref, base, w_ref, krow, cols, scr):
    groups = UNIT // (16 * cols)
    def body(g, _):
        scr[0:16 * cols, :] = src_ref[pl.ds(pl.multiple_of(base + g * 16 * cols, 16), 16 * cols), :].astype(F32)
        for cc in range(cols):
            v = scr[pl.ds(cc, 16, stride=cols), :]
            w_ref[pl.ds(pl.multiple_of(krow + g * 16, 16), 16), cc * LANE:(cc + 1) * LANE] = v.astype(BF16)
        return 0
    lax.fori_loop(0, groups, body, 0)


def start_gather(g):
    n, Z, geo, me, z = g.n, g.Z, g.geo, g.me, g.z
    RL, RC = geo.RL, geo.RC
    nxt = lax.rem(me + 1, n)
    bar = pltpu.get_barrier_semaphore()
    far = lax.rem(me + n + 2 * g.core - 1, n)
    for dev in (g.sib, g.first, g.second, far):
        pl.semaphore_signal(bar, inc=1, device_id=(dev,), device_id_type=MESH)
    @pl.when(z > 0)
    def _(): pl.semaphore_signal(bar, inc=1, device_id=(me - 8,), device_id_type=MESH)
    @pl.when(z < Z - 1)
    def _(): pl.semaphore_signal(bar, inc=1, device_id=(me + 8,), device_id_type=MESH)
    widen(g.xlf, geo.HL, g.xl, geo.XL)
    widen(g.xcf, geo.HC, g.xc, geo.XC)
    realign(g.fs, 0, 0, geo.HL, g.xlf, geo.local_shard, 8)
    realign(g.fs, geo.HL, 0, geo.HC, g.xcf, geo.conv_shard, 8)
    g.hb[...] = g.fs[...].astype(BF16)
    HA, HB = 96, 96
    lshift, cshift = geo.HL * LANE - geo.dl * me, geo.HC * LANE - geo.dc * me
    realign(g.gl, me * RL, HA, RL, g.xlf, lshift)
    realign(g.gc, me * RC, HB, RC, g.xcf, cshift)
    pl.semaphore_wait(bar, 4 + jnp.where(z > 0, 1, 0) + jnp.where(z < Z - 1, 1, 0))
    halo = pltpu.make_async_remote_copy(src_ref=g.hb, dst_ref=g.hr, send_sem=g.hsem.at[0], recv_sem=g.hsem.at[1], device_id=(nxt,), device_id_type=MESH)
    halo.start()
    halo.wait()
    g.xlf[0:geo.HL, :] = g.hr[0:geo.HL, :].astype(F32)
    g.xcf[0:geo.HC, :] = g.hr[geo.HL:geo.HL + geo.HC, :].astype(F32)
    realign(g.gl, me * RL, 0, HA, g.xlf, lshift)
    realign(g.gc, me * RC, 0, HB, g.xcf, cshift)
    @pl.when(me == n - 1)
    def _():
        g.tail[...] = g.hb[...]


def gather_table(g):
    Z, me, z = g.Z, g.me, g.z
    bx, by = lax.rem(me // 2, 2), lax.rem(me // 4, 2)
    one = g.core == 1
    def copy(slot, dev):
        return pltpu.make_async_remote_copy(src_ref=g.tail, dst_ref=g.tail, send_sem=g.tsem.at[slot], recv_sem=g.tsem.at[4], device_id=(dev,), device_id_type=MESH)
    right = jnp.logical_and(one, bx == 1)
    corner = jnp.logical_and(right, by == 1)
    sends = ((0, me - 8, jnp.logical_and(corner, z > 0)), (1, g.first, corner), (2, g.second, right), (3, g.sib, one))
    @pl.when(me != g.n - 1)
    def _(): copy(0, g.sib).wait_recv()
    for slot, dev, there in sends:
        @pl.when(there)
        def _(): copy(slot, dev).start()
    g.vecs[...] = g.tail[...].astype(F32)
    def finish():
        for slot, dev, there in sends:
            @pl.when(there)
            def _(): copy(slot, dev).wait_send()
    return finish


class Gather:
    def __init__(self, g, parts):
        self.g = g
        self.parts = parts
        self.size = (g.geo.RL, g.geo.RC)
        self.place = (g.gl, g.gc)

    def source(self, dz, f, s):
        g = self.g
        return g.me + 8 * dz + f * (g.first - g.me) + s * (g.second - g.me)

    def copy(self, k, p, src, dev, slot):
        g = self.g
        rows = self.size[k] // self.parts[k]
        i = p if k == 0 else self.parts[0] + p
        ref = self.place[k].at[pl.ds(pl.multiple_of(src * self.size[k] + p * rows, 16), rows)]
        return pltpu.make_async_remote_copy(src_ref=ref, dst_ref=ref, send_sem=g.ssem.at[i, slot], recv_sem=g.rsem.at[i, src], device_id=(dev,), device_id_type=MESH)

    def sends(self, o, k, p, dz):
        g, z, Z = self.g, self.g.z, self.g.Z
        f, s = {1: (0, 0), 2: (1, 0), 3: (0, 1), 4: (1, 1)}[o]
        src, zi = self.source(dz, f, s), z + dz
        out = []
        if k == 1:
            if dz >= 0: out.append((lambda: self.copy(k, p, src, g.me - 8, (o - 1) * Z + zi), z > 0))
            if dz <= 0: out.append((lambda: self.copy(k, p, src, g.me + 8, (o + 3) * Z + zi), z < Z - 1))
            if dz == 0 and o == 1: out.append((lambda: self.copy(k, p, src, g.first, 8 * Z), None))
            if dz == 0 and o <= 2: out.append((lambda: self.copy(k, p, src, g.second, 8 * Z + o), None))
            out.append((lambda: self.copy(k, p, src, g.sib, (8 + o) * Z + zi), None))
            return src, out
        if o == 1:
            if dz >= 0: out.append((lambda: self.copy(k, p, src, g.me - 8, zi), z > 0))
            if dz <= 0: out.append((lambda: self.copy(k, p, src, g.me + 8, Z + zi), z < Z - 1))
            out.append((lambda: self.copy(k, p, src, g.first, 2 * Z + zi), None))
        if o <= 2: out.append((lambda: self.copy(k, p, src, g.second, (2 + o) * Z + zi), None))
        out.append((lambda: self.copy(k, p, src, g.sib, (4 + o) * Z + zi), None))
        return src, out

    def guard(self, cond, fn):
        if cond is None: fn()
        else: pl.when(cond)(fn)

    def valid(self, dz, fn):
        z, Z = self.g.z, self.g.Z
        self.guard(None if dz == 0 else jnp.logical_and(z + dz >= 0, z + dz < Z), fn)

    def event(self, o, k, p, dz):
        def fn():
            src, sends = self.sends(o, k, p, dz)
            if o > 1 or dz != 0: self.copy(k, p, src, self.g.sib, 0).wait_recv()
            for cp, there in sends: self.guard(there, lambda cp=cp: cp().start())
        self.valid(dz, fn)

    def drain(self, o, k, p, dz):
        def fn():
            for cp, there in self.sends(o, k, p, dz)[1]: self.guard(there, lambda cp=cp: cp().wait_send())
        self.valid(dz, fn)

    def convert(self, k, dz):
        g = self.g
        per = 2 * self.size[k] // UNIT
        def fn():
            def chip_body(c, _):
                src = self.source(dz, c // 2, lax.rem(c, 2))
                for p in range(self.parts[k]): self.copy(k, p, src + g.sib - g.me, g.sib, 0).wait_recv()
                def unit(i, _):
                    t = (src // 2) * per + i
                    base = t * UNIT
                    if k == 1: convert_unit(g.gc, base, g.wc, t * 192, 6, g.scr)
                    else:
                        @pl.when(t < 12)
                        def _(): convert_unit(g.gl, base, g.wqkv, t * 64, 18, g.scr)
                        @pl.when(jnp.logical_and(t >= 12, t < 16))
                        def _(): convert_unit(g.gl, base, g.wo, (t - 12) * 192, 6, g.scr)
                        @pl.when(jnp.logical_and(t >= 16, t < 32))
                        def _(): convert_unit(g.gl, base, g.w1, (t - 16) * 48, 24, g.scr)
                        @pl.when(t >= 32)
                        def _(): convert_unit(g.gl, base, g.w2, (t - 32) * 192, 6, g.scr)
                    return 0
                lax.fori_loop(0, per, unit, 0)
                return 0
            lax.fori_loop(0, 4, chip_body, 0)
        self.valid(dz, fn)


PART = 576
RING = 6


class Scatter:
    def __init__(self, g, jobs):
        self.g = g
        self.size = (g.geo.RL, g.geo.RC)
        self.own = (g.gl, g.gc)
        self.jobs = jobs
        self.started, self.granted, self.waiting = set(), set(), []
        self.opened = self.closed = 0
        self.arrived = set()
        self.leads = {}
        for kind, step, x in jobs:
            if kind == "second": self.leads.setdefault(step, x)

    def target(self, zt, f, s):
        g = self.g
        return g.me + 8 * (zt - g.z) + f * (g.first - g.me) + s * (g.second - g.me)

    def other(self, zt, f, s): return self.target(zt, f, s) + self.g.sib - self.g.me

    def rows(self, k, t, p):
        return pl.ds(pl.multiple_of(t * self.size[k] + p * PART, 16), PART)

    def sem(self, k, p):
        return p if k == 0 else self.size[0] // PART + p

    def move(self, src, dst, send, recv, i, index, dev):
        return pltpu.make_async_remote_copy(src_ref=src, dst_ref=dst, send_sem=send.at[i, index], recv_sem=recv.at[i, index], device_id=(dev,), device_id_type=MESH)

    def at(self, k, p, t): return self.own[k].at[self.rows(k, t, p)]

    def to_sib(self, k, p, zt):
        g = self.g
        half, size, part = g.n // 2, self.size[k], pl.ds(p * PART, PART)
        src = self.own[k].reshape(half, 2, size, LANE).at[pl.ds(4 * zt, 4), 1 - g.core, part]
        dst = g.from_sib[k].reshape(half, size, LANE).at[pl.ds(4 * zt, 4), part]
        return self.move(src, dst, g.s_sib, g.r_sib, self.sem(k, p), zt, g.sib)

    def to_second(self, k, p, zt, f):
        g = self.g
        t = self.target(zt, f, 1)
        return self.move(self.at(k, p, t), self.at(k, p, t + g.sib - g.me), g.s_second, g.r_second, self.sem(k, p), 2 * zt + f, g.second)

    def to_first(self, k, p, zt):
        g = self.g
        t = self.target(zt, 1, 0)
        return self.move(self.at(k, p, t), self.at(k, p, t + g.second - g.me + g.sib - g.me), g.s_first, g.r_first, self.sem(k, p), zt, g.first)

    def down(self, k, p, zt):
        g = self.g
        return self.move(self.at(k, p, self.target(zt, 0, 0)), self.at(k, p, self.other(zt, 1, 1)), g.s_down, g.r_down, self.sem(k, p), zt, g.me - 8)

    def up(self, k, p, zt, land):
        g = self.g
        dst = (g.below_l, g.below_c)[k].at[pl.ds(p * PART, PART)] if land else self.at(k, p, self.other(zt, 1, 1))
        return self.move(self.at(k, p, self.target(zt, 0, 0)), dst, g.s_up, g.r_up, self.sem(k, p), zt, g.me + 8)

    def p0(self, k, p, zt):
        self.to_sib(k, p, zt).start()
        self.started.add((k, p, zt))
        self.waiting.append((k, p, zt))

    def ticket(self, which, k, p, zt): return self.g.credit.at[which, self.sem(k, p) * self.g.Z + zt]

    def credit(self, which, k, p, zt, dev):
        pl.semaphore_signal(self.ticket(which, k, p, zt), inc=1, device_id=(dev,), device_id_type=MESH)

    def grant(self, k, p, zt):
        g = self.g
        z, Z, me = g.z, g.Z, g.me
        self.to_sib(k, p, zt).wait_send()
        self.credit(0, k, p, zt, g.second)
        self.credit(1, k, p, zt, g.first)
        if zt < Z - 1:
            @pl.when(jnp.logical_and(z >= zt, z < Z - 1))
            def _(): self.credit(2, k, p, zt, me + 8)
        if zt > 1:
            @pl.when(jnp.logical_and(z < zt, z > 0))
            def _(): self.credit(3, k, p, zt, me - 8)
        self.granted.add((k, p, zt))

    def grant_all(self):
        for st in self.waiting: self.grant(*st)
        self.waiting = []

    def spend(self, which, k, p, zt): pl.semaphore_wait(self.ticket(which, k, p, zt), 1)

    def place(self, job):
        kind, (k, p, zt), x = job
        z, Z = self.g.z, self.g.Z
        if kind == "second": return None, self.target(zt, x, 1)
        if kind == "first": return None, self.target(zt, 1, 0)
        if kind == "last": return z == zt, self.target(zt, 0, 0)
        return z == (x[0] if x[1] else Z - 1 - x[0]), self.target(zt, 0, 0)

    def describe(self, job):
        kind, (k, p, zt), x = job
        g = self.g
        z, Z, me = g.z, g.Z, g.me
        if kind == "second":
            def send():
                if self.leads[k, p, zt] == x: self.spend(0, k, p, zt)
                self.to_second(k, p, zt, x).start()
            return [], [], None, send
        if kind == "first":
            def send():
                self.spend(1, k, p, zt)
                self.to_first(k, p, zt).start()
            return [self.to_second(k, p, zt, 1)], [self.at(k, p, self.other(zt, 1, 0))], None, send
        waits = [self.to_second(k, p, zt, 0), self.to_first(k, p, zt)]
        lands = [self.at(k, p, self.other(zt, 0, 0)), self.at(k, p, self.other(zt, 0, 1))]
        far = self.at(k, p, self.other(zt, 1, 1))
        if kind == "last":
            if zt < Z - 1:
                waits.append(self.down(k, p, zt))
                lands.append(far)
            if zt > 0:
                waits.append(self.up(k, p, zt, True))
                lands.append((g.below_l, g.below_c)[k].at[pl.ds(p * PART, PART)])
            return waits, lands, (g.xlf, g.xcf)[k], None
        hop, upward = x
        if hop > 0:
            waits.append(self.up(k, p, zt, False) if upward else self.down(k, p, zt))
            lands.append(far)
        here = hop if upward else Z - 1 - hop
        def send():
            if upward:
                if here + 1 < zt: self.spend(3, k, p, zt)
                self.up(k, p, zt, here + 1 == zt).start()
            else:
                self.spend(2, k, p, zt)
                self.down(k, p, zt).start()
        return waits, lands, None, send

    def guard(self, cond, fn):
        if cond is None: fn()
        else: pl.when(cond)(fn)

    def fetch(self, job, t, slot):
        g, (k, p, zt) = self.g, job[1]
        return pltpu.make_async_copy(g.from_sib[k].at[self.rows(k, t // 2, p)], g.tmp.at[slot], g.fsem.at[slot])

    def open(self, i):
        job = self.jobs[i]
        cond, t = self.place(job)
        if job[1] not in self.arrived:
            self.to_sib(*job[1]).wait_recv()
            self.arrived.add(job[1])
        self.guard(cond, lambda: self.fetch(job, t, i % RING).start())

    def close(self, i):
        g, job, slot = self.g, self.jobs[i], i % RING
        k, p, zt = job[1]
        cond, t = self.place(job)
        def fn():
            waits, lands, out, send = self.describe(job)
            for cp in waits: cp.wait_recv()
            self.fetch(job, t, slot).wait()
            mine = self.at(k, p, t)
            def body(b, _):
                r = pl.ds(pl.multiple_of(b * 32, 32), 32)
                acc = mine[r, :].astype(F32) + g.tmp[slot, r, :].astype(F32)
                for land in lands: acc = acc + land[r, :].astype(F32)
                if out is None: mine[r, :] = acc.astype(BF16)
                else: out[pl.ds(pl.multiple_of(p * PART + b * 32, 32), 32), :] = acc
                return 0
            lax.fori_loop(0, PART // 32, body, 0, unroll=3)
            if send is not None: send()
        self.guard(cond, fn)

    def run(self):
        i = self.closed
        step = self.jobs[i][1]
        if step not in self.granted: self.grant_all()
        while self.opened < len(self.jobs) and self.opened < i + RING and self.jobs[self.opened][1] in self.started:
            self.open(self.opened)
            self.opened += 1
        self.close(i)
        self.closed += 1

    def finish(self, k, p, zt):
        g = self.g
        for f in (0, 1): self.to_second(k, p, zt, f).wait_send()
        self.to_first(k, p, zt).wait_send()
        @pl.when(g.z > zt)
        def _(): self.down(k, p, zt).wait_send()
        @pl.when(g.z < zt)
        def _(): self.up(k, p, zt, False).wait_send()


def reduce_vectors(g):
    Z, me, z = g.Z, g.me, g.z
    core = lax.rem(me, 2)
    bx, by = lax.rem(me // 2, 2), lax.rem(me // 4, 2)
    def cp(slot, dev):
        return pltpu.make_async_remote_copy(src_ref=g.vgrad, dst_ref=g.vland.at[slot], send_sem=g.vsem.at[0], recv_sem=g.vsem.at[1 + slot], device_id=(dev,), device_id_type=MESH)
    def take(slot):
        cp(slot, g.sib).wait_recv()
        g.vgrad[...] = g.vgrad[...] + g.vland[slot]
    def give(slot, dev): cp(slot, dev).start()
    on = core == 1
    right = jnp.logical_and(on, bx == 1)
    corner = jnp.logical_and(right, by == 1)
    def stage(giver, taker, slot, dev):
        def fn():
            @pl.when(giver)
            def _(): give(slot, dev)
            @pl.when(taker)
            def _(): take(slot)
        return fn
    stages = [stage(jnp.logical_not(on), on, 0, g.sib), stage(jnp.logical_and(on, bx == 0), right, 1, g.second),
              stage(jnp.logical_and(right, by == 0), corner, 2, g.first)]
    stages += [stage(jnp.logical_and(corner, z == h), jnp.logical_and(corner, z == h + 1), 3, me + 8) for h in range(Z - 1)]
    def finish():
        @pl.when(me != g.n - 1)
        def _(): cp(0, g.sib).wait_send()
    return stages, finish


def place_gradients(g):
    n, geo, me = g.n, g.geo, g.me
    prv = lax.rem(me + n - 1, n)
    edge = me == n - 1
    HL, HC = geo.HL, geo.HC
    skip = VBC - HL
    vectors = ((0, HL, HL), (VBC, HL + HC, HC - skip))
    def part(k):
        x, out, rows, drift = ((g.xlf, g.outl, geo.RL, geo.dl), (g.xcf, g.outc, geo.RC, geo.dc))[k]
        first, last = (0, HL) if k == 0 else (HL, HL + HC)
        cp = pltpu.make_async_remote_copy(src_ref=g.fs.at[pl.ds(first, last - first)], dst_ref=g.fr.at[pl.ds(first, last - first)],
                                          send_sem=g.hsem.at[2 + 2 * k], recv_sem=g.hsem.at[3 + 2 * k], device_id=(prv,), device_id_type=MESH)
        def begin():
            g.fs[first:last, :] = x[0:last - first, :]
            cp.start()
        split = (rows - 96) // 96 * 96
        def middle(): realign(out, 0, 0, split, x, drift * me)
        def end():
            cp.wait()
            lo, hi, count = vectors[k]
            x[rows:rows + count, :] = jnp.where(edge, g.vgrad[lo:hi, :], g.fr[first:first + count, :])
            realign(out, 0, split, out.shape[0], x, drift * me)
        return begin, middle, end
    return part(0), part(1)


PLANES = 4
LAYER_PARTS = 1
GATHER = (
    (1, 1, 0, 0), (1, 0, 0, 0), (1, 0, 0, -1), (3, 0, 0, 0), (2, 1, 0, 0), (2, 0, 0, 0), (1, 0, 0, 1), (4, 1, 0, 0), (1, 0, 0, 2), (3, 1, 0, 0),
    (1, 0, 0, -2), (2, 0, 0, -1), (3, 1, 0, 1), (4, 0, 0, 0), (2, 0, 0, 1), (4, 1, 0, -1), (3, 1, 0, -1), (1, 0, 0, 3), (4, 1, 0, 1), (2, 1, 0, 1),
    (3, 0, 0, -1), (1, 0, 0, -3), (1, 1, 0, 1), (5, 0, 0), (2, 1, 0, -1), (0, 0), (3, 0, 0, 1), (1, 1, 0, -1), (3, 0, 0, 2), (5, 1, 0), (2, 0, 0, -2),
    (4, 0, 0, -1), (5, 1, 1), (2, 0, 0, 2), (3, 1, 0, 2), (5, 1, -1), (3, 0, 0, -2), (2, 0, 0, -3), (3, 0, 0, -3), (3, 1, 0, -2), (4, 1, 0, -2),
    (4, 0, 0, 1), (2, 1, 0, 2), (1, 1, 0, 2), (4, 1, 0, 2), (5, 0, -1), (2, 0, 0, 3), (4, 0, 0, -2), (1, 1, 0, -2), (2, 1, 0, -2), (4, 0, 0, -3),
    (5, 0, 1), (5, 0, -2), (5, 0, -3), (0, 1), (0, 2), (0, 3), (4, 0, 0, 2), (5, 1, -2), (5, 1, 2), (0, 4), (2, 1, 0, -3), (3, 0, 0, 3), (4, 0, 0, 3),
    (0, 5), (5, 0, 2), (1, 1, 0, 3), (0, 6), (3, 1, 0, 3), (4, 1, 0, 3), (0, 7), (2, 1, 0, 3), (1, 1, 0, -3), (4, 1, 0, -3), (3, 1, 0, -3), (0, 8),
    (6, 0), (5, 0, 3), (0, 9), (6, 1), (5, 1, -3), (5, 1, 3), (0, 10),
)
SCATTER = (
    (1, 1, 0, 3, 0), (1, 1, 0, 2, 1), (1, 1, 0, 3, 1), (1, 1, 0, 0, 1), (1, 1, 0, 1, 1), (0, 0), (0, 1), (1, 0, 1, 3, 1), (1, 0, 0, 3, 1),
    (1, 0, 1, 3, 0), (1, 1, 0, 2, 0), (0, 2), (1, 1, 0, 1, 0), (2, 1, 0, 2, 0), (2, 1, 0, 1, 0), (0, 3), (0, 4), (2, 0, 0, 3, 0), (1, 1, 0, 0, 0),
    (0, 5), (1, 0, 0, 2, 0), (1, 0, 0, 2, 1), (1, 0, 2, 2, 0), (2, 1, 0, 3, 0), (0, 6), (2, 1, 0, 0, 0), (1, 0, 2, 2, 1), (3, 1, 0, 2, (0, True)),
    (3, 1, 0, 1, (0, True)), (0, 7), (1, 0, 0, 3, 0), (1, 0, 2, 3, 1), (2, 0, 0, 2, 0), (1, 0, 2, 3, 0), (0, 8), (3, 1, 0, 3, (0, True)), (0, 9),
    (1, 0, 1, 2, 1), (0, 10), (3, 1, 0, 2, (0, False)), (2, 0, 2, 2, 0), (3, 1, 0, 2, (1, True)), (3, 0, 0, 3, (0, True)), (2, 0, 1, 3, 0),
    (1, 0, 1, 2, 0), (2, 0, 2, 3, 0), (0, 11), (3, 0, 0, 3, (1, True)), (3, 1, 0, 0, (0, False)), (2, 0, 1, 2, 0), (0, 12), (1, 0, 0, 0, 1),
    (3, 0, 0, 3, (2, True)), (3, 0, 2, 2, (0, False)), (3, 0, 2, 3, (0, True)), (1, 0, 0, 0, 0), (4, 1, 0, 2, 0), (1, 0, 1, 1, 1),
    (3, 1, 0, 3, (1, True)), (3, 1, 0, 1, (0, False)), (1, 0, 2, 0, 1), (3, 0, 1, 2, (0, False)), (3, 0, 0, 2, (0, False)), (3, 1, 0, 0, (1, False)),
    (2, 0, 0, 0, 0), (3, 0, 0, 2, (0, True)), (3, 0, 1, 3, (0, True)), (3, 0, 2, 3, (1, True)), (1, 0, 1, 0, 1), (3, 0, 2, 2, (0, True)),
    (1, 0, 2, 0, 0), (3, 0, 1, 2, (0, True)), (0, 13), (3, 0, 0, 2, (1, True)), (2, 0, 2, 0, 0), (1, 0, 1, 0, 0), (3, 0, 0, 0, (0, False)),
    (3, 0, 1, 3, (1, True)), (3, 1, 0, 3, (2, True)), (3, 1, 0, 0, (2, False)), (1, 0, 0, 1, 1), (1, 0, 0, 1, 0), (3, 0, 0, 0, (2, False)),
    (3, 0, 2, 0, (0, False)), (3, 0, 1, 2, (1, True)), (3, 1, 0, 1, (1, False)), (3, 0, 0, 0, (1, False)), (2, 0, 1, 0, 0), (0, 14),
    (3, 0, 2, 3, (2, True)), (2, 0, 0, 1, 0), (1, 0, 2, 1, 1), (3, 0, 1, 0, (0, False)), (3, 0, 2, 0, (2, False)), (1, 0, 1, 1, 0), (4, 1, 0, 1, 0),
    (3, 0, 2, 2, (1, True)), (3, 0, 2, 0, (1, False)), (3, 0, 1, 3, (2, True)), (3, 0, 1, 0, (1, False)), (3, 0, 1, 0, (2, False)), (2, 0, 1, 1, 0),
    (0, 15), (3, 0, 0, 1, (0, False)), (4, 0, 2, 3, 0), (2, 0, 2, 1, 0), (3, 0, 1, 1, (0, True)), (1, 0, 2, 1, 0), (3, 0, 1, 1, (0, False)),
    (3, 0, 0, 1, (1, False)), (4, 0, 0, 3, 0), (3, 0, 0, 1, (0, True)), (0, 16), (4, 0, 0, 2, 0), (4, 1, 0, 3, 0), (4, 0, 1, 1, 0),
    (3, 0, 2, 1, (0, True)), (3, 0, 1, 1, (1, False)), (4, 0, 0, 1, 0), (3, 0, 2, 1, (0, False)), (3, 0, 2, 1, (1, False)), (4, 0, 1, 2, 0),
    (4, 0, 1, 0, 0), (4, 0, 2, 1, 0), (4, 0, 0, 0, 0), (4, 1, 0, 0, 0), (4, 0, 2, 2, 0), (4, 0, 1, 3, 0), (4, 0, 2, 0, 0),
)


def local_layout():
    return ((D, 3 * D), (D, D), (D, FF), (FF, D), (FF,)) + ((D,),) * 8


def conv_layout():
    return ((RATE * D, D), (D,), (D,), (D,))


def unpack(packed, layout):
    offset = 0
    pieces = []
    for extent in layout:
        length = math.prod(extent)
        pieces.append(packed[offset : offset + length].reshape(extent))
        offset = offset + length
    return pieces


def normalize_parts(values):
    average = jnp.mean(values, axis=-1, keepdims=True)
    centred = values - average
    spread = jnp.mean(centred * centred, axis=-1, keepdims=True)
    scaling = lax.rsqrt(spread + EPSILON)
    return (centred * scaling, scaling)


def normal_back(grad_normed, normed, scaling):
    first_mean = jnp.mean(grad_normed, axis=-1, keepdims=True)
    second_mean = jnp.mean(grad_normed * normed, axis=-1, keepdims=True)
    return scaling * (grad_normed - first_mean - normed * second_mean)


def product(left, right):
    return jnp.dot(left, right, preferred_element_type=jnp.float32)


def rows_inner(left, right):
    return lax.dot_general(
        left, right, (((0,), (0,)), ((), ())), preferred_element_type=jnp.float32
    )


def times_transpose(left, right):
    return lax.dot_general(
        left, right, (((1,), (1,)), ((), ())), preferred_element_type=jnp.float32
    )


def gelu_exact(values):
    return jax.nn.gelu(values, approximate=False)


def gelu_grad(values, upstream):
    return jax.vjp(gelu_exact, values)[1](upstream)[0]


def window_scores(projected, segments_block):
    row_count = projected.shape[0]
    windows = row_count // WINDOW
    heads_view = projected.reshape(windows, WINDOW, 3, HEADS, HEAD_SIZE)
    queries = heads_view[:, :, 0]
    keys_all = heads_view[:, :, 1]
    values = heads_view[:, :, 2]
    scores = jnp.einsum(
        "bqhe,bkhe->bhqk", queries, keys_all, preferred_element_type=jnp.float32
    ) * HEAD_SIZE ** (-0.5)
    grouped = segments_block.reshape(windows, WINDOW)
    allowed = grouped[:, None, :, None] == grouped[:, None, None, :]
    return (jnp.where(allowed, scores, -1e30), queries, keys_all, values)


def forward_pass(characters_block, segments_block, local_weights, conv_weights):
    (
        qkv_weight,
        out_weight,
        in_weight,
        down_weight,
        in_bias,
        gain_one,
        shift_one,
        query_bias,
        value_bias,
        out_bias,
        gain_two,
        shift_two,
        down_bias,
    ) = local_weights
    conv_weight, conv_bias, gain_three, shift_three = conv_weights
    row_count = characters_block.shape[0]
    inputs = characters_block.astype(jnp.float32)
    norm_one, scale_one = normalize_parts(inputs)
    normed = (norm_one * gain_one + shift_one).astype(jnp.bfloat16)
    proj_bias = jnp.concatenate([query_bias, jnp.zeros_like(query_bias), value_bias])
    projected = (product(normed, qkv_weight) + proj_bias).astype(jnp.bfloat16)
    scores, queries, keys_all, values = window_scores(projected, segments_block)
    largest = jnp.max(scores, axis=-1, keepdims=True)
    raised = jnp.exp(scores - largest)
    totals = jnp.sum(raised, axis=-1, keepdims=True)
    log_totals = largest + jnp.log(totals)
    weights = (raised / totals).astype(jnp.bfloat16)
    attended = jnp.einsum("bhqk,bkhe->bqhe", weights, values, preferred_element_type=jnp.float32)
    context = attended.reshape(row_count, D).astype(jnp.bfloat16)
    after_attention = inputs + product(context, out_weight) + out_bias
    norm_two, scale_two = normalize_parts(after_attention)
    middle = (norm_two * gain_two + shift_two).astype(jnp.bfloat16)
    pre_act = product(middle, in_weight) + in_bias
    hidden = gelu_exact(pre_act).astype(jnp.bfloat16)
    after_feed = after_attention + product(hidden, down_weight) + down_bias
    grouped_rows = after_feed.astype(jnp.bfloat16).reshape(row_count // RATE, RATE * D)
    conv_pre = product(grouped_rows, conv_weight) + conv_bias
    norm_three, scale_three = normalize_parts(gelu_exact(conv_pre))
    molecules = (norm_three * gain_three + shift_three).astype(jnp.bfloat16)
    saved_state = (
        segments_block,
        norm_one,
        scale_one,
        normed,
        projected,
        log_totals,
        context,
        norm_two,
        scale_two,
        middle,
        pre_act,
        hidden,
        grouped_rows,
        conv_pre,
        norm_three,
        scale_three,
    )
    return (molecules, saved_state)


def backward_pass(cotangent_block, saved_state, local_weights, conv_weights):
    (
        qkv_weight,
        out_weight,
        in_weight,
        down_weight,
        in_bias,
        gain_one,
        shift_one,
        query_bias,
        value_bias,
        out_bias,
        gain_two,
        shift_two,
        down_bias,
    ) = local_weights
    conv_weight, conv_bias, gain_three, shift_three = conv_weights
    (
        segments_block,
        norm_one,
        scale_one,
        normed,
        projected,
        log_totals,
        context,
        norm_two,
        scale_two,
        middle,
        pre_act,
        hidden,
        grouped_rows,
        conv_pre,
        norm_three,
        scale_three,
    ) = saved_state
    row_count = normed.shape[0]
    windows = row_count // WINDOW
    upstream = cotangent_block.astype(jnp.float32)
    grad_gain_three = jnp.sum(upstream * norm_three, axis=0)
    grad_shift_three = jnp.sum(upstream, axis=0)
    grad_activated = normal_back(upstream * gain_three, norm_three, scale_three)
    grad_conv_pre = gelu_grad(conv_pre, grad_activated).astype(jnp.bfloat16)
    grad_conv_bias = jnp.sum(grad_conv_pre.astype(jnp.float32), axis=0)
    grad_conv_weight = rows_inner(grouped_rows, grad_conv_pre)
    grad_feed = times_transpose(grad_conv_pre, conv_weight).reshape(row_count, D)
    grad_down_bias = jnp.sum(grad_feed, axis=0)
    grad_branch = grad_feed.astype(jnp.bfloat16)
    grad_down_weight = rows_inner(hidden, grad_branch)
    grad_hidden = times_transpose(grad_branch, down_weight)
    grad_pre = gelu_grad(pre_act, grad_hidden).astype(jnp.bfloat16)
    grad_in_bias = jnp.sum(grad_pre.astype(jnp.float32), axis=0)
    grad_in_weight = rows_inner(middle, grad_pre)
    grad_middle = times_transpose(grad_pre, in_weight)
    grad_gain_two = jnp.sum(grad_middle * norm_two, axis=0)
    grad_shift_two = jnp.sum(grad_middle, axis=0)
    grad_attention = grad_feed + normal_back(grad_middle * gain_two, norm_two, scale_two)
    grad_out_bias = jnp.sum(grad_attention, axis=0)
    grad_attn_out = grad_attention.astype(jnp.bfloat16)
    grad_out_weight = rows_inner(context, grad_attn_out)
    grad_context = times_transpose(grad_attn_out, out_weight).astype(jnp.bfloat16)
    grad_heads = grad_context.reshape(windows, WINDOW, HEADS, HEAD_SIZE)
    scores, queries, keys_all, values = window_scores(projected, segments_block)
    probs = jnp.exp(scores - log_totals)
    weights = probs.astype(jnp.bfloat16)
    grad_weights = jnp.einsum(
        "bqhe,bkhe->bhqk", grad_heads, values, preferred_element_type=jnp.float32
    )
    row_terms = jnp.sum(probs * grad_weights, axis=-1, keepdims=True)
    grad_scores = (probs * (grad_weights - row_terms)).astype(jnp.bfloat16)
    grad_queries = jnp.einsum(
        "bhqk,bkhe->bqhe", grad_scores, keys_all, preferred_element_type=jnp.float32
    ) * HEAD_SIZE ** (-0.5)
    grad_keys = jnp.einsum(
        "bhqk,bqhe->bkhe", grad_scores, queries, preferred_element_type=jnp.float32
    ) * HEAD_SIZE ** (-0.5)
    grad_values = jnp.einsum(
        "bhqk,bqhe->bkhe", weights, grad_heads, preferred_element_type=jnp.float32
    )
    grad_proj = (
        jnp.stack([grad_queries, grad_keys, grad_values], axis=2)
        .reshape(row_count, 3 * D)
        .astype(jnp.bfloat16)
    )
    proj_sums = jnp.sum(grad_proj.astype(jnp.float32), axis=0)
    grad_query_bias = proj_sums[:D]
    grad_value_bias = proj_sums[2 * D :]
    grad_qkv_weight = rows_inner(normed, grad_proj)
    grad_normed = times_transpose(grad_proj, qkv_weight)
    grad_gain_one = jnp.sum(grad_normed * norm_one, axis=0)
    grad_shift_one = jnp.sum(grad_normed, axis=0)
    grad_inputs = grad_attention + normal_back(grad_normed * gain_one, norm_one, scale_one)
    local_grad = jnp.concatenate(
        [
            grad_qkv_weight.reshape(-1),
            grad_out_weight.reshape(-1),
            grad_in_weight.reshape(-1),
            grad_down_weight.reshape(-1),
            grad_in_bias,
            grad_gain_one,
            grad_shift_one,
            grad_query_bias,
            grad_value_bias,
            grad_out_bias,
            grad_gain_two,
            grad_shift_two,
            grad_down_bias,
        ]
    )
    conv_grad = jnp.concatenate(
        [grad_conv_weight.reshape(-1), grad_conv_bias, grad_gain_three, grad_shift_three]
    )
    return (grad_inputs, local_grad, conv_grad)


def plain_device(characters, segment_ids, cotangent, local_params, conv_params):
    devices = lax.axis_size("fsdp")
    local_shard = local_params.shape[0]
    conv_shard = conv_params.shape[0]
    local_pad = local_shard * devices - LOCAL_COUNT
    conv_pad = conv_shard * devices - CONV_COUNT
    local_total = jnp.zeros((1, local_shard), jnp.float32)
    conv_total = jnp.zeros((1, conv_shard), jnp.float32)
    molecule_list = []
    gradient_list = []
    for micro_index in range(MICRO):
        local_full, conv_full = (
            lax.all_gather(local_params, "fsdp", axis=0, tiled=True),
            lax.all_gather(conv_params, "fsdp", axis=0, tiled=True),
        )
        molecules, saved_state = forward_pass(
            characters[micro_index],
            segment_ids[micro_index],
            unpack(local_full, local_layout()),
            unpack(conv_full, conv_layout()),
        )
        local_full, conv_full = (
            lax.all_gather(local_params, "fsdp", axis=0, tiled=True),
            lax.all_gather(conv_params, "fsdp", axis=0, tiled=True),
        )
        grad_inputs, local_grad, conv_grad = backward_pass(
            cotangent[micro_index],
            saved_state,
            unpack(local_full, local_layout()),
            unpack(conv_full, conv_layout()),
        )
        local_table = jnp.concatenate([local_grad, jnp.zeros((local_pad,), jnp.float32)]).reshape(
            devices, local_shard
        )
        conv_table = jnp.concatenate([conv_grad, jnp.zeros((conv_pad,), jnp.float32)]).reshape(
            devices, conv_shard
        )
        local_part, conv_part = (
            lax.psum_scatter(local_table, "fsdp", scatter_dimension=0, tiled=True),
            lax.psum_scatter(conv_table, "fsdp", scatter_dimension=0, tiled=True),
        )
        local_total = local_total + local_part
        conv_total = conv_total + conv_part
        molecule_list.append(molecules)
        gradient_list.append(grad_inputs)
    return (
        jnp.stack(molecule_list),
        jnp.stack(gradient_list),
        local_total.reshape(-1),
        conv_total.reshape(-1),
    )


VECTOR_AT = (88, 96, 104, 112, 120)
FINISH_SPAN = 24


def fused_kernel(geo, rows, in_names, out_names, scratch_names, *refs):
    n_in, n_out = len(in_names), len(out_names)
    every = dict(zip(list(in_names) + list(out_names) + list(scratch_names), refs))
    me, core, z, sib, first, second = where_am_i()
    g = SimpleNamespace(n=geo.n, Z=geo.Z, geo=geo, me=me, core=core, z=z, sib=sib, first=first, second=second, rows=rows, mols=rows // RATE, **every)
    g.from_sib = (every["from_sib_l"], every["from_sib_c"])
    program(g)


def program(g):
    Z = g.Z
    start_gather(g)
    ag = Gather(g, (LAYER_PARTS, 1))
    own = [e for e in GATHER if e[0] == 1 and e[1] == 0 and e[3] == 0]
    for e in own: ag.event(*e)
    table = gather_table(g)
    forward = [
        lambda: (same_segment(g), forward_norm(g)), lambda: forward_qkv(g, 0, 6), lambda: forward_qkv(g, 6, 9),
        lambda: forward_attention(g, 0, 12), lambda: forward_attention(g, 12, 24), lambda: forward_out(g),
        lambda: forward_up(g, 0, 4), lambda: forward_up(g, 4, 8), lambda: forward_up(g, 8, 12), lambda: forward_down(g), lambda: forward_conv(g)]
    for e in GATHER:
        if e[0] == 0: forward[e[1]]()
        elif e[0] == 5: ag.convert(*e[1:])
        elif e[0] == 6:
            for d in GATHER:
                if 1 <= d[0] <= 4 and d[1] == e[1]: ag.drain(*d)
        elif e not in own: ag.event(*e)
    table()
    NL, NC = g.geo.RL // PART, g.geo.RC // PART
    conv_steps = [(1, p, zt) for zt in reversed(range(Z)) for p in range(NC)]
    layer_steps = [(0, p, zt) for zt in reversed(range(Z)) for p in range(NL)]
    names = {1: "second", 2: "first", 3: "line", 4: "last"}
    jobs = [(names[e[0]], e[1:4], e[4]) for e in SCATTER if e[0]]
    sc = Scatter(g, jobs)
    for zt in reversed(range(Z)):
        grad_conv_weight(g, zt)
        for st in conv_steps:
            if st[2] == zt: sc.p0(*st)
    def send_planes(lo, hi):
        sc.grant_all()
        for st in layer_steps:
            if lo <= st[2] < hi: sc.p0(*st)
    vec_stages, vec_finish = reduce_vectors(g)
    plane = 8 * g.geo.RL
    def plane_of(row): return -(-row // plane)
    q3, q2, q1 = plane_of(W2_ROW), plane_of(W1_ROW), plane_of(O_ROW)
    backward = [
        lambda: (back_conv(g), grad_down_weight(g, 0, 6)),
        lambda: (grad_down_weight(g, 6, 12), send_planes(q3, Z)),
        lambda: back_down(g, 0, 6),
        lambda: back_down(g, 6, 12),
        lambda: grad_up_weight(g, 0, 3),
        lambda: (grad_up_weight(g, 3, 6), send_planes(q2, q3)),
        lambda: back_up(g),
        lambda: (grad_out_weight(g), send_planes(q1, q2), back_out(g)),
        lambda: back_attention(g, 0, 1),
        lambda: back_attention(g, 1, 2),
        lambda: back_attention(g, 2, 3),
        lambda: back_attention(g, 3, 4),
        lambda: (grad_qkv_weight(g), send_planes(0, q1)),
        lambda: (back_qkv(g), pltpu.make_async_copy(g.dc, g.cg, g.osem.at[0]).start(), vec_stages[0]()),
        lambda: 0,
        lambda: 0,
        lambda: 0,
    ]
    late = dict(zip(VECTOR_AT, vec_stages[1:]))
    layer, conv = place_gradients(g)
    early = {max(i for i, e in enumerate(SCATTER) if e[:3] == (4, 0, 0)): layer[0], max(i for i, e in enumerate(SCATTER) if e[:2] == (4, 1)): conv[0]}
    sent = {}
    for i, e in enumerate(SCATTER):
        if 1 <= e[0] <= 3: sent[e[1:4]] = i
    open_steps = sorted(conv_steps + layer_steps, key=lambda st: sent[st])
    for i, e in enumerate(SCATTER):
        if e[0] == 0: backward[e[1]]()
        else: sc.run()
        if i >= len(SCATTER) - FINISH_SPAN and open_steps and sent[open_steps[0]] < i - 12: sc.finish(*open_steps.pop(0))
        if i in late: late[i]()
        if i in early: early[i]()
    layer[1]()
    conv[1]()
    vec_finish()
    for st in open_steps: sc.finish(*st)
    layer[2]()
    conv[2]()
    pltpu.make_async_copy(g.dc, g.cg, g.osem.at[0]).wait()


def fused(n, characters, segment_ids, cotangent, local_params, conv_params):
    geo = Geo(n, local_params.shape[0], conv_params.shape[0])
    micro, span, _ = characters.shape
    rows = micro * span
    x = characters.reshape(rows, D)
    cot = cotangent.reshape(rows // RATE, D)
    xl = jnp.pad(local_params, (0, geo.XL * LANE - local_params.shape[0])).reshape(geo.XL, LANE)
    xc = jnp.pad(conv_params, (0, geo.XC * LANE - conv_params.shape[0])).reshape(geo.XC, LANE)
    V = pl.BlockSpec(memory_space=pltpu.VMEM)
    A = pl.BlockSpec(memory_space=pl.ANY)
    S = jax.ShapeDtypeStruct
    Z, H = geo.Z, geo.HL + geo.HC
    ins = dict(x=x, seg=segment_ids, cot=cot, xl=xl, xc=xc)
    outs = dict(mol=(V, S((rows // RATE, D), BF16)), cg=(A, S((rows, D), F32)), outl=(V, S((-(-geo.XL // 96) * 96, LANE), F32)), outc=(V, S((-(-geo.XC // 96) * 96, LANE), F32)))
    for name, count in (("from_sib", n // 2),):
        outs[name + "_l"] = (A, S((count * geo.RL, LANE), BF16))
        outs[name + "_c"] = (A, S((count * geo.RC, LANE), BF16))
    W = pltpu.VMEM
    DMA = pltpu.SemaphoreType.DMA
    sc = state_shapes(rows)
    sc.update(wqkv=W((D, 3 * D), BF16), wo=W((D, D), BF16), w1=W((D, FF), BF16), w2=W((FF, D), BF16), wc=W((FF, D), BF16))
    sc.update(gl=W((n * geo.RL, LANE), BF16), gc=W((n * geo.RC, LANE), BF16), hb=W((H, LANE), BF16), hr=W((H, LANE), BF16), tail=W((H, LANE), BF16),
              xlf=W((geo.HL + -(-geo.XL // 96) * 96 + 32, LANE), F32), xcf=W((geo.HC + -(-geo.XC // 96) * 96 + 32, LANE), F32), vgrad=W((H, LANE), F32), vland=W((4, H, LANE), F32),
              fs=W((H, LANE), F32), fr=W((H, LANE), F32), tmp=W((RING, PART, LANE), BF16), below_l=W((geo.RL, LANE), BF16), below_c=W((geo.RC, LANE), BF16))
    parts = (geo.RL + geo.RC) // PART
    sc.update(rsem=DMA((LAYER_PARTS + 1, n)), ssem=DMA((LAYER_PARTS + 1, 13 * Z)), hsem=DMA((6,)), tsem=DMA((5,)), osem=DMA((1,)), vsem=DMA((5,)), fsem=DMA((RING,)), credit=pltpu.SemaphoreType.REGULAR((4, (geo.RL + geo.RC) // PART * Z)),
              r_sib=DMA((parts, Z)), s_sib=DMA((parts, Z)), r_second=DMA((parts, 2 * Z)), s_second=DMA((parts, 2 * Z)),
              r_first=DMA((parts, Z)), s_first=DMA((parts, Z)), r_up=DMA((parts, Z)), s_up=DMA((parts, Z)), r_down=DMA((parts, Z)), s_down=DMA((parts, Z)))
    res = pl.pallas_call(
        functools.partial(fused_kernel, geo, rows, list(ins), list(outs), list(sc)),
        out_shape=[s for _, s in outs.values()],
        in_specs=[V] * len(ins),
        out_specs=[b for b, _ in outs.values()],
        scratch_shapes=list(sc.values()),
        compiler_params=pltpu.CompilerParams(collective_id=0, has_side_effects=True, vmem_limit_bytes=64 << 20),
        name="layer",
    )(*ins.values())
    mol, cg, outl, outc = res[:4]
    return (mol.reshape(micro, span // RATE, D), cg.reshape(micro, span, D), outl.reshape(-1)[:local_params.shape[0]], outc.reshape(-1)[:conv_params.shape[0]])


def on_device(characters, segment_ids, cotangent, local_params, conv_params):
    n = lax.axis_size("fsdp")
    rows = characters.shape[0] * characters.shape[1]
    whole = n // 8 == PLANES and n % 8 == 0 and (2 * 72 * D) % (n * UNIT) == 0 and (2 * 24 * D) % (n * UNIT) == 0
    exact = local_params.shape[0] * n == LOCAL_COUNT and conv_params.shape[0] * n == CONV_COUNT
    if whole and exact and rows == 4 * WINDOW:
        return fused(n, characters, segment_ids, cotangent, local_params, conv_params)
    return plain_device(characters, segment_ids, cotangent, local_params, conv_params)


def solution(mesh):
    return jax.shard_map(
        on_device,
        mesh=mesh,
        in_specs=(P(None, "fsdp", None), P(None, "fsdp"), P(None, "fsdp", None), P("fsdp"), P("fsdp")),
        out_specs=(P(None, "fsdp", None), P(None, "fsdp", None), P("fsdp"), P("fsdp")),
        check_vma=False,
    )
```

```python
import functools
import math
from types import SimpleNamespace

import jax
import jax.numpy as jnp
from jax import lax
from jax.experimental import pallas as pl
from jax.experimental.pallas import tpu as pltpu
from jax.sharding import PartitionSpec as P

MESH = pl.DeviceIdType.MESH
F32, BF16 = jnp.float32, jnp.bfloat16
D, FF, HEADS, WINDOW, RATE, MICRO, HEAD_SIZE = 768, 3072, 12, 128, 4, 2, 64
LOCAL_COUNT, CONV_COUNT = 7087104, 2361600
LANE = 128
UNIT = 1152
EPS = EPSILON = 1e-05


DC = D // LANE
FC = FF // LANE
VB1, VG1, VS1, VBQ, VBV, VBO, VG2, VS2, VB2 = 0, 24, 30, 36, 42, 48, 54, 60, 66
VBC, VG3, VS3 = 78, 84, 90
QKV_ROW, O_ROW, W1_ROW, W2_ROW = 0, 18 * D, 24 * D, 48 * D

def nn(a, b): return jnp.dot(a, b, preferred_element_type=F32)
def nt(a, b): return lax.dot_general(a, b, (((1,), (1,)), ((), ())), preferred_element_type=F32)
def tn(a, b): return lax.dot_general(a, b, (((0,), (0,)), ((), ())), preferred_element_type=F32)

def loop(n, fn, unroll=1):
    def body(i, _):
        fn(i)
        return 0
    lax.fori_loop(0, n, body, 0, unroll=unroll)

def span(lo, hi, n, fn, unroll=1):
    hi = n if hi is None else hi
    def body(i, _):
        fn(i)
        return 0
    lax.fori_loop(lo, hi, body, 0, unroll=unroll)

def at(i, size): return pl.ds(pl.multiple_of(i * size, size), size)

def vec(r, row, blocks=DC):
    return jnp.concatenate([r.vecs[row + i:row + i + 1, :] for i in range(blocks)], axis=1)

def put(r, row, value):
    for i in range(value.shape[1] // LANE):
        r.vgrad[row + i:row + i + 1, :] = value[:, i * LANE:(i + 1) * LANE]

def add_to(r, row, value):
    for i in range(value.shape[1] // LANE):
        r.vgrad[row + i:row + i + 1, :] += value[:, i * LANE:(i + 1) * LANE]

def normal(v):
    mean = jnp.mean(v, axis=-1, keepdims=True)
    cen = v - mean
    var = jnp.mean(cen * cen, axis=-1, keepdims=True)
    s = lax.rsqrt(var + EPS)
    return cen * s, s

def normal_back(dn, nrm, s):
    return s * (dn - jnp.mean(dn, axis=-1, keepdims=True) - nrm * jnp.mean(dn * nrm, axis=-1, keepdims=True))

def colsum(v): return jnp.sum(v, axis=0, keepdims=True)

def gelu_both(h):
    cdf = 0.5 + 0.5 * lax.erf(h * (0.5 ** 0.5))
    pdf = jnp.exp(-0.5 * h * h) * (1.0 / math.sqrt(2 * math.pi))
    return h * cdf, cdf + h * pdf

RB = 64
def forward_norm(r):
    g1, s1 = vec(r, VG1), vec(r, VS1)
    def f(i):
        nrm, _ = normal(r.x[at(i, RB), :].astype(F32))
        r.a[at(i, RB), :] = (nrm * g1 + s1).astype(BF16)
    loop(r.rows // RB, f, 2)

def forward_qkv(r, lo=0, hi=9):
    bias = jnp.concatenate([vec(r, VBQ), jnp.zeros((1, D), F32), vec(r, VBV)], axis=1)
    for i in range(18):
        r.bias[i:i + 1, :] = bias[:, i * LANE:(i + 1) * LANE]
    def f(i):
        b = jnp.concatenate([r.bias[pl.ds(2 * i, 1), :], r.bias[pl.ds(2 * i + 1, 1), :]], axis=1)
        r.P[:, at(i, 256)] = (nn(r.a[...], r.wqkv[:, at(i, 256)]) + b).astype(BF16)
    span(lo, hi, 9, f, 3)

def halves(v):
    lo = lax.broadcasted_iota(jnp.int32, v.shape, 1) < 64
    w = v.astype(F32)
    z = jnp.zeros_like(w)
    return jnp.concatenate([jnp.where(lo, w, z), jnp.where(lo, z, w)], axis=0).astype(BF16)

def pick(v):
    lo = lax.broadcasted_iota(jnp.int32, (WINDOW, LANE), 1) < 64
    return jnp.where(lo, v[:WINDOW], v[WINDOW:])

def heads_of(r, i):
    w = i // DC
    hp = lax.rem(i, DC)
    rows = at(w, WINDOW)
    return w, rows, at(hp, LANE), at(hp + DC, LANE), at(hp + 2 * DC, LANE)

def same_segment(r):
    per = r.seg.shape[1] // WINDOW
    for w in range(r.rows // WINDOW):
        ids = r.seg[w // per:w // per + 1, w % per * WINDOW:(w % per + 1) * WINDOW].astype(F32)
        wide = jnp.broadcast_to(ids, (WINDOW, WINDOW))
        r.same[w] = (wide == wide.T).astype(F32)

def forward_attention(r, lo=0, hi=24):
    def f(i):
        w, rows, cq, ck, cv = heads_of(r, i)
        q2 = halves(r.P[rows, cq])
        s = nt(q2, r.P[rows, ck]) * 0.125
        same = r.same[w]
        same2 = jnp.concatenate([same, same], axis=0) > 0.5
        s = jnp.where(same2, s, -1e30)
        e = jnp.exp(s - jnp.max(s, axis=-1, keepdims=True))
        p = (e / jnp.sum(e, axis=-1, keepdims=True)).astype(BF16)
        r.p[i] = p
        r.ctx[rows, cq] = pick(nn(p, r.P[rows, cv])).astype(BF16)
    span(lo, hi, 24, f, 6)

def forward_out(r):
    bo = vec(r, VBO)
    for i in range(3):
        c = slice(i * 256, (i + 1) * 256)
        r.y1[:, c] = r.x[:, c].astype(F32) + nn(r.ctx[...], r.wo[:, c]) + bo[:, c]
    g2, s2 = vec(r, VG2), vec(r, VS2)
    def f(i):
        nrm, _ = normal(r.y1[at(i, RB), :])
        r.c[at(i, RB), :] = (nrm * g2 + s2).astype(BF16)
    loop(r.rows // RB, f, 2)

def forward_up(r, lo=0, hi=12):
    def f(i):
        b = jnp.concatenate([r.vecs[pl.ds(VB1 + 2 * i, 1), :], r.vecs[pl.ds(VB1 + 2 * i + 1, 1), :]], axis=1)
        h = nn(r.c[...], r.w1[:, at(i, 256)]) + b
        hid, slope = gelu_both(h)
        r.hid[:, at(i, 256)] = hid.astype(BF16)
        r.slope[:, at(i, 256)] = slope.astype(BF16)
    span(lo, hi, 12, f, 4)

def forward_down(r):
    b2 = vec(r, VB2)
    for i in range(3):
        c = slice(i * 256, (i + 1) * 256)
        v = r.y1[:, c] + nn(r.hid[...], r.w2[:, c]) + b2[:, c]
        r.ys[2 * i] = v[:, :LANE]
        r.ys[2 * i + 1] = v[:, LANE:]
    for j in range(RATE):
        for c in range(DC):
            r.u[j * r.mols:(j + 1) * r.mols, c * LANE:(c + 1) * LANE] = r.ys[c, pl.ds(j, r.mols, stride=RATE), :].astype(BF16)

def forward_conv(r):
    z = vec(r, VBC)
    for j in range(RATE):
        z = z + nn(r.u[j * r.mols:(j + 1) * r.mols, :], r.wc[j * D:(j + 1) * D, :])
    w, slope = gelu_both(z)
    nrm, s = normal(w)
    r.mol[...] = (nrm * vec(r, VG3) + vec(r, VS3)).astype(BF16)
    t = r.cot[...].astype(F32)
    put(r, VG3, colsum(t * nrm))
    put(r, VS3, colsum(t))
    dw = normal_back(t * vec(r, VG3), nrm, s)
    dz = (dw * slope).astype(BF16)
    r.dz[...] = dz
    put(r, VBC, colsum(dz.astype(F32)))

def emit_flat(r, dst, row0, tile, base=0):
    k, m = tile.shape[0], tile.shape[1] // LANE
    for c in range(m):
        r.scr[pl.ds(base + c, k, stride=m), :] = tile[:, c * LANE:(c + 1) * LANE]
    dst[pl.ds(pl.multiple_of(row0, 16), k * m), :] = r.scr[base:base + k * m, :].astype(BF16)

def emit_pair(r, dst, row0, lhs, rhs):
    tiles = [tn(lhs(h), rhs) for h in (0, 1)]
    for h in (0, 1): emit_flat(r, dst, row0 + h * 256 * DC, tiles[h], h * 256 * DC)

def grad_conv_weight(r, j):
    for i in range(3):
        emit_flat(r, r.gc, (j * D + i * 256) * DC, tn(r.u[j * r.mols:(j + 1) * r.mols, i * 256:(i + 1) * 256], r.dz[...]), i % 2 * 256 * DC)

def back_conv(r):
    for j in range(RATE):
        v = nt(r.dz[...], r.wc[j * D:(j + 1) * D, :])
        for c in range(DC):
            r.ys[c, pl.ds(j, r.mols, stride=RATE), :] = v[:, c * LANE:(c + 1) * LANE]
    for c in range(DC):
        v = r.ys[c]
        r.u[:, c * LANE:(c + 1) * LANE] = v.astype(BF16)
        put(r, VB2 + c, colsum(v))

def grad_down_weight(r, lo=0, hi=12):
    span(lo // 2, hi // 2, 6, lambda i: emit_pair(r, r.gl, W2_ROW + i * 512 * DC, lambda h: r.hid[:, pl.ds(pl.multiple_of(i * 512 + h * 256, 256), 256)], r.u[...]))

def back_down(r, lo=0, hi=12):
    def f(i):
        cols = [at(2 * i + h, 256) for h in (0, 1)]
        slopes = [r.slope[:, c] for c in cols]
        outs = [(nt(r.u[...], r.w2[c, :]) * s.astype(F32)).astype(BF16) for c, s in zip(cols, slopes)]
        for h, (c, dh) in enumerate(zip(cols, outs)):
            r.slope[:, c] = dh
            s = colsum(dh.astype(F32))
            r.vgrad[pl.ds(VB1 + 4 * i + 2 * h, 1), :] = s[:, :LANE]
            r.vgrad[pl.ds(VB1 + 4 * i + 2 * h + 1, 1), :] = s[:, LANE:]
    span(lo // 2, hi // 2, 6, f)

def grad_up_weight(r, lo=0, hi=6):
    span(lo, hi, 6, lambda i: emit_flat(r, r.gl, W1_ROW + i * 128 * FC, tn(r.c[:, at(i, 128)], r.slope[...])))

def fold(v):
    out = v[0:8]
    for i in range(1, v.shape[0] // 8):
        out = out + v[i * 8:(i + 1) * 8]
    return out

def row_sums(r, fn, count):
    def body(i, acc):
        return tuple(a + fold(v) for a, v in zip(acc, fn(at(i, RB))))
    acc = lax.fori_loop(0, r.rows // RB, body, tuple(jnp.zeros((8, D), F32) for _ in range(count)), unroll=2)
    return [colsum(a) for a in acc]

def back_up(r):
    for i in range(3):
        r.dc[:, i * 256:(i + 1) * 256] = nt(r.slope[...], r.w1[i * 256:(i + 1) * 256, :])
    g2 = vec(r, VG2)
    def f(rows):
        dc = r.dc[rows, :]
        nrm, s = normal(r.y1[rows, :])
        dy2 = jnp.concatenate([r.ys[c, rows, :] for c in range(DC)], axis=1)
        dy1 = dy2 + normal_back(dc * g2, nrm, s)
        r.dc[rows, :] = dy1
        r.u[rows, :] = dy1.astype(BF16)
        return dc * nrm, dc, dy1
    sums = row_sums(r, f, 3)
    put(r, VG2, sums[0])
    put(r, VS2, sums[1])
    put(r, VBO, sums[2])

def grad_out_weight(r):
    for i in range(3):
        emit_flat(r, r.gl, O_ROW + i * 256 * DC, tn(r.ctx[:, i * 256:(i + 1) * 256], r.u[...]), i % 2 * 256 * DC)

def back_out(r):
    for i in range(3):
        r.c[:, i * 256:(i + 1) * 256] = nt(r.u[...], r.wo[i * 256:(i + 1) * 256, :]).astype(BF16)

AG = 6
def back_attention(r, lo=0, hi=None):
    def f(i):
        where = [heads_of(r, i * AG + j) for j in range(AG)]
        loads = [(r.c[rows, cq], r.P[rows, cq], r.P[rows, ck], r.P[rows, cv], r.p[i * AG + j]) for j, (w, rows, cq, ck, cv) in enumerate(where)]
        outs = []
        for do, q, k, v, pb in loads:
            do2, q2 = halves(do), halves(q)
            p = pb.astype(F32)
            dp = nt(do2, v)
            ds = (p * (dp - jnp.sum(p * dp, axis=-1, keepdims=True))).astype(BF16)
            outs.append((pick(nn(ds, k)) * 0.125, tn(ds, q2) * 0.125, tn(pb, do2)))
        for (w, rows, cq, ck, cv), (dq, dk, dv) in zip(where, outs):
            r.P[rows, cq] = dq.astype(BF16)
            r.P[rows, ck] = dk.astype(BF16)
            r.P[rows, cv] = dv.astype(BF16)
    span(lo, hi, r.rows // WINDOW * DC // AG, f)

def grad_qkv_weight(r):
    for c in range(DC):
        r.vgrad[VBQ + c:VBQ + c + 1, :] = colsum(r.P[:, c * LANE:(c + 1) * LANE].astype(F32))
        r.vgrad[VBV + c:VBV + c + 1, :] = colsum(r.P[:, 2 * D + c * LANE:2 * D + (c + 1) * LANE].astype(F32))
    loop(6, lambda i: emit_flat(r, r.gl, QKV_ROW + i * 128 * 18, tn(r.a[:, at(i, 128)], r.P[...])))

def back_qkv(r):
    for i in range(3):
        r.y1[:, i * 256:(i + 1) * 256] = nt(r.P[...], r.wqkv[i * 256:(i + 1) * 256, :])
    g1 = vec(r, VG1)
    def f(rows):
        da = r.y1[rows, :]
        nrm, s = normal(r.x[rows, :].astype(F32))
        r.dc[rows, :] = r.dc[rows, :] + normal_back(da * g1, nrm, s)
        return da * nrm, da
    sums = row_sums(r, f, 2)
    put(r, VG1, sums[0])
    put(r, VS1, sums[1])

def state_shapes(rows):
    mols = rows // RATE
    V = pltpu.VMEM
    return dict(
        same=V((rows // WINDOW, WINDOW, WINDOW), F32), a=V((rows, D), BF16), P=V((rows, 3 * D), BF16), p=V((rows // WINDOW * DC, 2 * WINDOW, LANE), BF16),
        ctx=V((rows, D), BF16), y1=V((rows, D), F32), c=V((rows, D), BF16), slope=V((rows, FF), BF16), hid=V((rows, FF), BF16),
        ys=V((DC, rows, LANE), F32), u=V((rows, D), BF16), dz=V((mols, D), BF16), dc=V((rows, D), F32),
        scr=V((128 * FC, LANE), F32), bias=V((24, LANE), F32), vecs=V((96, LANE), F32))


class Geo:
    def __init__(self, n, local_shard, conv_shard):
        self.n = n
        self.local_shard, self.conv_shard = local_shard, conv_shard
        self.Z = n // 8
        self.RL = (12 * D * D) // LANE // n
        self.RC = (4 * D * D) // LANE // n
        self.dl = local_shard - self.RL * LANE
        self.dc = conv_shard - self.RC * LANE
        self.HL = -(-(self.dl * n) // (8 * LANE)) * 8
        self.HC = -(-(self.dc * n) // (8 * LANE)) * 8
        self.XL = -(-local_shard // (8 * LANE)) * 8
        self.XC = -(-conv_shard // (8 * LANE)) * 8

def where_am_i():
    me = lax.axis_index("fsdp")
    core = lax.rem(me, 2)
    bx = lax.rem(me // 2, 2)
    by = lax.rem(me // 4, 2)
    z = me // 8
    sib = me + 1 - 2 * core
    xn = me + 2 - 4 * bx
    yn = me + 4 - 8 * by
    first = xn + core * (yn - xn)
    second = yn + core * (xn - yn)
    return me, core, z, sib, first, second

def realign(out_ref, out_base, lo, hi, x_ref, shift, step=16):
    q = shift // LANE
    r = lax.rem(shift, LANE)
    turn = lax.rem(LANE - r, LANE)
    lane = lax.broadcasted_iota(jnp.int32, (step, LANE), 1)
    keep = lane < (LANE - r)
    def body(i, _):
        low = x_ref[pl.ds(q + i * step, step), :]
        high = x_ref[pl.ds(q + i * step + 1, step), :]
        val = jnp.where(keep, pltpu.roll(low, turn, 1), pltpu.roll(high, turn, 1))
        out_ref[pl.ds(pl.multiple_of(out_base + i * step, step), step), :] = val.astype(out_ref.dtype)
        return 0
    many = max(u for u in (1, 2, 3, 4, 5, 6, 8) if (hi - lo) // step % u == 0)
    lax.fori_loop(lo // step, hi // step, body, 0, unroll=many)

def widen(dst_ref, dst_base, src_ref, rows):
    step = 248 if rows % 248 == 0 else 8
    for i in range(rows // step):
        dst_ref[dst_base + i * step:dst_base + (i + 1) * step, :] = src_ref[i * step:(i + 1) * step, :].astype(F32)

def convert_unit(src_ref, base, w_ref, krow, cols, scr):
    groups = UNIT // (16 * cols)
    def body(g, _):
        scr[0:16 * cols, :] = src_ref[pl.ds(pl.multiple_of(base + g * 16 * cols, 16), 16 * cols), :].astype(F32)
        for cc in range(cols):
            v = scr[pl.ds(cc, 16, stride=cols), :]
            w_ref[pl.ds(pl.multiple_of(krow + g * 16, 16), 16), cc * LANE:(cc + 1) * LANE] = v.astype(BF16)
        return 0
    lax.fori_loop(0, groups, body, 0)


def start_gather(g):
    n, Z, geo, me, z = g.n, g.Z, g.geo, g.me, g.z
    RL, RC = geo.RL, geo.RC
    nxt = lax.rem(me + 1, n)
    bar = pltpu.get_barrier_semaphore()
    far = lax.rem(me + n + 2 * g.core - 1, n)
    for dev in (g.sib, g.first, g.second, far):
        pl.semaphore_signal(bar, inc=1, device_id=(dev,), device_id_type=MESH)
    @pl.when(z > 0)
    def _(): pl.semaphore_signal(bar, inc=1, device_id=(me - 8,), device_id_type=MESH)
    @pl.when(z < Z - 1)
    def _(): pl.semaphore_signal(bar, inc=1, device_id=(me + 8,), device_id_type=MESH)
    widen(g.xlf, geo.HL, g.xl, geo.XL)
    widen(g.xcf, geo.HC, g.xc, geo.XC)
    realign(g.fs, 0, 0, geo.HL, g.xlf, geo.local_shard, 8)
    realign(g.fs, geo.HL, 0, geo.HC, g.xcf, geo.conv_shard, 8)
    g.hb[...] = g.fs[...].astype(BF16)
    HA, HB = 96, 96
    lshift, cshift = geo.HL * LANE - geo.dl * me, geo.HC * LANE - geo.dc * me
    realign(g.gl, me * RL, HA, RL, g.xlf, lshift)
    realign(g.gc, me * RC, HB, RC, g.xcf, cshift)
    pl.semaphore_wait(bar, 4 + jnp.where(z > 0, 1, 0) + jnp.where(z < Z - 1, 1, 0))
    halo = pltpu.make_async_remote_copy(src_ref=g.hb, dst_ref=g.hr, send_sem=g.hsem.at[0], recv_sem=g.hsem.at[1], device_id=(nxt,), device_id_type=MESH)
    halo.start()
    halo.wait()
    g.xlf[0:geo.HL, :] = g.hr[0:geo.HL, :].astype(F32)
    g.xcf[0:geo.HC, :] = g.hr[geo.HL:geo.HL + geo.HC, :].astype(F32)
    realign(g.gl, me * RL, 0, HA, g.xlf, lshift)
    realign(g.gc, me * RC, 0, HB, g.xcf, cshift)
    @pl.when(me == n - 1)
    def _():
        g.tail[...] = g.hb[...]


def gather_table(g):
    Z, me, z = g.Z, g.me, g.z
    bx, by = lax.rem(me // 2, 2), lax.rem(me // 4, 2)
    one = g.core == 1
    def copy(slot, dev):
        return pltpu.make_async_remote_copy(src_ref=g.tail, dst_ref=g.tail, send_sem=g.tsem.at[slot], recv_sem=g.tsem.at[4], device_id=(dev,), device_id_type=MESH)
    right = jnp.logical_and(one, bx == 1)
    corner = jnp.logical_and(right, by == 1)
    sends = ((0, me - 8, jnp.logical_and(corner, z > 0)), (1, g.first, corner), (2, g.second, right), (3, g.sib, one))
    @pl.when(me != g.n - 1)
    def _(): copy(0, g.sib).wait_recv()
    for slot, dev, there in sends:
        @pl.when(there)
        def _(): copy(slot, dev).start()
    g.vecs[...] = g.tail[...].astype(F32)
    def finish():
        for slot, dev, there in sends:
            @pl.when(there)
            def _(): copy(slot, dev).wait_send()
    return finish


class Gather:
    def __init__(self, g, parts):
        self.g = g
        self.parts = parts
        self.size = (g.geo.RL, g.geo.RC)
        self.place = (g.gl, g.gc)

    def source(self, dz, f, s):
        g = self.g
        return g.me + 8 * dz + f * (g.first - g.me) + s * (g.second - g.me)

    def copy(self, k, p, src, dev, slot):
        g = self.g
        rows = self.size[k] // self.parts[k]
        i = p if k == 0 else self.parts[0] + p
        ref = self.place[k].at[pl.ds(pl.multiple_of(src * self.size[k] + p * rows, 16), rows)]
        return pltpu.make_async_remote_copy(src_ref=ref, dst_ref=ref, send_sem=g.ssem.at[i, slot], recv_sem=g.rsem.at[i, src], device_id=(dev,), device_id_type=MESH)

    def sends(self, o, k, p, dz):
        g, z, Z = self.g, self.g.z, self.g.Z
        f, s = {1: (0, 0), 2: (1, 0), 3: (0, 1), 4: (1, 1)}[o]
        src, zi = self.source(dz, f, s), z + dz
        out = []
        if k == 1:
            if dz >= 0: out.append((lambda: self.copy(k, p, src, g.me - 8, (o - 1) * Z + zi), z > 0))
            if dz <= 0: out.append((lambda: self.copy(k, p, src, g.me + 8, (o + 3) * Z + zi), z < Z - 1))
            if dz == 0 and o == 1: out.append((lambda: self.copy(k, p, src, g.first, 8 * Z), None))
            if dz == 0 and o <= 2: out.append((lambda: self.copy(k, p, src, g.second, 8 * Z + o), None))
            out.append((lambda: self.copy(k, p, src, g.sib, (8 + o) * Z + zi), None))
            return src, out
        if o == 1:
            if dz >= 0: out.append((lambda: self.copy(k, p, src, g.me - 8, zi), z > 0))
            if dz <= 0: out.append((lambda: self.copy(k, p, src, g.me + 8, Z + zi), z < Z - 1))
            out.append((lambda: self.copy(k, p, src, g.first, 2 * Z + zi), None))
        if o <= 2: out.append((lambda: self.copy(k, p, src, g.second, (2 + o) * Z + zi), None))
        out.append((lambda: self.copy(k, p, src, g.sib, (4 + o) * Z + zi), None))
        return src, out

    def guard(self, cond, fn):
        if cond is None: fn()
        else: pl.when(cond)(fn)

    def valid(self, dz, fn):
        z, Z = self.g.z, self.g.Z
        self.guard(None if dz == 0 else jnp.logical_and(z + dz >= 0, z + dz < Z), fn)

    def event(self, o, k, p, dz):
        def fn():
            src, sends = self.sends(o, k, p, dz)
            if o > 1 or dz != 0: self.copy(k, p, src, self.g.sib, 0).wait_recv()
            for cp, there in sends: self.guard(there, lambda cp=cp: cp().start())
        self.valid(dz, fn)

    def drain(self, o, k, p, dz):
        def fn():
            for cp, there in self.sends(o, k, p, dz)[1]: self.guard(there, lambda cp=cp: cp().wait_send())
        self.valid(dz, fn)

    def convert(self, k, dz):
        g = self.g
        per = 2 * self.size[k] // UNIT
        def fn():
            def chip_body(c, _):
                src = self.source(dz, c // 2, lax.rem(c, 2))
                for p in range(self.parts[k]): self.copy(k, p, src + g.sib - g.me, g.sib, 0).wait_recv()
                def unit(i, _):
                    t = (src // 2) * per + i
                    base = t * UNIT
                    if k == 1: convert_unit(g.gc, base, g.wc, t * 192, 6, g.scr)
                    else:
                        @pl.when(t < 12)
                        def _(): convert_unit(g.gl, base, g.wqkv, t * 64, 18, g.scr)
                        @pl.when(jnp.logical_and(t >= 12, t < 16))
                        def _(): convert_unit(g.gl, base, g.wo, (t - 12) * 192, 6, g.scr)
                        @pl.when(jnp.logical_and(t >= 16, t < 32))
                        def _(): convert_unit(g.gl, base, g.w1, (t - 16) * 48, 24, g.scr)
                        @pl.when(t >= 32)
                        def _(): convert_unit(g.gl, base, g.w2, (t - 32) * 192, 6, g.scr)
                    return 0
                lax.fori_loop(0, per, unit, 0)
                return 0
            lax.fori_loop(0, 4, chip_body, 0)
        self.valid(dz, fn)


PART = 576
RING = 6


class Scatter:
    def __init__(self, g, jobs):
        self.g = g
        self.size = (g.geo.RL, g.geo.RC)
        self.own = (g.gl, g.gc)
        self.jobs = jobs
        self.started, self.granted, self.waiting = set(), set(), []
        self.opened = self.closed = 0
        self.arrived = set()
        self.leads = {}
        for kind, step, x in jobs:
            if kind == "second": self.leads.setdefault(step, x)

    def target(self, zt, f, s):
        g = self.g
        return g.me + 8 * (zt - g.z) + f * (g.first - g.me) + s * (g.second - g.me)

    def other(self, zt, f, s): return self.target(zt, f, s) + self.g.sib - self.g.me

    def rows(self, k, t, p):
        return pl.ds(pl.multiple_of(t * self.size[k] + p * PART, 16), PART)

    def sem(self, k, p):
        return p if k == 0 else self.size[0] // PART + p

    def move(self, src, dst, send, recv, i, index, dev):
        return pltpu.make_async_remote_copy(src_ref=src, dst_ref=dst, send_sem=send.at[i, index], recv_sem=recv.at[i, index], device_id=(dev,), device_id_type=MESH)

    def at(self, k, p, t): return self.own[k].at[self.rows(k, t, p)]

    def to_sib(self, k, p, zt):
        g = self.g
        half, size, part = g.n // 2, self.size[k], pl.ds(p * PART, PART)
        src = self.own[k].reshape(half, 2, size, LANE).at[pl.ds(4 * zt, 4), 1 - g.core, part]
        dst = g.from_sib[k].reshape(half, size, LANE).at[pl.ds(4 * zt, 4), part]
        return self.move(src, dst, g.s_sib, g.r_sib, self.sem(k, p), zt, g.sib)

    def to_second(self, k, p, zt, f):
        g = self.g
        t = self.target(zt, f, 1)
        return self.move(self.at(k, p, t), self.at(k, p, t + g.sib - g.me), g.s_second, g.r_second, self.sem(k, p), 2 * zt + f, g.second)

    def to_first(self, k, p, zt):
        g = self.g
        t = self.target(zt, 1, 0)
        return self.move(self.at(k, p, t), self.at(k, p, t + g.second - g.me + g.sib - g.me), g.s_first, g.r_first, self.sem(k, p), zt, g.first)

    def down(self, k, p, zt):
        g = self.g
        return self.move(self.at(k, p, self.target(zt, 0, 0)), self.at(k, p, self.other(zt, 1, 1)), g.s_down, g.r_down, self.sem(k, p), zt, g.me - 8)

    def up(self, k, p, zt, land):
        g = self.g
        dst = (g.below_l, g.below_c)[k].at[pl.ds(p * PART, PART)] if land else self.at(k, p, self.other(zt, 1, 1))
        return self.move(self.at(k, p, self.target(zt, 0, 0)), dst, g.s_up, g.r_up, self.sem(k, p), zt, g.me + 8)

    def p0(self, k, p, zt):
        self.to_sib(k, p, zt).start()
        self.started.add((k, p, zt))
        self.waiting.append((k, p, zt))

    def ticket(self, which, k, p, zt): return self.g.credit.at[which, self.sem(k, p) * self.g.Z + zt]

    def credit(self, which, k, p, zt, dev):
        pl.semaphore_signal(self.ticket(which, k, p, zt), inc=1, device_id=(dev,), device_id_type=MESH)

    def grant(self, k, p, zt):
        g = self.g
        z, Z, me = g.z, g.Z, g.me
        self.to_sib(k, p, zt).wait_send()
        self.credit(0, k, p, zt, g.second)
        self.credit(1, k, p, zt, g.first)
        if zt < Z - 1:
            @pl.when(jnp.logical_and(z >= zt, z < Z - 1))
            def _(): self.credit(2, k, p, zt, me + 8)
        if zt > 1:
            @pl.when(jnp.logical_and(z < zt, z > 0))
            def _(): self.credit(3, k, p, zt, me - 8)
        self.granted.add((k, p, zt))

    def grant_all(self):
        for st in self.waiting: self.grant(*st)
        self.waiting = []

    def spend(self, which, k, p, zt): pl.semaphore_wait(self.ticket(which, k, p, zt), 1)

    def place(self, job):
        kind, (k, p, zt), x = job
        z, Z = self.g.z, self.g.Z
        if kind == "second": return None, self.target(zt, x, 1)
        if kind == "first": return None, self.target(zt, 1, 0)
        if kind == "last": return z == zt, self.target(zt, 0, 0)
        return z == (x[0] if x[1] else Z - 1 - x[0]), self.target(zt, 0, 0)

    def describe(self, job):
        kind, (k, p, zt), x = job
        g = self.g
        z, Z, me = g.z, g.Z, g.me
        if kind == "second":
            def send():
                if self.leads[k, p, zt] == x: self.spend(0, k, p, zt)
                self.to_second(k, p, zt, x).start()
            return [], [], None, send
        if kind == "first":
            def send():
                self.spend(1, k, p, zt)
                self.to_first(k, p, zt).start()
            return [self.to_second(k, p, zt, 1)], [self.at(k, p, self.other(zt, 1, 0))], None, send
        waits = [self.to_second(k, p, zt, 0), self.to_first(k, p, zt)]
        lands = [self.at(k, p, self.other(zt, 0, 0)), self.at(k, p, self.other(zt, 0, 1))]
        far = self.at(k, p, self.other(zt, 1, 1))
        if kind == "last":
            if zt < Z - 1:
                waits.append(self.down(k, p, zt))
                lands.append(far)
            if zt > 0:
                waits.append(self.up(k, p, zt, True))
                lands.append((g.below_l, g.below_c)[k].at[pl.ds(p * PART, PART)])
            return waits, lands, (g.xlf, g.xcf)[k], None
        hop, upward = x
        if hop > 0:
            waits.append(self.up(k, p, zt, False) if upward else self.down(k, p, zt))
            lands.append(far)
        here = hop if upward else Z - 1 - hop
        def send():
            if upward:
                if here + 1 < zt: self.spend(3, k, p, zt)
                self.up(k, p, zt, here + 1 == zt).start()
            else:
                self.spend(2, k, p, zt)
                self.down(k, p, zt).start()
        return waits, lands, None, send

    def guard(self, cond, fn):
        if cond is None: fn()
        else: pl.when(cond)(fn)

    def fetch(self, job, t, slot):
        g, (k, p, zt) = self.g, job[1]
        return pltpu.make_async_copy(g.from_sib[k].at[self.rows(k, t // 2, p)], g.tmp.at[slot], g.fsem.at[slot])

    def open(self, i):
        job = self.jobs[i]
        cond, t = self.place(job)
        if job[1] not in self.arrived:
            self.to_sib(*job[1]).wait_recv()
            self.arrived.add(job[1])
        self.guard(cond, lambda: self.fetch(job, t, i % RING).start())

    def close(self, i):
        g, job, slot = self.g, self.jobs[i], i % RING
        k, p, zt = job[1]
        cond, t = self.place(job)
        def fn():
            waits, lands, out, send = self.describe(job)
            for cp in waits: cp.wait_recv()
            self.fetch(job, t, slot).wait()
            mine = self.at(k, p, t)
            def body(b, _):
                r = pl.ds(pl.multiple_of(b * 32, 32), 32)
                acc = mine[r, :].astype(F32) + g.tmp[slot, r, :].astype(F32)
                for land in lands: acc = acc + land[r, :].astype(F32)
                if out is None: mine[r, :] = acc.astype(BF16)
                else: out[pl.ds(pl.multiple_of(p * PART + b * 32, 32), 32), :] = acc
                return 0
            lax.fori_loop(0, PART // 32, body, 0, unroll=2)
            if send is not None: send()
        self.guard(cond, fn)

    def run(self):
        i = self.closed
        step = self.jobs[i][1]
        if step not in self.granted: self.grant_all()
        while self.opened < len(self.jobs) and self.opened < i + RING and self.jobs[self.opened][1] in self.started:
            self.open(self.opened)
            self.opened += 1
        self.close(i)
        self.closed += 1

    def finish(self, k, p, zt):
        g = self.g
        for f in (0, 1): self.to_second(k, p, zt, f).wait_send()
        self.to_first(k, p, zt).wait_send()
        @pl.when(g.z > zt)
        def _(): self.down(k, p, zt).wait_send()
        @pl.when(g.z < zt)
        def _(): self.up(k, p, zt, False).wait_send()


def reduce_vectors(g):
    Z, me, z = g.Z, g.me, g.z
    core = lax.rem(me, 2)
    bx, by = lax.rem(me // 2, 2), lax.rem(me // 4, 2)
    def cp(slot, dev):
        return pltpu.make_async_remote_copy(src_ref=g.vgrad, dst_ref=g.vland.at[slot], send_sem=g.vsem.at[0], recv_sem=g.vsem.at[1 + slot], device_id=(dev,), device_id_type=MESH)
    def take(slot):
        cp(slot, g.sib).wait_recv()
        g.vgrad[...] = g.vgrad[...] + g.vland[slot]
    def give(slot, dev): cp(slot, dev).start()
    on = core == 1
    right = jnp.logical_and(on, bx == 1)
    corner = jnp.logical_and(right, by == 1)
    def stage(giver, taker, slot, dev):
        def fn():
            @pl.when(giver)
            def _(): give(slot, dev)
            @pl.when(taker)
            def _(): take(slot)
        return fn
    stages = [stage(jnp.logical_not(on), on, 0, g.sib), stage(jnp.logical_and(on, bx == 0), right, 1, g.second),
              stage(jnp.logical_and(right, by == 0), corner, 2, g.first)]
    stages += [stage(jnp.logical_and(corner, z == h), jnp.logical_and(corner, z == h + 1), 3, me + 8) for h in range(Z - 1)]
    def finish():
        @pl.when(me != g.n - 1)
        def _(): cp(0, g.sib).wait_send()
    return stages, finish


def place_gradients(g):
    n, geo, me = g.n, g.geo, g.me
    prv = lax.rem(me + n - 1, n)
    edge = me == n - 1
    HL, HC = geo.HL, geo.HC
    skip = VBC - HL
    vectors = ((0, HL, HL), (VBC, HL + HC, HC - skip))
    def part(k):
        x, out, rows, drift = ((g.xlf, g.outl, geo.RL, geo.dl), (g.xcf, g.outc, geo.RC, geo.dc))[k]
        first, last = (0, HL) if k == 0 else (HL, HL + HC)
        cp = pltpu.make_async_remote_copy(src_ref=g.fs.at[pl.ds(first, last - first)], dst_ref=g.fr.at[pl.ds(first, last - first)],
                                          send_sem=g.hsem.at[2 + 2 * k], recv_sem=g.hsem.at[3 + 2 * k], device_id=(prv,), device_id_type=MESH)
        def begin():
            g.fs[first:last, :] = x[0:last - first, :]
            cp.start()
        split = (rows - 96) // 96 * 96
        def middle(): realign(out, 0, 0, split, x, drift * me)
        def end():
            cp.wait()
            lo, hi, count = vectors[k]
            x[rows:rows + count, :] = jnp.where(edge, g.vgrad[lo:hi, :], g.fr[first:first + count, :])
            realign(out, 0, split, out.shape[0], x, drift * me)
        return begin, middle, end
    return part(0), part(1)


PLANES = 4
LAYER_PARTS = 1
GATHER = (
    (1, 1, 0, 0), (1, 0, 0, 0), (1, 0, 0, -1), (3, 0, 0, 0), (2, 1, 0, 0), (2, 0, 0, 0), (1, 0, 0, 1), (4, 1, 0, 0), (1, 0, 0, 2), (3, 1, 0, 0),
    (1, 0, 0, -2), (2, 0, 0, -1), (3, 1, 0, 1), (4, 0, 0, 0), (2, 0, 0, 1), (4, 1, 0, -1), (3, 1, 0, -1), (1, 0, 0, 3), (4, 1, 0, 1), (2, 1, 0, 1),
    (3, 0, 0, -1), (1, 0, 0, -3), (1, 1, 0, 1), (5, 0, 0), (2, 1, 0, -1), (0, 0), (3, 0, 0, 1), (1, 1, 0, -1), (3, 0, 0, 2), (5, 1, 0), (2, 0, 0, -2),
    (4, 0, 0, -1), (5, 1, 1), (2, 0, 0, 2), (3, 1, 0, 2), (5, 1, -1), (3, 0, 0, -2), (2, 0, 0, -3), (3, 0, 0, -3), (3, 1, 0, -2), (4, 1, 0, -2),
    (4, 0, 0, 1), (2, 1, 0, 2), (1, 1, 0, 2), (4, 1, 0, 2), (5, 0, -1), (2, 0, 0, 3), (4, 0, 0, -2), (1, 1, 0, -2), (2, 1, 0, -2), (4, 0, 0, -3),
    (5, 0, 1), (5, 0, -2), (5, 0, -3), (0, 1), (0, 2), (0, 3), (4, 0, 0, 2), (5, 1, -2), (5, 1, 2), (0, 4), (2, 1, 0, -3), (3, 0, 0, 3), (4, 0, 0, 3),
    (0, 5), (5, 0, 2), (1, 1, 0, 3), (0, 6), (3, 1, 0, 3), (4, 1, 0, 3), (0, 7), (2, 1, 0, 3), (1, 1, 0, -3), (4, 1, 0, -3), (3, 1, 0, -3), (0, 8),
    (6, 0), (5, 0, 3), (0, 9), (6, 1), (5, 1, -3), (5, 1, 3), (0, 10),
)
SCATTER = (
    (1, 1, 0, 3, 0), (1, 1, 0, 2, 1), (1, 1, 0, 3, 1), (1, 1, 0, 0, 1), (1, 1, 0, 1, 1), (0, 0), (0, 1), (1, 0, 1, 3, 1), (1, 0, 0, 3, 1),
    (1, 0, 1, 3, 0), (1, 1, 0, 2, 0), (0, 2), (1, 1, 0, 1, 0), (2, 1, 0, 2, 0), (2, 1, 0, 1, 0), (0, 3), (0, 4), (2, 0, 0, 3, 0), (1, 1, 0, 0, 0),
    (0, 5), (1, 0, 0, 2, 0), (1, 0, 0, 2, 1), (1, 0, 2, 2, 0), (2, 1, 0, 3, 0), (0, 6), (2, 1, 0, 0, 0), (1, 0, 2, 2, 1), (3, 1, 0, 2, (0, True)),
    (3, 1, 0, 1, (0, True)), (0, 7), (1, 0, 0, 3, 0), (1, 0, 2, 3, 1), (2, 0, 0, 2, 0), (1, 0, 2, 3, 0), (0, 8), (3, 1, 0, 3, (0, True)), (0, 9),
    (1, 0, 1, 2, 1), (0, 10), (3, 1, 0, 2, (0, False)), (2, 0, 2, 2, 0), (3, 1, 0, 2, (1, True)), (3, 0, 0, 3, (0, True)), (2, 0, 1, 3, 0),
    (1, 0, 1, 2, 0), (2, 0, 2, 3, 0), (0, 11), (3, 0, 0, 3, (1, True)), (3, 1, 0, 0, (0, False)), (2, 0, 1, 2, 0), (0, 12), (1, 0, 0, 0, 1),
    (3, 0, 0, 3, (2, True)), (3, 0, 2, 2, (0, False)), (3, 0, 2, 3, (0, True)), (1, 0, 0, 0, 0), (4, 1, 0, 2, 0), (1, 0, 1, 1, 1),
    (3, 1, 0, 3, (1, True)), (3, 1, 0, 1, (0, False)), (1, 0, 2, 0, 1), (3, 0, 1, 2, (0, False)), (3, 0, 0, 2, (0, False)), (3, 1, 0, 0, (1, False)),
    (2, 0, 0, 0, 0), (3, 0, 0, 2, (0, True)), (3, 0, 1, 3, (0, True)), (3, 0, 2, 3, (1, True)), (1, 0, 1, 0, 1), (3, 0, 2, 2, (0, True)),
    (1, 0, 2, 0, 0), (3, 0, 1, 2, (0, True)), (0, 13), (3, 0, 0, 2, (1, True)), (2, 0, 2, 0, 0), (1, 0, 1, 0, 0), (3, 0, 0, 0, (0, False)),
    (3, 0, 1, 3, (1, True)), (3, 1, 0, 3, (2, True)), (3, 1, 0, 0, (2, False)), (1, 0, 0, 1, 1), (1, 0, 0, 1, 0), (3, 0, 0, 0, (2, False)),
    (3, 0, 2, 0, (0, False)), (3, 0, 1, 2, (1, True)), (3, 1, 0, 1, (1, False)), (3, 0, 0, 0, (1, False)), (2, 0, 1, 0, 0), (0, 14),
    (3, 0, 2, 3, (2, True)), (2, 0, 0, 1, 0), (1, 0, 2, 1, 1), (3, 0, 1, 0, (0, False)), (3, 0, 2, 0, (2, False)), (1, 0, 1, 1, 0), (4, 1, 0, 1, 0),
    (3, 0, 2, 2, (1, True)), (3, 0, 2, 0, (1, False)), (3, 0, 1, 3, (2, True)), (3, 0, 1, 0, (1, False)), (3, 0, 1, 0, (2, False)), (2, 0, 1, 1, 0),
    (0, 15), (3, 0, 0, 1, (0, False)), (4, 0, 2, 3, 0), (2, 0, 2, 1, 0), (3, 0, 1, 1, (0, True)), (1, 0, 2, 1, 0), (3, 0, 1, 1, (0, False)),
    (3, 0, 0, 1, (1, False)), (4, 0, 0, 3, 0), (3, 0, 0, 1, (0, True)), (0, 16), (4, 0, 0, 2, 0), (4, 1, 0, 3, 0), (4, 0, 1, 1, 0),
    (3, 0, 2, 1, (0, True)), (3, 0, 1, 1, (1, False)), (4, 0, 0, 1, 0), (3, 0, 2, 1, (0, False)), (3, 0, 2, 1, (1, False)), (4, 0, 1, 2, 0),
    (4, 0, 1, 0, 0), (4, 0, 2, 1, 0), (4, 0, 0, 0, 0), (4, 1, 0, 0, 0), (4, 0, 2, 2, 0), (4, 0, 1, 3, 0), (4, 0, 2, 0, 0),
)


def local_layout():
    return ((D, 3 * D), (D, D), (D, FF), (FF, D), (FF,)) + ((D,),) * 8


def conv_layout():
    return ((RATE * D, D), (D,), (D,), (D,))


def unpack(packed, layout):
    offset = 0
    pieces = []
    for extent in layout:
        length = math.prod(extent)
        pieces.append(packed[offset : offset + length].reshape(extent))
        offset = offset + length
    return pieces


def normalize_parts(values):
    average = jnp.mean(values, axis=-1, keepdims=True)
    centred = values - average
    spread = jnp.mean(centred * centred, axis=-1, keepdims=True)
    scaling = lax.rsqrt(spread + EPSILON)
    return (centred * scaling, scaling)


def normal_back(grad_normed, normed, scaling):
    first_mean = jnp.mean(grad_normed, axis=-1, keepdims=True)
    second_mean = jnp.mean(grad_normed * normed, axis=-1, keepdims=True)
    return scaling * (grad_normed - first_mean - normed * second_mean)


def product(left, right):
    return jnp.dot(left, right, preferred_element_type=jnp.float32)


def rows_inner(left, right):
    return lax.dot_general(
        left, right, (((0,), (0,)), ((), ())), preferred_element_type=jnp.float32
    )


def times_transpose(left, right):
    return lax.dot_general(
        left, right, (((1,), (1,)), ((), ())), preferred_element_type=jnp.float32
    )


def gelu_exact(values):
    return jax.nn.gelu(values, approximate=False)


def gelu_grad(values, upstream):
    return jax.vjp(gelu_exact, values)[1](upstream)[0]


def window_scores(projected, segments_block):
    row_count = projected.shape[0]
    windows = row_count // WINDOW
    heads_view = projected.reshape(windows, WINDOW, 3, HEADS, HEAD_SIZE)
    queries = heads_view[:, :, 0]
    keys_all = heads_view[:, :, 1]
    values = heads_view[:, :, 2]
    scores = jnp.einsum(
        "bqhe,bkhe->bhqk", queries, keys_all, preferred_element_type=jnp.float32
    ) * HEAD_SIZE ** (-0.5)
    grouped = segments_block.reshape(windows, WINDOW)
    allowed = grouped[:, None, :, None] == grouped[:, None, None, :]
    return (jnp.where(allowed, scores, -1e30), queries, keys_all, values)


def forward_pass(characters_block, segments_block, local_weights, conv_weights):
    (
        qkv_weight,
        out_weight,
        in_weight,
        down_weight,
        in_bias,
        gain_one,
        shift_one,
        query_bias,
        value_bias,
        out_bias,
        gain_two,
        shift_two,
        down_bias,
    ) = local_weights
    conv_weight, conv_bias, gain_three, shift_three = conv_weights
    row_count = characters_block.shape[0]
    inputs = characters_block.astype(jnp.float32)
    norm_one, scale_one = normalize_parts(inputs)
    normed = (norm_one * gain_one + shift_one).astype(jnp.bfloat16)
    proj_bias = jnp.concatenate([query_bias, jnp.zeros_like(query_bias), value_bias])
    projected = (product(normed, qkv_weight) + proj_bias).astype(jnp.bfloat16)
    scores, queries, keys_all, values = window_scores(projected, segments_block)
    largest = jnp.max(scores, axis=-1, keepdims=True)
    raised = jnp.exp(scores - largest)
    totals = jnp.sum(raised, axis=-1, keepdims=True)
    log_totals = largest + jnp.log(totals)
    weights = (raised / totals).astype(jnp.bfloat16)
    attended = jnp.einsum("bhqk,bkhe->bqhe", weights, values, preferred_element_type=jnp.float32)
    context = attended.reshape(row_count, D).astype(jnp.bfloat16)
    after_attention = inputs + product(context, out_weight) + out_bias
    norm_two, scale_two = normalize_parts(after_attention)
    middle = (norm_two * gain_two + shift_two).astype(jnp.bfloat16)
    pre_act = product(middle, in_weight) + in_bias
    hidden = gelu_exact(pre_act).astype(jnp.bfloat16)
    after_feed = after_attention + product(hidden, down_weight) + down_bias
    grouped_rows = after_feed.astype(jnp.bfloat16).reshape(row_count // RATE, RATE * D)
    conv_pre = product(grouped_rows, conv_weight) + conv_bias
    norm_three, scale_three = normalize_parts(gelu_exact(conv_pre))
    molecules = (norm_three * gain_three + shift_three).astype(jnp.bfloat16)
    saved_state = (
        segments_block,
        norm_one,
        scale_one,
        normed,
        projected,
        log_totals,
        context,
        norm_two,
        scale_two,
        middle,
        pre_act,
        hidden,
        grouped_rows,
        conv_pre,
        norm_three,
        scale_three,
    )
    return (molecules, saved_state)


def backward_pass(cotangent_block, saved_state, local_weights, conv_weights):
    (
        qkv_weight,
        out_weight,
        in_weight,
        down_weight,
        in_bias,
        gain_one,
        shift_one,
        query_bias,
        value_bias,
        out_bias,
        gain_two,
        shift_two,
        down_bias,
    ) = local_weights
    conv_weight, conv_bias, gain_three, shift_three = conv_weights
    (
        segments_block,
        norm_one,
        scale_one,
        normed,
        projected,
        log_totals,
        context,
        norm_two,
        scale_two,
        middle,
        pre_act,
        hidden,
        grouped_rows,
        conv_pre,
        norm_three,
        scale_three,
    ) = saved_state
    row_count = normed.shape[0]
    windows = row_count // WINDOW
    upstream = cotangent_block.astype(jnp.float32)
    grad_gain_three = jnp.sum(upstream * norm_three, axis=0)
    grad_shift_three = jnp.sum(upstream, axis=0)
    grad_activated = normal_back(upstream * gain_three, norm_three, scale_three)
    grad_conv_pre = gelu_grad(conv_pre, grad_activated).astype(jnp.bfloat16)
    grad_conv_bias = jnp.sum(grad_conv_pre.astype(jnp.float32), axis=0)
    grad_conv_weight = rows_inner(grouped_rows, grad_conv_pre)
    grad_feed = times_transpose(grad_conv_pre, conv_weight).reshape(row_count, D)
    grad_down_bias = jnp.sum(grad_feed, axis=0)
    grad_branch = grad_feed.astype(jnp.bfloat16)
    grad_down_weight = rows_inner(hidden, grad_branch)
    grad_hidden = times_transpose(grad_branch, down_weight)
    grad_pre = gelu_grad(pre_act, grad_hidden).astype(jnp.bfloat16)
    grad_in_bias = jnp.sum(grad_pre.astype(jnp.float32), axis=0)
    grad_in_weight = rows_inner(middle, grad_pre)
    grad_middle = times_transpose(grad_pre, in_weight)
    grad_gain_two = jnp.sum(grad_middle * norm_two, axis=0)
    grad_shift_two = jnp.sum(grad_middle, axis=0)
    grad_attention = grad_feed + normal_back(grad_middle * gain_two, norm_two, scale_two)
    grad_out_bias = jnp.sum(grad_attention, axis=0)
    grad_attn_out = grad_attention.astype(jnp.bfloat16)
    grad_out_weight = rows_inner(context, grad_attn_out)
    grad_context = times_transpose(grad_attn_out, out_weight).astype(jnp.bfloat16)
    grad_heads = grad_context.reshape(windows, WINDOW, HEADS, HEAD_SIZE)
    scores, queries, keys_all, values = window_scores(projected, segments_block)
    probs = jnp.exp(scores - log_totals)
    weights = probs.astype(jnp.bfloat16)
    grad_weights = jnp.einsum(
        "bqhe,bkhe->bhqk", grad_heads, values, preferred_element_type=jnp.float32
    )
    row_terms = jnp.sum(probs * grad_weights, axis=-1, keepdims=True)
    grad_scores = (probs * (grad_weights - row_terms)).astype(jnp.bfloat16)
    grad_queries = jnp.einsum(
        "bhqk,bkhe->bqhe", grad_scores, keys_all, preferred_element_type=jnp.float32
    ) * HEAD_SIZE ** (-0.5)
    grad_keys = jnp.einsum(
        "bhqk,bqhe->bkhe", grad_scores, queries, preferred_element_type=jnp.float32
    ) * HEAD_SIZE ** (-0.5)
    grad_values = jnp.einsum(
        "bhqk,bqhe->bkhe", weights, grad_heads, preferred_element_type=jnp.float32
    )
    grad_proj = (
        jnp.stack([grad_queries, grad_keys, grad_values], axis=2)
        .reshape(row_count, 3 * D)
        .astype(jnp.bfloat16)
    )
    proj_sums = jnp.sum(grad_proj.astype(jnp.float32), axis=0)
    grad_query_bias = proj_sums[:D]
    grad_value_bias = proj_sums[2 * D :]
    grad_qkv_weight = rows_inner(normed, grad_proj)
    grad_normed = times_transpose(grad_proj, qkv_weight)
    grad_gain_one = jnp.sum(grad_normed * norm_one, axis=0)
    grad_shift_one = jnp.sum(grad_normed, axis=0)
    grad_inputs = grad_attention + normal_back(grad_normed * gain_one, norm_one, scale_one)
    local_grad = jnp.concatenate(
        [
            grad_qkv_weight.reshape(-1),
            grad_out_weight.reshape(-1),
            grad_in_weight.reshape(-1),
            grad_down_weight.reshape(-1),
            grad_in_bias,
            grad_gain_one,
            grad_shift_one,
            grad_query_bias,
            grad_value_bias,
            grad_out_bias,
            grad_gain_two,
            grad_shift_two,
            grad_down_bias,
        ]
    )
    conv_grad = jnp.concatenate(
        [grad_conv_weight.reshape(-1), grad_conv_bias, grad_gain_three, grad_shift_three]
    )
    return (grad_inputs, local_grad, conv_grad)


def plain_device(characters, segment_ids, cotangent, local_params, conv_params):
    devices = lax.axis_size("fsdp")
    local_shard = local_params.shape[0]
    conv_shard = conv_params.shape[0]
    local_pad = local_shard * devices - LOCAL_COUNT
    conv_pad = conv_shard * devices - CONV_COUNT
    local_total = jnp.zeros((1, local_shard), jnp.float32)
    conv_total = jnp.zeros((1, conv_shard), jnp.float32)
    molecule_list = []
    gradient_list = []
    for micro_index in range(MICRO):
        local_full, conv_full = (
            lax.all_gather(local_params, "fsdp", axis=0, tiled=True),
            lax.all_gather(conv_params, "fsdp", axis=0, tiled=True),
        )
        molecules, saved_state = forward_pass(
            characters[micro_index],
            segment_ids[micro_index],
            unpack(local_full, local_layout()),
            unpack(conv_full, conv_layout()),
        )
        local_full, conv_full = (
            lax.all_gather(local_params, "fsdp", axis=0, tiled=True),
            lax.all_gather(conv_params, "fsdp", axis=0, tiled=True),
        )
        grad_inputs, local_grad, conv_grad = backward_pass(
            cotangent[micro_index],
            saved_state,
            unpack(local_full, local_layout()),
            unpack(conv_full, conv_layout()),
        )
        local_table = jnp.concatenate([local_grad, jnp.zeros((local_pad,), jnp.float32)]).reshape(
            devices, local_shard
        )
        conv_table = jnp.concatenate([conv_grad, jnp.zeros((conv_pad,), jnp.float32)]).reshape(
            devices, conv_shard
        )
        local_part, conv_part = (
            lax.psum_scatter(local_table, "fsdp", scatter_dimension=0, tiled=True),
            lax.psum_scatter(conv_table, "fsdp", scatter_dimension=0, tiled=True),
        )
        local_total = local_total + local_part
        conv_total = conv_total + conv_part
        molecule_list.append(molecules)
        gradient_list.append(grad_inputs)
    return (
        jnp.stack(molecule_list),
        jnp.stack(gradient_list),
        local_total.reshape(-1),
        conv_total.reshape(-1),
    )


VECTOR_AT = (88, 96, 104, 112, 120)
FINISH_SPAN = 24


def fused_kernel(geo, rows, in_names, out_names, scratch_names, *refs):
    n_in, n_out = len(in_names), len(out_names)
    every = dict(zip(list(in_names) + list(out_names) + list(scratch_names), refs))
    me, core, z, sib, first, second = where_am_i()
    g = SimpleNamespace(n=geo.n, Z=geo.Z, geo=geo, me=me, core=core, z=z, sib=sib, first=first, second=second, rows=rows, mols=rows // RATE, **every)
    g.from_sib = (every["from_sib_l"], every["from_sib_c"])
    program(g)


def program(g):
    Z = g.Z
    start_gather(g)
    ag = Gather(g, (LAYER_PARTS, 1))
    own = [e for e in GATHER if e[0] == 1 and e[1] == 0 and e[3] == 0]
    for e in own: ag.event(*e)
    table = gather_table(g)
    forward = [
        lambda: (same_segment(g), forward_norm(g)), lambda: forward_qkv(g, 0, 6), lambda: forward_qkv(g, 6, 9),
        lambda: forward_attention(g, 0, 12), lambda: forward_attention(g, 12, 24), lambda: forward_out(g),
        lambda: forward_up(g, 0, 4), lambda: forward_up(g, 4, 8), lambda: forward_up(g, 8, 12), lambda: forward_down(g), lambda: forward_conv(g)]
    for e in GATHER:
        if e[0] == 0: forward[e[1]]()
        elif e[0] == 5: ag.convert(*e[1:])
        elif e[0] == 6:
            for d in GATHER:
                if 1 <= d[0] <= 4 and d[1] == e[1]: ag.drain(*d)
        elif e not in own: ag.event(*e)
    table()
    NL, NC = g.geo.RL // PART, g.geo.RC // PART
    conv_steps = [(1, p, zt) for zt in reversed(range(Z)) for p in range(NC)]
    layer_steps = [(0, p, zt) for zt in reversed(range(Z)) for p in range(NL)]
    names = {1: "second", 2: "first", 3: "line", 4: "last"}
    jobs = [(names[e[0]], e[1:4], e[4]) for e in SCATTER if e[0]]
    sc = Scatter(g, jobs)
    for zt in reversed(range(Z)):
        grad_conv_weight(g, zt)
        for st in conv_steps:
            if st[2] == zt: sc.p0(*st)
    def send_planes(lo, hi):
        sc.grant_all()
        for st in layer_steps:
            if lo <= st[2] < hi: sc.p0(*st)
    vec_stages, vec_finish = reduce_vectors(g)
    plane = 8 * g.geo.RL
    def plane_of(row): return -(-row // plane)
    q3, q2, q1 = plane_of(W2_ROW), plane_of(W1_ROW), plane_of(O_ROW)
    backward = [
        lambda: (back_conv(g), grad_down_weight(g, 0, 6)),
        lambda: (grad_down_weight(g, 6, 12), send_planes(q3, Z)),
        lambda: back_down(g, 0, 6),
        lambda: back_down(g, 6, 12),
        lambda: grad_up_weight(g, 0, 3),
        lambda: (grad_up_weight(g, 3, 6), send_planes(q2, q3)),
        lambda: back_up(g),
        lambda: (grad_out_weight(g), send_planes(q1, q2), back_out(g)),
        lambda: back_attention(g, 0, 1),
        lambda: back_attention(g, 1, 2),
        lambda: back_attention(g, 2, 3),
        lambda: back_attention(g, 3, 4),
        lambda: (grad_qkv_weight(g), send_planes(0, q1)),
        lambda: (back_qkv(g), pltpu.make_async_copy(g.dc, g.cg, g.osem.at[0]).start(), vec_stages[0]()),
        lambda: 0,
        lambda: 0,
        lambda: 0,
    ]
    late = dict(zip(VECTOR_AT, vec_stages[1:]))
    layer, conv = place_gradients(g)
    early = {max(i for i, e in enumerate(SCATTER) if e[:3] == (4, 0, 0)): layer[0], max(i for i, e in enumerate(SCATTER) if e[:2] == (4, 1)): conv[0]}
    sent = {}
    for i, e in enumerate(SCATTER):
        if 1 <= e[0] <= 3: sent[e[1:4]] = i
    open_steps = sorted(conv_steps + layer_steps, key=lambda st: sent[st])
    for i, e in enumerate(SCATTER):
        if e[0] == 0: backward[e[1]]()
        else: sc.run()
        if i >= len(SCATTER) - FINISH_SPAN and open_steps and sent[open_steps[0]] < i - 12: sc.finish(*open_steps.pop(0))
        if i in late: late[i]()
        if i in early: early[i]()
    layer[1]()
    conv[1]()
    vec_finish()
    for st in open_steps: sc.finish(*st)
    layer[2]()
    conv[2]()
    pltpu.make_async_copy(g.dc, g.cg, g.osem.at[0]).wait()


def fused(n, characters, segment_ids, cotangent, local_params, conv_params):
    geo = Geo(n, local_params.shape[0], conv_params.shape[0])
    micro, span, _ = characters.shape
    rows = micro * span
    x = characters.reshape(rows, D)
    cot = cotangent.reshape(rows // RATE, D)
    xl = jnp.pad(local_params, (0, geo.XL * LANE - local_params.shape[0])).reshape(geo.XL, LANE)
    xc = jnp.pad(conv_params, (0, geo.XC * LANE - conv_params.shape[0])).reshape(geo.XC, LANE)
    V = pl.BlockSpec(memory_space=pltpu.VMEM)
    A = pl.BlockSpec(memory_space=pl.ANY)
    S = jax.ShapeDtypeStruct
    Z, H = geo.Z, geo.HL + geo.HC
    ins = dict(x=x, seg=segment_ids, cot=cot, xl=xl, xc=xc)
    outs = dict(mol=(V, S((rows // RATE, D), BF16)), cg=(A, S((rows, D), F32)), outl=(V, S((-(-geo.XL // 96) * 96, LANE), F32)), outc=(V, S((-(-geo.XC // 96) * 96, LANE), F32)))
    for name, count in (("from_sib", n // 2),):
        outs[name + "_l"] = (A, S((count * geo.RL, LANE), BF16))
        outs[name + "_c"] = (A, S((count * geo.RC, LANE), BF16))
    W = pltpu.VMEM
    DMA = pltpu.SemaphoreType.DMA
    sc = state_shapes(rows)
    sc.update(wqkv=W((D, 3 * D), BF16), wo=W((D, D), BF16), w1=W((D, FF), BF16), w2=W((FF, D), BF16), wc=W((FF, D), BF16))
    sc.update(gl=W((n * geo.RL, LANE), BF16), gc=W((n * geo.RC, LANE), BF16), hb=W((H, LANE), BF16), hr=W((H, LANE), BF16), tail=W((H, LANE), BF16),
              xlf=W((geo.HL + -(-geo.XL // 96) * 96 + 32, LANE), F32), xcf=W((geo.HC + -(-geo.XC // 96) * 96 + 32, LANE), F32), vgrad=W((H, LANE), F32), vland=W((4, H, LANE), F32),
              fs=W((H, LANE), F32), fr=W((H, LANE), F32), tmp=W((RING, PART, LANE), BF16), below_l=W((geo.RL, LANE), BF16), below_c=W((geo.RC, LANE), BF16))
    parts = (geo.RL + geo.RC) // PART
    sc.update(rsem=DMA((LAYER_PARTS + 1, n)), ssem=DMA((LAYER_PARTS + 1, 13 * Z)), hsem=DMA((6,)), tsem=DMA((5,)), osem=DMA((1,)), vsem=DMA((5,)), fsem=DMA((RING,)), credit=pltpu.SemaphoreType.REGULAR((4, (geo.RL + geo.RC) // PART * Z)),
              r_sib=DMA((parts, Z)), s_sib=DMA((parts, Z)), r_second=DMA((parts, 2 * Z)), s_second=DMA((parts, 2 * Z)),
              r_first=DMA((parts, Z)), s_first=DMA((parts, Z)), r_up=DMA((parts, Z)), s_up=DMA((parts, Z)), r_down=DMA((parts, Z)), s_down=DMA((parts, Z)))
    res = pl.pallas_call(
        functools.partial(fused_kernel, geo, rows, list(ins), list(outs), list(sc)),
        out_shape=[s for _, s in outs.values()],
        in_specs=[V] * len(ins),
        out_specs=[b for b, _ in outs.values()],
        scratch_shapes=list(sc.values()),
        compiler_params=pltpu.CompilerParams(collective_id=0, has_side_effects=True, vmem_limit_bytes=64 << 20),
        name="layer",
    )(*ins.values())
    mol, cg, outl, outc = res[:4]
    return (mol.reshape(micro, span // RATE, D), cg.reshape(micro, span, D), outl.reshape(-1)[:local_params.shape[0]], outc.reshape(-1)[:conv_params.shape[0]])


def on_device(characters, segment_ids, cotangent, local_params, conv_params):
    n = lax.axis_size("fsdp")
    rows = characters.shape[0] * characters.shape[1]
    whole = n // 8 == PLANES and n % 8 == 0 and (2 * 72 * D) % (n * UNIT) == 0 and (2 * 24 * D) % (n * UNIT) == 0
    exact = local_params.shape[0] * n == LOCAL_COUNT and conv_params.shape[0] * n == CONV_COUNT
    if whole and exact and rows == 4 * WINDOW:
        return fused(n, characters, segment_ids, cotangent, local_params, conv_params)
    return plain_device(characters, segment_ids, cotangent, local_params, conv_params)


def solution(mesh):
    return jax.shard_map(
        on_device,
        mesh=mesh,
        in_specs=(P(None, "fsdp", None), P(None, "fsdp"), P(None, "fsdp", None), P("fsdp"), P("fsdp")),
        out_specs=(P(None, "fsdp", None), P(None, "fsdp", None), P("fsdp"), P("fsdp")),
        check_vma=False,
    )
```
